32 devices in a mesh: row: 4 (over y, core), seq: 8 (over z, x).
Axes of the slice: x: 2, y: 2, z: 4, core: 2. Of those that a mesh axis runs over, the one named last changes fastest.
Arguments:
- tokens: bfloat16 [4, 2048, 1024], P('row', 'seq'), may hold values from -6 to 6
- cotangent: bfloat16 [4, 2048, 1024], P('row', 'seq'), may hold values from -6 to 6
- pair_lengths: int32 [4, 8], P('row'), may hold values from 1 to 513, 2048 in all within a row
- prefix_key: bfloat16 [64, 1024], replicated, may hold values from -6 to 6
- prefix_value: bfloat16 [64, 1024], replicated, may hold values from -6 to 6
- w_query: bfloat16 [1024, 1024], P('row'), may hold values from -0.1875 to 0.1875
- b_query: bfloat16 [1024], replicated, may hold values from -0.59765625 to 0.59765625
- w_key: bfloat16 [1024, 1024], P('row'), may hold values from -0.1875 to 0.1875
- w_value: bfloat16 [1024, 1024], P('row'), may hold values from -0.1875 to 0.1875
- b_value: bfloat16 [1024], replicated, may hold values from -0.29882812 to 0.29882812
- w_out: bfloat16 [1024, 1024], P('row'), may hold values from -1 to 1
- b_out: bfloat16 [1024], replicated, may hold values from -0.59765625 to 0.59765625
- gain_attn: bfloat16 [1024], replicated, may hold values from 0.5 to 1.5
- shift_attn: bfloat16 [1024], replicated, may hold values from -0.59765625 to 0.59765625
- w_up: bfloat16 [1024, 4096], P('row'), may hold values from -0.1875 to 0.1875
- b_up: bfloat16 [4096], replicated, may hold values from -0.59765625 to 0.59765625
- w_down: bfloat16 [4096, 1024], P('row'), may hold values from -0.09375 to 0.09375
- b_down: bfloat16 [1024], replicated, may hold values from -0.59765625 to 0.59765625
- gain_ffn: bfloat16 [1024], replicated, may hold values from 0.5 to 1.5
- shift_ffn: bfloat16 [1024], replicated, may hold values from -0.59765625 to 0.59765625
Outputs:
- out_tokens: bfloat16 [4, 2048, 1024], P('row', 'seq')
- grad_tokens: bfloat16 [4, 2048, 1024], P('row', 'seq')
- grad_prefix_key: float32 [64, 1024], replicated
- grad_prefix_value: float32 [64, 1024], replicated
The draws below stay inside these ranges and needn't reach their ends.
Inputs may be any that keep to these rules, and one draw needn't show every extreme that they name: `pair_lengths`: each row's 8 pair lengths sum to 2048; in each row the longest pair has exactly 513 tokens.
All inputs are finite; a program needn't handle non-finite values.
Results may differ from the reference program's by a relative error of at most 0.02.
Values may be sent and summed in bfloat16 or wider, within the bound.
No kernel may reach another device: no remote copies, remote signals or barrier semaphores. Data moves between devices by JAX's collectives and lax.ppermute only.
A program may use at most 192 MiB of HBM per device.

```python
import math
import jax
import jax.numpy as jnp
import numpy as np
from jax import lax

D = 1024
HEADS = 16
HEAD_DIM = 64
FF = 4096
PREFIX = 64
PAIR_MOST = 513
ROW_LEN = 2048
ROWS = 4
PAIRS = 8


def block_levels(own_key, dims, cuts, smallest, top_value):
    def one(axis_at, parts):
        steps = jax.random.uniform(jax.random.fold_in(jax.random.fold_in(own_key, 6), axis_at), (parts,), jnp.float32, smallest / len(cuts), top_value / len(cuts))
        return jnp.repeat(jnp.exp(steps), dims[axis_at] // parts).reshape((-1,) + (1,) * (len(dims) - axis_at - 1))

    gain = one(*cuts[0])
    for cut in cuts[1:]:
        gain = gain * one(*cut)
    return gain


def split_up(number_of, total, most, lean):
    loads = [(1 << 20) // math.isqrt(standing ** lean) + 1 for standing in range(2, number_of + 1)]
    spare, holding = total - most - (number_of - 1), [1] * (number_of - 1)
    while spare > 0:
        free = [i for i in range(number_of - 1) if holding[i] < most]
        mass, remaining = sum([loads[i] for i in free]), spare
        for i in free:
            addition = min(most - holding[i], max(1, remaining * loads[i] // mass), spare)
            holding[i] = holding[i] + addition
            spare = spare - addition
    return np.array([most] + holding)


def ragged_sizes(key, amount, total, bound, slope):
    if amount == 2:
        one = jax.random.randint(key, (), max(1, total - bound), min(bound, total - 1) + 1)
        return jnp.stack([one, total - one])
    sizes = jnp.asarray(split_up(amount, total, bound, slope), jnp.int32)
    twos = (amount - 1) // 2
    donor, receiver = sizes[1:1 + 2 * twos:2], sizes[2:2 + 2 * twos:2]
    room = jnp.minimum(donor - 1, bound - receiver)
    shifted = jax.random.randint(jax.random.fold_in(key, 1), (twos,), 0, 1 << 20) % (room + 1)
    sizes = sizes.at[1:1 + 2 * twos:2].set(donor - shifted).at[2:2 + 2 * twos:2].set(receiver + shifted)
    return sizes[jax.random.permutation(jax.random.fold_in(key, 2), amount)]


def bell_draw(key, shape, width, bound, cuts=(), kind=jnp.bfloat16):
    factor_of = block_levels(key, shape, cuts, -0.22, 0.18) if cuts else 1.0
    drawn = jax.random.normal(key, shape, jnp.float32) * width * factor_of
    return jnp.minimum(jnp.maximum(drawn, -bound), bound).astype(kind)


def setup_inputs(seed: int = 0) -> dict:
    seeds = jax.random.split(jax.random.key(seed), 21)
    tokens = bell_draw(seeds[0], (ROWS, ROW_LEN, D), 1.0, 6.0, ((0, 4), (1, 8)))
    cotangent = bell_draw(seeds[1], (ROWS, ROW_LEN, D), 1.0, 6.0, ((0, 4), (1, 8)))
    pair_lengths = jax.vmap(lambda own: ragged_sizes(own, PAIRS, ROW_LEN, PAIR_MOST, 2))(jax.random.split(seeds[2], ROWS)).reshape((ROWS, PAIRS)).astype(jnp.int32)
    prefix_key = bell_draw(seeds[3], (PREFIX, D), 1.0, 6.0)
    prefix_value = bell_draw(seeds[4], (PREFIX, D), 1.0, 6.0)
    w_query = bell_draw(seeds[5], (D, D), D ** -0.5, 0.1875, ((0, 4),))
    b_query = bell_draw(seeds[6], (D,), 0.1, 0.59765625)
    w_key = bell_draw(seeds[7], (D, D), D ** -0.5, 0.1875, ((0, 4),))
    w_value = bell_draw(seeds[8], (D, D), D ** -0.5, 0.1875, ((0, 4),))
    b_value = bell_draw(seeds[9], (D,), 0.05, 0.29882812)
    w_out = bell_draw(seeds[10], (D, D), (D // 32) ** -0.5, 1.0, ((0, 4),))
    b_out = bell_draw(seeds[11], (D,), 0.1, 0.59765625)
    gain_attn = jnp.clip(1.0 + 0.1 * jax.random.normal(seeds[12], (D,), jnp.float32), 0.5, 1.5).astype(jnp.bfloat16)
    shift_attn = bell_draw(seeds[13], (D,), 0.1, 0.59765625)
    w_up = bell_draw(seeds[14], (D, FF), D ** -0.5, 0.1875, ((0, 4),))
    b_up = bell_draw(seeds[15], (FF,), 0.1, 0.59765625)
    w_down = bell_draw(seeds[16], (FF, D), FF ** -0.5, 0.09375, ((0, 4),))
    b_down = bell_draw(seeds[17], (D,), 0.1, 0.59765625)
    gain_ffn = jnp.clip(1.0 + 0.1 * jax.random.normal(seeds[18], (D,), jnp.float32), 0.5, 1.5).astype(jnp.bfloat16)
    shift_ffn = bell_draw(seeds[19], (D,), 0.1, 0.59765625)
    return {"tokens": tokens, "cotangent": cotangent, "pair_lengths": pair_lengths, "prefix_key": prefix_key, "prefix_value": prefix_value, "w_query": w_query, "b_query": b_query, "w_key": w_key, "w_value": w_value, "b_value": b_value, "w_out": w_out, "b_out": b_out, "gain_attn": gain_attn, "shift_attn": shift_attn, "w_up": w_up, "b_up": b_up, "w_down": w_down, "b_down": b_down, "gain_ffn": gain_ffn, "shift_ffn": shift_ffn}


@jax.custom_vjp
def low(v):
    return lax.optimization_barrier(v.astype(jnp.bfloat16)).astype(jnp.float32)

@jax.custom_vjp
def low_back(v):
    return v

def low_keep(v):
    return (low(v), None)

def low_pass(kept, grad):
    return (grad,)

def back_keep(v):
    return (v, None)

def back_low(kept, grad):
    return (low(grad),)
low.defvjp(low_keep, low_pass)
low_back.defvjp(back_keep, back_low)
ln_eps = 1e-05
masked_fill = -1e+30
highest = lax.Precision.HIGHEST

def layer_norm(field, gain_vec, shift_vec):
    average = lax.optimization_barrier(jnp.mean(field, axis=-1, keepdims=True))
    centred = field - average
    variance = lax.optimization_barrier(jnp.mean(centred * centred, axis=-1, keepdims=True))
    return centred * lax.rsqrt(variance + ln_eps) * gain_vec + shift_vec

def matmul(left, right):
    return jnp.dot(left, right, precision=highest, preferred_element_type=jnp.float32)

def to_float(array):
    return array.astype(jnp.float32)

def row_forward(inputs, labels, prefix_keys, prefix_values, params):
    w_query, b_query, w_key, w_value, b_value, w_out, b_out, gain_attn, shift_attn, w_up, b_up, w_down, b_down, gain_ffn, shift_ffn = params
    length = inputs.shape[0]
    queries = low_back(low(matmul(inputs, w_query) + b_query))
    keys = low_back(low(matmul(inputs, w_key)))
    values = low_back(low(matmul(inputs, w_value) + b_value))
    margin = PAIR_MOST
    pad_keys = jnp.pad(keys, ((margin, margin), (0, 0)))
    pad_values = jnp.pad(values, ((margin, margin), (0, 0)))
    pad_labels = jnp.pad(labels, (margin, margin), constant_values=-1)
    block_rows = math.gcd(512, length)
    window = block_rows + 2 * margin
    score_scale = HEAD_DIM ** (-0.5)
    prefix_count = prefix_keys.shape[0]
    head_keys = prefix_keys.reshape(prefix_count, HEADS, HEAD_DIM)
    head_values = prefix_values.reshape(prefix_count, HEADS, HEAD_DIM)

    def attend(first_pos):
        query_block = lax.dynamic_slice_in_dim(queries, first_pos, block_rows, 0).reshape(block_rows, HEADS, HEAD_DIM)
        query_labels = lax.dynamic_slice_in_dim(labels, first_pos, block_rows, 0)
        key_block = lax.dynamic_slice_in_dim(pad_keys, first_pos, window, 0).reshape(window, HEADS, HEAD_DIM)
        value_block = lax.dynamic_slice_in_dim(pad_values, first_pos, window, 0).reshape(window, HEADS, HEAD_DIM)
        key_labels = lax.dynamic_slice_in_dim(pad_labels, first_pos, window, 0)
        token_scores = jnp.einsum('qhd,khd->hqk', query_block, key_block, precision=highest) * score_scale
        allowed = query_labels[:, None] == key_labels[None, :]
        token_scores = jnp.where(allowed[None], token_scores, masked_fill)
        prefix_scores = jnp.einsum('qhd,khd->hqk', query_block, head_keys, precision=highest) * score_scale
        scores = low_back(jnp.concatenate([prefix_scores, token_scores], axis=-1))
        row_max = lax.optimization_barrier(jnp.max(scores, axis=-1, keepdims=True))
        exponent = jnp.exp(scores - row_max)
        probs = low(exponent / lax.optimization_barrier(jnp.sum(exponent, axis=-1, keepdims=True)))
        mixed = jnp.einsum('hqk,khd->qhd', probs[..., :prefix_count], head_values, precision=highest)
        mixed = mixed + jnp.einsum('hqk,khd->qhd', probs[..., prefix_count:], value_block, precision=highest)
        return mixed.reshape(block_rows, HEADS * HEAD_DIM)
    starts = jnp.arange(length // block_rows, dtype=jnp.int32) * block_rows
    attended = lax.map(jax.checkpoint(attend), starts).reshape(length, HEADS * HEAD_DIM)
    attended = low_back(low(attended))
    hidden_in = inputs + low_back(matmul(attended, w_out) + b_out)
    normed = layer_norm(hidden_in, gain_attn, shift_attn)

    def ffn_block(rows_in):
        pre_act = low_back(matmul(low(rows_in), w_up) + b_up)
        activated = low(jax.nn.gelu(pre_act, approximate=False))
        return rows_in + low_back(matmul(activated, w_down) + b_down)
    ffn_rows = math.gcd(4096, length)
    summed = lax.map(jax.checkpoint(ffn_block), normed.reshape(length // ffn_rows, ffn_rows, -1))
    summed = summed.reshape(length, -1)
    return layer_norm(summed, gain_ffn, shift_ffn)

def reference(tokens, cotangent, pair_lengths, prefix_key, prefix_value, w_query, b_query, w_key, w_value, b_value, w_out, b_out, gain_attn, shift_attn, w_up, b_up, w_down, b_down, gain_ffn, shift_ffn):
    params = tuple((to_float(array) for array in (w_query, b_query, w_key, w_value, b_value, w_out, b_out, gain_attn, shift_attn, w_up, b_up, w_down, b_down, gain_ffn, shift_ffn)))
    row_length = tokens.shape[1]
    places = jnp.arange(row_length, dtype=jnp.int32)
    pair_ends = jnp.cumsum(pair_lengths, axis=1).astype(jnp.int32)
    labels = lax.optimization_barrier(jnp.sum((places[None, :, None] >= pair_ends[:, None, :]).astype(jnp.int32), axis=2))
    prefix_keys = to_float(prefix_key)
    prefix_values = to_float(prefix_value)

    def one_row(row_items):
        row_in, row_labels, row_cot = row_items
        outputs, pull_back = jax.vjp(lambda first, second, third: row_forward(first, row_labels, second, third, params), row_in, prefix_keys, prefix_values)
        gradients = pull_back(row_cot)
        return (outputs, gradients[0], gradients[1], gradients[2])
    outputs, grad_rows, grad_pkeys, grad_pvalues = lax.map(one_row, (to_float(tokens), labels, to_float(cotangent)))
    return (outputs.astype(jnp.bfloat16), grad_rows.astype(jnp.bfloat16), lax.optimization_barrier(jnp.sum(grad_pkeys, axis=0)), lax.optimization_barrier(jnp.sum(grad_pvalues, axis=0)))
```

```python
import functools

import jax
import jax.numpy as jnp
from jax import lax
from jax.experimental import pallas as pl
from jax.experimental.pallas import tpu as pltpu
from jax.sharding import PartitionSpec as P

HEAD = 64
SCALE = HEAD**-0.5
LN_EPS = 1e-05
MASKED = -1e30
TILE = 256
CHUNK = 512

f32 = jnp.float32
bf16 = jnp.bfloat16
VM = pl.BlockSpec(memory_space=pltpu.VMEM)
SM = pl.BlockSpec(memory_space=pltpu.SMEM)
HB = pl.BlockSpec(memory_space=pl.ANY)


def shape_of(shape, kind):
    return jax.ShapeDtypeStruct(shape, kind)


def dot(a, b, ca=1, cb=0):
    return lax.dot_general(a, b, (((ca,), (cb,)), ((), ())), preferred_element_type=f32)


def row_at(offset, rows):
    return pl.ds(pl.multiple_of(offset, 64), rows)


def start_all(pairs, sems):
    made = [pltpu.make_async_copy(s, d, sems.at[i]) for i, (s, d) in enumerate(pairs)]
    for one in made:
        one.start()
    return made


def wait_all(made):
    for one in made:
        one.wait()


def normalised(v):
    centred = v - jnp.mean(v, axis=-1, keepdims=True)
    inv = lax.rsqrt(jnp.mean(centred * centred, axis=-1, keepdims=True) + LN_EPS)
    return centred * inv, inv


def norm_back(g, n, inv):
    return (g - jnp.mean(g, -1, keepdims=True) - n * jnp.mean(g * n, -1, keepdims=True)) * inv


def project_kernel(info, bq, bv, pk, pv, *rest, count, half):
    tok_in = rest[:6]
    own, mate = rest[6:9], rest[9:12]
    pieces = rest[12 : 12 + count]
    (q_ref, qt_ref, k_ref, kt_ref, v_ref, vt_ref, pk_ref, pkt_ref, pv_ref, pvt_ref, w_ref) = rest[
        12 + count : 23 + count
    ]
    tok, sem_x, sem_w = rest[23 + count :]
    core = info[0]
    tokens = tok_in[0].shape[0]
    width = tok.shape[1]
    pairs = []
    for i in range(6):
        slot = 2 * (i % 3) + (core if i < 3 else 1 - core)
        pairs.append((tok_in[i], tok.at[row_at(slot * tokens, tokens), :]))
    got_tok = start_all(pairs, sem_x)
    cols = pl.multiple_of(core * half, 128)
    got_w = []
    for i in (1, 2, 0):
        pairs = []
        for j, ref in enumerate((own[i], mate[i])):
            pairs.append((ref.at[:, pl.ds(cols, half)], w_ref.at[i, row_at(info[1 + j], ref.shape[0]), :]))
        for j, ref in enumerate(pieces):
            pairs.append(
                (
                    ref.at[:, pl.ds(i * width + cols, half)],
                    w_ref.at[i, row_at(info[3 + j], ref.shape[0]), :],
                )
            )
        got_w.append(start_all(pairs, sem_w.at[i]))
    pk_half, pv_half = pk[:, pl.ds(cols, half)], pv[:, pl.ds(cols, half)]
    pk_ref[...], pkt_ref[...] = pk_half, pk_half.astype(f32).T.astype(bf16)
    pv_ref[...], pvt_ref[...] = pv_half, pv_half.astype(f32).T.astype(bf16)
    wait_all(got_tok)
    bias_v = bv[:, pl.ds(cols, half)].astype(f32)
    bias_q = bq[:, pl.ds(cols, half)].astype(f32)
    blocks = k_ref.shape[0] // TILE
    wait_all(got_w[0])

    def key_block(b, carry):
        at = pl.ds(pl.multiple_of(b * TILE, TILE), TILE)
        full = dot(tok[at, :], w_ref[1])
        k_ref[at, :] = full.astype(bf16)
        kt_ref[:, at] = full.T.astype(bf16)
        return carry

    lax.fori_loop(0, blocks, key_block, 0)
    wait_all(got_w[1])

    def value_block(b, carry):
        at = pl.ds(pl.multiple_of(b * TILE, TILE), TILE)
        full = dot(tok[at, :], w_ref[2]) + bias_v
        v_ref[at, :] = full.astype(bf16)
        vt_ref[:, at] = full.T.astype(bf16)
        return carry

    lax.fori_loop(0, blocks, value_block, 0)
    wait_all(got_w[2])

    def query_block(b, carry):
        at = pl.ds(pl.multiple_of(b * TILE, TILE), TILE)
        src = pl.ds(pl.multiple_of(b * TILE + 2 * tokens, TILE), TILE)
        full = (dot(tok[src, :], w_ref[0]) + bias_q).astype(bf16).astype(f32) * SCALE
        q_ref[at, :] = full.astype(bf16)
        qt_ref[:, at] = full.T.astype(bf16)
        return carry

    lax.fori_loop(0, 2 * tokens // TILE, query_block, 0)


def project(info, bq, bv, pk, pv, toks, own, mate, pieces):
    tokens, width = toks[0].shape
    half = width // 2
    pre = pk.shape[0]
    n_q, n_k = 2 * tokens, 6 * tokens
    count = len(pieces)
    outs = [(n_q, half), (half, n_q), (n_k, half), (half, n_k), (n_k, half), (half, n_k)]
    outs += [(pre, half), (half, pre), (pre, half), (half, pre), (3, width, half)]
    return pl.pallas_call(
        functools.partial(project_kernel, count=count, half=half),
        out_shape=tuple(shape_of(s, bf16) for s in outs),
        in_specs=[SM] + [VM] * 4 + [HB] * (12 + count),
        out_specs=(VM,) * len(outs),
        scratch_shapes=[
            pltpu.VMEM((n_k, width), bf16),
            pltpu.SemaphoreType.DMA((6,)),
            pltpu.SemaphoreType.DMA((3, 2 + count)),
        ],
        compiler_params=pltpu.CompilerParams(vmem_limit_bytes=48 << 20),
        name="project",
    )(info, bq, bv, pk, pv, *toks, *own, *mate, *pieces)


def head_rows(ref, h, at):
    own = ref[pl.ds(h * HEAD, HEAD), at]
    zero = jnp.zeros_like(own)
    return jnp.concatenate([own, zero] if h % 2 == 0 else [zero, own], 0)


def head_cols(ref, h, at):
    block = ref[at, pl.ds((h // 2) * 2 * HEAD, 2 * HEAD)]
    lane = lax.broadcasted_iota(jnp.int32, block.shape, 1)
    return jnp.where((lane < HEAD) == (h % 2 == 0), block, jnp.zeros_like(block))


def pair_cols(h):
    return pl.ds((h // 2) * 2 * HEAD, 2 * HEAD)


def allowed_bias(k0, first, last):
    place = k0 + lax.broadcasted_iota(jnp.int32, (TILE, TILE), 0)
    return jnp.where((place >= first) & (place < last), 0.0, MASKED).astype(f32)


def forward_kernel(
    info, first, last, qt_ref, k_ref, vt_ref, pk_ref, pvt_ref, keep_ref, send_ref, ot_ref, lse_ref,
    stat, acc, bias, *, heads,
):
    tokens = keep_ref.shape[0]

    def one_query_tile(t, carry):
        at = pl.ds(pl.multiple_of(t * TILE, TILE), TILE)
        qs, qe = first[:, at], last[:, at]
        for h in range(heads):
            s = dot(pk_ref[:, pair_cols(h)], head_rows(qt_ref, h, at))
            top = jnp.max(s, axis=0, keepdims=True)
            p = jnp.exp(s - top)
            stat[pl.ds(h, 1), :] = top
            stat[pl.ds(heads + h, 1), :] = jnp.sum(p, axis=0, keepdims=True)
            acc[pl.ds(h * HEAD, HEAD), :] = dot(pvt_ref[pl.ds(h * HEAD, HEAD), :], p.astype(bf16))

        def one_key_tile(j, inner):
            k0 = pl.multiple_of(j * TILE, TILE)
            bias[...] = allowed_bias(k0, qs, qe)
            for h in range(heads):
                s = dot(k_ref[pl.ds(k0, TILE), pair_cols(h)], head_rows(qt_ref, h, at)) + bias[...]
                old = stat[pl.ds(h, 1), :]
                top = jnp.maximum(old, jnp.max(s, axis=0, keepdims=True))
                factor = jnp.exp(old - top)
                p = jnp.exp(s - top)
                stat[pl.ds(h, 1), :] = top
                stat[pl.ds(heads + h, 1), :] = stat[pl.ds(heads + h, 1), :] * factor + jnp.sum(
                    p, axis=0, keepdims=True
                )
                rows = pl.ds(h * HEAD, HEAD)
                acc[rows, :] = acc[rows, :] * factor + dot(
                    vt_ref[rows, pl.ds(k0, TILE)], p.astype(bf16)
                )
            return inner

        lax.fori_loop(info[1 + 2 * t], info[2 + 2 * t], one_key_tile, 0)
        for h in range(heads):
            rows = pl.ds(h * HEAD, HEAD)
            acc[rows, :] = acc[rows, :] / stat[pl.ds(heads + h, 1), :]
        ot_ref[:, at] = acc[...]
        lse_ref[:, at] = stat[pl.ds(0, heads), :] + jnp.log(stat[pl.ds(heads, heads), :])
        low = acc[...].T.astype(bf16)
        side = (t * TILE) // tokens
        rows = pl.ds(pl.multiple_of(t * TILE - side * tokens, TILE), TILE)

        @pl.when(side == info[0])
        def _():
            keep_ref[rows, :] = low

        @pl.when(side != info[0])
        def _():
            send_ref[rows, :] = low

        return carry

    lax.fori_loop(0, 2 * tokens // TILE, one_query_tile, 0)


def attend(info, first, last, qt, k, vt, pk, pvt):
    half, n_q = qt.shape
    heads = half // HEAD
    return pl.pallas_call(
        functools.partial(forward_kernel, heads=heads),
        out_shape=(
            shape_of((n_q // 2, half), bf16),
            shape_of((n_q // 2, half), bf16),
            shape_of((half, n_q), f32),
            shape_of((heads, n_q), f32),
        ),
        in_specs=[SM] + [VM] * 7,
        out_specs=(VM,) * 4,
        scratch_shapes=[
            pltpu.VMEM((2 * heads, TILE), f32),
            pltpu.VMEM((half, TILE), f32),
            pltpu.VMEM((TILE, TILE), f32),
        ],
        compiler_params=pltpu.CompilerParams(vmem_limit_bytes=40 << 20),
        name="attend",
    )(info, first, last, qt, k, vt, pk, pvt)


def tile_grads(h, k_b, v_b, kt_b, bias, qt_m, dot_m, q_m, do_m, lse, inner):
    s = dot(k_b, qt_m)
    if bias is not None:
        s = s + bias
    p = jnp.exp(s - lse)
    ds = (p * (dot(v_b, dot_m) - inner)).astype(bf16)
    return dot(p.astype(bf16), do_m), dot(ds, q_m), dot(kt_b, ds)


def sweep(ranges, at, first, last, refs, acc, heads):
    q_ref, qt_ref, k_ref, kt_ref, v_ref, do_ref, dot_ref, lse_ref, inner_ref, bias = refs
    dqt, dk, dv = acc
    qs, qe = first[:, at], last[:, at]

    def one_key_tile(j, carry):
        k0 = pl.multiple_of(j * TILE, TILE)
        r = pl.ds(k0, TILE)
        bias[...] = allowed_bias(k0, qs, qe)
        for h in range(heads):
            c, rows = pair_cols(h), pl.ds(h * HEAD, HEAD)
            gv, gk, gq = tile_grads(
                h, k_ref[r, c], v_ref[r, c], kt_ref[rows, r], bias[...], head_rows(qt_ref, h, at),
                head_rows(dot_ref, h, at), head_cols(q_ref, h, at), head_cols(do_ref, h, at),
                lse_ref[pl.ds(h, 1), at], inner_ref[pl.ds(h, 1), at],
            )
            dv[r, c] += gv
            dk[r, c] += gk
            dqt[rows, at] += gq
        return carry

    for lo, hi in ranges:
        lax.fori_loop(lo, hi, one_key_tile, 0)


def remote_grads_kernel(
    info, first, last, q_ref, qt_ref, k_ref, kt_ref, v_ref, pk_ref, pkt_ref, pv_ref, keep_in, recv_in,
    ot_ref, lse_ref, w_in, give_ref, keep_lo, keep_hi, pre_ref, dqt, do_s, dot_s, inner_s, dk, dv, bias,
    wsc, wsem, *, heads,
):
    copies = start_all([(w_in.at[1], wsc.at[0]), (w_in.at[2], wsc.at[1])], wsem)
    core = info[0]
    tokens = keep_in.shape[0]
    n_q, pre = q_ref.shape[0], pk_ref.shape[0]
    do_s[row_at(core * tokens, tokens), :] = keep_in[...]
    do_s[row_at((1 - core) * tokens, tokens), :] = recv_in[...]
    dk[...] = jnp.zeros_like(dk)
    dv[...] = jnp.zeros_like(dv)
    pre_ref[...] = jnp.zeros_like(pre_ref)

    def one_query_tile(t, carry):
        at = pl.ds(pl.multiple_of(t * TILE, TILE), TILE)
        dot_s[:, at] = do_s[at, :].astype(f32).T.astype(bf16)
        for h in range(heads):
            rows = pl.ds(h * HEAD, HEAD)
            inner_s[pl.ds(h, 1), at] = jnp.sum(
                dot_s[rows, at].astype(f32) * ot_ref[rows, at], axis=0, keepdims=True
            )
        for h in range(heads):
            c, rows = pair_cols(h), pl.ds(h * HEAD, HEAD)
            gv, gk, gq = tile_grads(
                h, pk_ref[:, c], pv_ref[:, c], pkt_ref[rows, :], None, head_rows(qt_ref, h, at),
                head_rows(dot_s, h, at), head_cols(q_ref, h, at), head_cols(do_s, h, at),
                lse_ref[pl.ds(h, 1), at], inner_s[pl.ds(h, 1), at],
            )
            pre_ref[pl.ds(0, pre), c] += gk
            pre_ref[pl.ds(pre, pre), c] += gv
            dqt[rows, at] = gq
        lo, hi = info[1 + 2 * t], info[2 + 2 * t]
        side = 2 * tokens // TILE
        refs = (q_ref, qt_ref, k_ref, kt_ref, v_ref, do_s, dot_s, lse_ref, inner_s, bias)
        ranges = ((lo, jnp.minimum(hi, side)), (jnp.maximum(lo, 2 * side), hi))
        sweep(ranges, at, first, last, refs, (dqt, dk, dv), heads)
        return carry

    lax.fori_loop(0, n_q // TILE, one_query_tile, 0)
    wait_all(copies)
    for i, keep in ((0, keep_lo), (1, keep_hi)):
        for mine in (True, False):
            block = core if mine else 1 - core
            r = row_at(i * 4 * tokens + block * tokens, tokens)
            out = dot(dk[r, :].astype(bf16), wsc[0], 1, 1) + dot(dv[r, :].astype(bf16), wsc[1], 1, 1)
            if mine:
                keep[...] = out
            else:
                give_ref[pl.ds(i * tokens, tokens), :] = out.astype(bf16)


def remote_grads(info, first, last, q, qt, k, kt, v, pk, pkt, pv, keep, recv, ot, lse, w):
    n_q, half = q.shape
    heads, tokens, width = half // HEAD, n_q // 2, w.shape[1]
    n_k, pre = k.shape[0], pk.shape[0]
    return pl.pallas_call(
        functools.partial(remote_grads_kernel, heads=heads),
        out_shape=(
            shape_of((2 * tokens, width), bf16),
            shape_of((tokens, width), f32),
            shape_of((tokens, width), f32),
            shape_of((2 * pre, half), f32),
            shape_of((half, n_q), f32),
            shape_of((n_q, half), bf16),
            shape_of((half, n_q), bf16),
            shape_of((heads, n_q), f32),
        ),
        in_specs=[SM] + [VM] * 14 + [HB],
        out_specs=(VM,) * 8,
        scratch_shapes=[
            pltpu.VMEM((n_k, half), f32),
            pltpu.VMEM((n_k, half), f32),
            pltpu.VMEM((TILE, TILE), f32),
            pltpu.VMEM((2, width, half), bf16),
            pltpu.SemaphoreType.DMA((2,)),
        ],
        compiler_params=pltpu.CompilerParams(vmem_limit_bytes=52 << 20),
        name="remote_grads",
    )(info, first, last, q, qt, k, kt, v, pk, pkt, pv, keep, recv, ot, lse, w)


def local_grads_kernel(
    info, first, last, q_ref, qt_ref, k_ref, kt_ref, v_ref, do_ref, dot_ref, lse_ref, inner_ref, dqt_in,
    gh_ref, w_in, keep_ref, give_ref, dqt, dk, dv, bias, wsc, wsem, *, heads,
):
    copies = start_all([(w_in, wsc)], wsem)
    core = info[0]
    n_q = q_ref.shape[0]
    tokens = n_q // 2
    dqt[...] = dqt_in[...]
    dk[...] = jnp.zeros_like(dk)
    dv[...] = jnp.zeros_like(dv)
    side = 2 * tokens // TILE

    def one_query_tile(t, carry):
        at = pl.ds(pl.multiple_of(t * TILE, TILE), TILE)
        lo, hi = info[1 + 2 * t], info[2 + 2 * t]
        refs = (q_ref, qt_ref, k_ref, kt_ref, v_ref, do_ref, dot_ref, lse_ref, inner_ref, bias)
        ranges = ((jnp.maximum(lo, side), jnp.minimum(hi, 2 * side)),)
        sweep(ranges, at, first, last, refs, (dqt, dk, dv), heads)
        return carry

    lax.fori_loop(0, n_q // TILE, one_query_tile, 0)
    wait_all(copies)
    for mine in (False, True):
        block = core if mine else 1 - core
        r = row_at(block * tokens, tokens)
        rk = row_at(block * tokens + n_q, tokens)
        dq = (dqt[:, r] * SCALE).T.astype(bf16)
        out = (
            dot(dq, wsc[0], 1, 1)
            + dot(dk[rk, :].astype(bf16), wsc[1], 1, 1)
            + dot(dv[rk, :].astype(bf16), wsc[2], 1, 1)
        )
        if mine:
            keep_ref[...] = out + gh_ref[...]
        else:
            give_ref[...] = out.astype(bf16)


def local_grads(info, first, last, q, qt, k, kt, v, do, dot_, lse, inner, dqt, gh, w):
    n_q, half = q.shape
    heads, tokens, width = half // HEAD, n_q // 2, w.shape[1]
    n_k = k.shape[0]
    return pl.pallas_call(
        functools.partial(local_grads_kernel, heads=heads),
        out_shape=(shape_of((tokens, width), f32), shape_of((tokens, width), bf16)),
        in_specs=[SM] + [VM] * 13 + [HB],
        out_specs=(VM,) * 2,
        scratch_shapes=[
            pltpu.VMEM((half, n_q), f32),
            pltpu.VMEM((n_k, half), f32),
            pltpu.VMEM((n_k, half), f32),
            pltpu.VMEM((TILE, TILE), f32),
            pltpu.VMEM((3, width, half), bf16),
            pltpu.SemaphoreType.DMA((1,)),
        ],
        compiler_params=pltpu.CompilerParams(vmem_limit_bytes=52 << 20),
        name="local_grads",
    )(info, first, last, q, qt, k, kt, v, do, dot_, lse, inner, dqt, gh, w)


def placed(refs, info, at, scale, dst, src_cols=None, dst_cols=None):
    pairs = []
    for i, ref in enumerate(refs):
        src = ref if src_cols is None else ref.at[:, src_cols]
        rows = row_at(info[at + i] * scale, ref.shape[0])
        pairs.append((src, dst.at[rows, :] if dst_cols is None else dst.at[rows, dst_cols]))
    return pairs


def out_pairs(parts, info, width, dst):
    return placed(parts[:2], info, 1, 1, dst) + placed(
        parts[2:], info, 3, 1, dst, pl.ds(3 * width, width)
    )


def up_kernel(info, own_att, got_att, tok, bo, ga, sa, bu, *rest, count):
    wo, wu = rest[:count], rest[count : 2 * count]
    nrm_ref, hat_ref, inv_ref, act_ref, slope_ref, wo_s, wu_s, sem_o, sem_u = rest[2 * count :]
    width, ff = wu_s.shape
    half = own_att.shape[1]
    got_o = start_all(out_pairs(wo, info, width, wo_s), sem_o)
    got_u = []
    for j in range(ff // width):
        cs = pl.ds(j * width, width)
        got_u.append(start_all(placed(wu, info, 1, 1, wu_s, cs, cs), sem_u.at[j]))
    core = info[0]
    wait_all(got_o)
    hidden = (
        tok[...].astype(f32)
        + dot(own_att[...], wo_s[row_at(core * half, half), :])
        + dot(got_att[...], wo_s[row_at((1 - core) * half, half), :])
        + bo[...].astype(f32)
    )
    hat, inv = normalised(hidden)
    hat_ref[...] = hat
    inv_ref[...] = jnp.broadcast_to(inv, inv_ref.shape)
    nrm = hat * ga[...].astype(f32) + sa[...].astype(f32)
    nrm_ref[...] = nrm
    low = nrm.astype(bf16)
    for j in range(ff // CHUNK):
        if (j * CHUNK) % width == 0:
            wait_all(got_u[j * CHUNK // width])
        cs = pl.ds(j * CHUNK, CHUNK)
        v = dot(low, wu_s[:, cs]) + bu[:, cs].astype(f32)
        phi = 0.5 + 0.5 * lax.erf(v * (0.5**0.5))
        act_ref[:, cs] = (v * phi).astype(bf16)
        slope_ref[:, cs] = (phi + v * (jnp.exp(v * v * -0.5) * 0.3989422804014327)).astype(bf16)


def up(info, own_att, got_att, tok, bo, ga, sa, bu, wo, wu):
    tokens, width = tok.shape
    ff, count = bu.shape[1], len(wo)
    return pl.pallas_call(
        functools.partial(up_kernel, count=count),
        out_shape=(
            shape_of((tokens, width), f32),
            shape_of((tokens, width), f32),
            shape_of((tokens, 128), f32),
            shape_of((tokens, ff), bf16),
            shape_of((tokens, ff), bf16),
        ),
        in_specs=[SM] + [VM] * 7 + [HB] * (2 * count),
        out_specs=(VM,) * 5,
        scratch_shapes=[
            pltpu.VMEM((width, width), bf16),
            pltpu.VMEM((width, ff), bf16),
            pltpu.SemaphoreType.DMA((count,)),
            pltpu.SemaphoreType.DMA((ff // width, count)),
        ],
        compiler_params=pltpu.CompilerParams(vmem_limit_bytes=50 << 20),
        name="up",
    )(info, own_att, got_att, tok, bo, ga, sa, bu, *wo, *wu)


def down_kernel(info, nrm_ref, hat_ref, inv_ref, act_ref, slope_ref, cot, bd, gf, sf, ga, *rest, count):
    wo, wu, wd = rest[:count], rest[count : 2 * count], rest[2 * count : 3 * count]
    out_ref, gh_ref, keep_ref, send_ref, wo_s, wu_s, wd_s, sem_o, sem_u, sem_d = rest[3 * count :]
    width, ff = wu_s.shape
    half = keep_ref.shape[1]
    got_d = start_all(placed(wd, info, 1, ff // width, wd_s), sem_d)
    got_u = start_all(placed(wu, info, 1, 1, wu_s), sem_u)
    got_o = start_all(out_pairs(wo, info, width, wo_s), sem_o)
    core = info[0]
    wait_all(got_d)
    summed = nrm_ref[...] + dot(act_ref[...], wd_s[...]) + bd[...].astype(f32)
    n, inv = normalised(summed)
    gain = gf[...].astype(f32)
    out_ref[...] = (n * gain + sf[...].astype(f32)).astype(bf16)
    gs = norm_back(cot[...].astype(f32) * gain, n, inv)
    low = gs.astype(bf16)
    wait_all(got_u)
    total = gs
    for j in range(ff // CHUNK):
        cs = pl.ds(j * CHUNK, CHUNK)
        gp = (dot(low, wd_s[cs, :], 1, 1) * slope_ref[:, cs].astype(f32)).astype(bf16)
        total = total + dot(gp, wu_s[:, cs], 1, 1)
    gh = norm_back(total * ga[...].astype(f32), hat_ref[...], inv_ref[:, :1])
    gh_ref[...] = gh
    gh_low = gh.astype(bf16)
    wait_all(got_o)
    send_ref[...] = dot(gh_low, wo_s[row_at((1 - core) * half, half), :], 1, 1).astype(bf16)
    keep_ref[...] = dot(gh_low, wo_s[row_at(core * half, half), :], 1, 1).astype(bf16)


def down(info, nrm, hat, inv, act, slope, cot, bd, gf, sf, ga, wo, wu, wd):
    tokens, width = nrm.shape
    ff, count = act.shape[1], len(wo)
    return pl.pallas_call(
        functools.partial(down_kernel, count=count),
        out_shape=(
            shape_of((tokens, width), bf16),
            shape_of((tokens, width), f32),
            shape_of((tokens, width // 2), bf16),
            shape_of((tokens, width // 2), bf16),
        ),
        in_specs=[SM] + [VM] * 10 + [HB] * (3 * count),
        out_specs=(VM,) * 4,
        scratch_shapes=[
            pltpu.VMEM((width, width), bf16),
            pltpu.VMEM((width, ff), bf16),
            pltpu.VMEM((ff, width), bf16),
            pltpu.SemaphoreType.DMA((count,)),
            pltpu.SemaphoreType.DMA((count,)),
            pltpu.SemaphoreType.DMA((count,)),
        ],
        compiler_params=pltpu.CompilerParams(vmem_limit_bytes=58 << 20),
        name="down",
    )(info, nrm, hat, inv, act, slope, cot, bd, gf, sf, ga, *wo, *wu, *wd)


def per_device(
    tokens, cotangent, pair_lengths, prefix_key, prefix_value, w_query, b_query, w_key, w_value, b_value,
    w_out, b_out, gain_attn, shift_attn, w_up, b_up, w_down, b_down, gain_ffn, shift_ffn,
):
    n_row, n_seq = lax.axis_size("row"), lax.axis_size("seq")
    r, s = lax.axis_index("row"), lax.axis_index("seq")
    core, x, zbit = r & 1, s & 1, (s >> 1) & 1
    tok_count, width = tokens.shape[1], tokens.shape[2]

    def by_core(a):
        return lax.ppermute(a, "row", [(i, i ^ 1) for i in range(n_row)])

    def by_y(a):
        return lax.ppermute(a, "row", [(i, i ^ 2) for i in range(n_row)])

    def by_seq(a, bit):
        return lax.ppermute(a, "seq", [(i, i ^ bit) for i in range(n_seq)])

    def swapped(a, shift):
        route = []
        for i in range(n_row):
            for j in range(n_seq):
                to = (j | 1) + 2 * shift - 1
                if 0 <= to < n_seq:
                    route.append((i * n_seq + j, ((i & ~1) | (j & 1)) * n_seq + to + (i & 1)))
        return lax.ppermute(a, ("row", "seq"), route)

    own = swapped(tokens[0], 0)
    below = lax.ppermute(own, "seq", [(j, j + 2) for j in range(n_seq - 2)])
    above = lax.ppermute(own, "seq", [(j + 2, j) for j in range(n_seq - 2)])
    toks = [below, own, above]
    toks = toks + [by_core(a) for a in toks]
    cot = swapped(cotangent[0], 0)

    h = x ^ zbit
    first_q, second_q = 2 * h + x, 2 * h + 1 - x

    def quarter(shards, which):
        rows = shards[0].shape[0] // 4
        cut = [lax.dynamic_slice_in_dim(a, which * rows, rows, 0) for a in shards]
        return cut[0] if len(cut) == 1 else jnp.concatenate(cut, 1)

    groups = ((w_query, w_key, w_value, w_out), (w_up,), (w_down,))
    gathered = []
    for shards in groups:
        one = by_y(quarter(shards, first_q))
        two = by_y(quarter(shards, second_q))
        got = [one, two, by_seq(one, 1), by_seq(one, 2)]
        gathered.append(got + [by_core(a) for a in got])
    mates = [by_core(a) for a in (w_query, w_key, w_value, w_out, w_up, w_down)]
    m = w_query.shape[0]
    offsets = [r * m, (r ^ 1) * m]
    for base in ((r ^ 2) * m, (r ^ 3) * m):
        for which in (first_q, second_q, 2 * (1 - h) + 1 - x, 2 * (1 - h) + x):
            offsets.append(base + which * (m // 4))

    theirs = by_core(pair_lengths)
    lengths = jnp.where(x == core, pair_lengths, theirs)[0]
    pairs = lengths.shape[0]
    later = jnp.arange(pairs)[:, None] >= jnp.arange(pairs)[None, :]
    ends = jnp.sum(jnp.where(later, lengths[None, :], 0), axis=1)
    base = (s // 2) * 2 * tok_count
    place = base + jnp.arange(2 * tok_count, dtype=jnp.int32)
    passed = ends[:, None] <= place[None, :]
    origin = base - 2 * tok_count
    first = jnp.max(jnp.where(passed, ends[:, None], 0), axis=0) - origin
    last = jnp.min(jnp.where(passed, n_seq * tok_count, ends[:, None]), axis=0) - origin
    bounds = jnp.stack([first[::TILE] // TILE, (last[TILE - 1 :: TILE] + TILE - 1) // TILE], 1)
    tile_info = jnp.concatenate([core[None], bounds.reshape(-1)]).astype(jnp.int32)
    info = jnp.stack([core] + offsets).astype(jnp.int32)
    first, last = first[None], last[None]

    def row(a):
        return a.reshape(1, -1)

    q, qt, k, kt, v, vt, pk, pkt, pv, pvt, w_half = project(
        info, row(b_query), row(b_value), prefix_key, prefix_value, toks,
        (w_query, w_key, w_value), mates[:3], gathered[0],
    )
    att_keep, att_send, ot, lse = attend(tile_info, first, last, qt, k, vt, pk, pvt)
    parts_o = [w_out, mates[3]] + gathered[0]
    parts_u = [w_up, mates[4]] + gathered[1]
    parts_d = [w_down, mates[5]] + gathered[2]
    nrm, hat, inv, act, slope = up(
        info, att_keep, by_core(att_send), own, row(b_out), row(gain_attn), row(shift_attn), row(b_up),
        parts_o, parts_u,
    )
    result, gh, ga_keep, ga_send = down(
        info, nrm, hat, inv, act, slope, cot, row(b_down), row(gain_ffn), row(shift_ffn), row(gain_attn),
        parts_o, parts_u, parts_d,
    )
    out_tokens = swapped(result, 0)
    give, keep_lo, keep_hi, pre, dqt, do, dot_, inner = remote_grads(
        tile_info, first, last, q, qt, k, kt, v, pk, pkt, pv, ga_keep, by_core(ga_send), ot, lse, w_half
    )
    got = by_core(give)
    low_part = swapped((keep_lo + got[:tok_count].astype(f32)).astype(bf16), -1)
    high_part = swapped((keep_hi + got[tok_count:].astype(f32)).astype(bf16), 1)

    def added(a, exchange):
        low = a.astype(bf16)
        return low.astype(f32) + exchange(low).astype(f32)

    pre = added(pre, by_y)
    bit = 1
    while bit < n_seq:
        pre = added(pre, functools.partial(by_seq, bit=bit))
        bit *= 2
    other = by_core(pre)
    pre = jnp.concatenate(
        [jnp.where(core == 0, pre, other), jnp.where(core == 0, other, pre)], axis=1
    )

    keep, give = local_grads(
        tile_info, first, last, q, qt, k, kt, v, do, dot_, lse, inner, dqt, gh, w_half
    )
    mine = swapped((keep + by_core(give).astype(f32)).astype(bf16), 0)
    grad_tokens = (mine.astype(f32) + low_part.astype(f32) + high_part.astype(f32)).astype(bf16)
    n_pre = prefix_key.shape[0]
    return out_tokens[None], grad_tokens[None], pre[:n_pre], pre[n_pre:]


def solution(mesh):
    both, split, whole = P("row", "seq", None), P("row", None), P()
    return jax.shard_map(
        per_device,
        mesh=mesh,
        in_specs=(
            both, both, split, whole, whole, split, whole, split, split, whole, split, whole, whole, whole,
            split, whole, split, whole, whole, whole,
        ),
        out_specs=(both, both, whole, whole),
        check_vma=False,
    )
```

```python
import functools

import jax
import jax.numpy as jnp
from jax import lax
from jax.experimental import pallas as pl
from jax.experimental.pallas import tpu as pltpu
from jax.sharding import PartitionSpec as P

HEAD = 64
SCALE = HEAD**-0.5
LN_EPS = 1e-05
MASKED = -1e30
TILE = 256
CHUNK = 512
GRAD_LAGS = (0, 1, 2)

f32 = jnp.float32
bf16 = jnp.bfloat16
VM = pl.BlockSpec(memory_space=pltpu.VMEM)
SM = pl.BlockSpec(memory_space=pltpu.SMEM)
HB = pl.BlockSpec(memory_space=pl.ANY)


def cost(us):
    return pl.CostEstimate(flops=int(us * 1e9), bytes_accessed=0, transcendentals=0)


def shape_of(shape, kind):
    return jax.ShapeDtypeStruct(shape, kind)


def dot(a, b, ca=1, cb=0):
    return lax.dot_general(a, b, (((ca,), (cb,)), ((), ())), preferred_element_type=f32)


def row_at(offset, rows):
    return pl.ds(pl.multiple_of(offset, 64), rows)


def start_all(pairs, sems):
    made = [pltpu.make_async_copy(s, d, sems.at[i]) for i, (s, d) in enumerate(pairs)]
    for one in made:
        one.start()
    return made


def wait_all(made):
    for one in made:
        one.wait()


def normalised(v):
    centred = v - jnp.mean(v, axis=-1, keepdims=True)
    inv = lax.rsqrt(jnp.mean(centred * centred, axis=-1, keepdims=True) + LN_EPS)
    return centred * inv, inv


def norm_back(g, n, inv):
    return (g - jnp.mean(g, -1, keepdims=True) - n * jnp.mean(g * n, -1, keepdims=True)) * inv


def pack_kernel(info, *rest, plan, n_in):
    srcs, outs, sem = rest[:n_in], rest[n_in:-1], rest[-1]
    pairs = []
    for i, which, o, col in plan:
        rows, cols = outs[o].shape[0], srcs[i].shape[1]
        pairs.append((srcs[i].at[row_at(info[which] * rows, rows), :], outs[o].at[:, pl.ds(col, cols)]))
    wait_all(start_all(pairs, sem))


def pack(info, srcs, shapes, plan):
    return pl.pallas_call(
        functools.partial(pack_kernel, plan=plan, n_in=len(srcs)),
        out_shape=tuple(shape_of(a, bf16) for a in shapes),
        in_specs=[SM] + [HB] * len(srcs),
        out_specs=(VM,) * len(shapes),
        scratch_shapes=[pltpu.SemaphoreType.DMA((len(plan),))],
        name="pack",
        cost_estimate=cost(2),
    )(info, *srcs)


def head_rows(ref, h, at):
    own = ref[pl.ds(h * HEAD, HEAD), at]
    zero = jnp.zeros_like(own)
    return jnp.concatenate([own, zero] if h % 2 == 0 else [zero, own], 0)


def head_cols(ref, h, at):
    block = ref[at, pl.ds((h // 2) * 2 * HEAD, 2 * HEAD)]
    lane = lax.broadcasted_iota(jnp.int32, block.shape, 1)
    return jnp.where((lane < HEAD) == (h % 2 == 0), block, jnp.zeros_like(block))


def pair_cols(h):
    return pl.ds((h // 2) * 2 * HEAD, 2 * HEAD)


def allowed_bias(k0, first, last):
    place = k0 + lax.broadcasted_iota(jnp.int32, (TILE, TILE), 0)
    return jnp.where((place >= first) & (place < last), 0.0, MASKED).astype(f32)


def staged(heads, stages, lags):
    held = [{} for _ in stages]
    for step in range(heads + sum(lags)):
        behind = 0
        for i, stage in enumerate(stages):
            behind += lags[i]
            h = step - behind
            if 0 <= h < heads:
                held[i][h] = stage(h, held[i - 1].pop(h) if i else None)


def front_kernel(info, tiles, first, last, bq, bv, pk, pv, *rest, count, half):
    tok_in = rest[:6]
    own, mate = rest[6:9], rest[9:12]
    pieces = rest[12 : 12 + count]
    outs = rest[12 + count : 26 + count]
    (keep_ref, send_ref, ot_ref, lse_ref, pk_ref, pkt_ref, pv_ref, q_out, qt_out, k_out, kt_out, v_out,
     w_out, pvt_ref) = outs
    (tok, w_ref, q_ref, qt_ref, k_ref, kt_ref, v_ref, vt_ref, stat, acc, bias, sem_x, sem_w,
     sem_o) = rest[26 + count :]
    core = info[0]
    tokens = tok_in[0].shape[0]
    width = tok.shape[1]
    pairs = []
    for i in range(6):
        slot = 2 * (i % 3) + (core if i < 3 else 1 - core)
        pairs.append((tok_in[i], tok.at[row_at(slot * tokens, tokens), :]))
    got_tok = start_all(pairs, sem_x)
    cols = pl.multiple_of(core * half, 128)
    got_w = []
    for i in (1, 2, 0):
        pairs = []
        for j, ref in enumerate((own[i], mate[i])):
            pairs.append((ref.at[:, pl.ds(cols, half)], w_ref.at[i, row_at(info[1 + j], ref.shape[0]), :]))
        for j, ref in enumerate(pieces):
            pairs.append(
                (
                    ref.at[:, pl.ds(i * width + cols, half)],
                    w_ref.at[i, row_at(info[3 + j], ref.shape[0]), :],
                )
            )
        got_w.append(start_all(pairs, sem_w.at[i]))
    pk_half, pv_half = pk[:, pl.ds(cols, half)], pv[:, pl.ds(cols, half)]
    pk_ref[...], pkt_ref[...] = pk_half, pk_half.astype(f32).T.astype(bf16)
    pv_ref[...], pvt_ref[...] = pv_half, pv_half.astype(f32).T.astype(bf16)
    bias_v = bv[:, pl.ds(cols, half)].astype(f32)
    bias_q = bq[:, pl.ds(cols, half)].astype(f32)
    blocks = k_ref.shape[0] // TILE
    wait_all(got_tok)
    wait_all(got_w[0])

    def key_block(b, carry):
        at = pl.ds(pl.multiple_of(b * TILE, TILE), TILE)
        full = dot(tok[at, :], w_ref[1])
        k_ref[at, :] = full.astype(bf16)
        kt_ref[:, at] = full.T.astype(bf16)
        return carry

    lax.fori_loop(0, blocks, key_block, 0)
    wait_all(got_w[1])

    def value_block(b, carry):
        at = pl.ds(pl.multiple_of(b * TILE, TILE), TILE)
        full = dot(tok[at, :], w_ref[2]) + bias_v
        v_ref[at, :] = full.astype(bf16)
        vt_ref[:, at] = full.T.astype(bf16)
        return carry

    lax.fori_loop(0, blocks, value_block, 0)
    wait_all(got_w[2])

    def query_block(b, carry):
        at = pl.ds(pl.multiple_of(b * TILE, TILE), TILE)
        src = pl.ds(pl.multiple_of(b * TILE + 2 * tokens, TILE), TILE)
        full = (dot(tok[src, :], w_ref[0]) + bias_q).astype(bf16).astype(f32) * SCALE
        q_ref[at, :] = full.astype(bf16)
        qt_ref[:, at] = full.T.astype(bf16)
        return carry

    lax.fori_loop(0, 2 * tokens // TILE, query_block, 0)
    saved = start_all(
        [(w_ref, w_out), (k_ref, k_out), (kt_ref, kt_out), (v_ref, v_out), (q_ref, q_out), (qt_ref, qt_out)],
        sem_o,
    )
    heads = half // HEAD

    def one_query_tile(t, carry):
        at = pl.ds(pl.multiple_of(t * TILE, TILE), TILE)
        qs, qe = first[:, at], last[:, at]

        def prefix_score(h, _):
            return dot(pk_ref[:, pair_cols(h)], head_rows(qt_ref, h, at))

        def prefix_soft(h, s):
            top = jnp.max(s, axis=0, keepdims=True)
            p = jnp.exp(s - top)
            stat[pl.ds(h, 1), :] = top
            stat[pl.ds(heads + h, 1), :] = jnp.sum(p, axis=0, keepdims=True)
            return p.astype(bf16)

        def prefix_mix(h, p):
            acc[pl.ds(h * HEAD, HEAD), :] = dot(pvt_ref[pl.ds(h * HEAD, HEAD), :], p)

        staged(heads, (prefix_score, prefix_soft, prefix_mix), (0, 1, 3))

        def one_key_tile(j, inner):
            k0 = pl.multiple_of(j * TILE, TILE)
            bias[...] = allowed_bias(k0, qs, qe)

            def score(h, _):
                return dot(k_ref[pl.ds(k0, TILE), pair_cols(h)], head_rows(qt_ref, h, at))

            def soft(h, s):
                s = s + bias[...]
                old = stat[pl.ds(h, 1), :]
                top = jnp.maximum(old, jnp.max(s, axis=0, keepdims=True))
                factor = jnp.exp(old - top)
                p = jnp.exp(s - top)
                stat[pl.ds(h, 1), :] = top
                total = jnp.sum(p, axis=0, keepdims=True)
                stat[pl.ds(heads + h, 1), :] = stat[pl.ds(heads + h, 1), :] * factor + total
                return p.astype(bf16), factor

            def mix(h, held):
                p, factor = held
                rows = pl.ds(h * HEAD, HEAD)
                acc[rows, :] = acc[rows, :] * factor + dot(vt_ref[rows, pl.ds(k0, TILE)], p)

            staged(heads, (score, soft, mix), (0, 1, 3))
            return inner

        lax.fori_loop(tiles[1 + 2 * t], tiles[2 + 2 * t], one_key_tile, 0)
        for h in range(heads):
            rows = pl.ds(h * HEAD, HEAD)
            acc[rows, :] = acc[rows, :] / stat[pl.ds(heads + h, 1), :]
        ot_ref[:, at] = acc[...]
        lse_ref[:, at] = stat[pl.ds(0, heads), :] + jnp.log(stat[pl.ds(heads, heads), :])
        low = acc[...].T.astype(bf16)
        side = (t * TILE) // tokens
        rows = pl.ds(pl.multiple_of(t * TILE - side * tokens, TILE), TILE)

        @pl.when(side == core)
        def _():
            keep_ref[rows, :] = low

        @pl.when(side != core)
        def _():
            send_ref[rows, :] = low

        return carry

    lax.fori_loop(0, 2 * tokens // TILE, one_query_tile, 0)
    wait_all(saved)


def front(info, tiles, first, last, bq, bv, pk, pv, toks, own, mate, pieces):
    tokens, width = toks[0].shape
    half = width // 2
    heads, pre = half // HEAD, pk.shape[0]
    n_q, n_k = 2 * tokens, 6 * tokens
    count = len(pieces)
    outs = [((tokens, half), bf16), ((tokens, half), bf16), ((half, n_q), f32), ((heads, n_q), f32)]
    outs += [((pre, half), bf16), ((half, pre), bf16), ((pre, half), bf16)]
    kept = [(n_q, half), (half, n_q), (n_k, half), (half, n_k), (n_k, half)]
    outs += [(a, bf16) for a in kept] + [((3, width, half), bf16)]
    vmem = [pltpu.VMEM((n_k, width), bf16), pltpu.VMEM((3, width, half), bf16)]
    vmem += [pltpu.VMEM(a, bf16) for a in kept + [(half, n_k)]]
    return pl.pallas_call(
        functools.partial(front_kernel, count=count, half=half),
        out_shape=tuple(shape_of(*a) for a in outs) + (shape_of((half, pre), bf16),),
        in_specs=[SM, SM] + [VM] * 6 + [HB] * (12 + count),
        out_specs=(VM,) * 7 + (HB,) * 6 + (VM,),
        scratch_shapes=vmem
        + [
            pltpu.VMEM((2 * heads, TILE), f32),
            pltpu.VMEM((half, TILE), f32),
            pltpu.VMEM((TILE, TILE), f32),
            pltpu.SemaphoreType.DMA((6,)),
            pltpu.SemaphoreType.DMA((3, 2 + count)),
            pltpu.SemaphoreType.DMA((6,)),
        ],
        compiler_params=pltpu.CompilerParams(vmem_limit_bytes=48 << 20),
        name="front",
        cost_estimate=cost(20),
    )(info, tiles, first, last, bq, bv, pk, pv, *toks, *own, *mate, *pieces)


def grad_stages(q, qt, kb, vb, ktb, do, do_t, lse, inner, bias, put):
    def products(h, _):
        return dot(kb(h), qt(h)), dot(vb(h), do_t(h))

    def scores(h, held):
        s, dp = held
        if bias is not None:
            s = s + bias[...]
        p = jnp.exp(s - lse(h))
        return p.astype(bf16), (p * (dp - inner(h))).astype(bf16)

    def sums(h, held):
        p, ds = held
        put(h, dot(p, do(h)), dot(ds, q(h)), dot(ktb(h), ds))

    return products, scores, sums


def sweep(ranges, at, first, last, refs, acc, heads):
    q_ref, qt_ref, k_ref, kt_ref, v_ref, do_ref, dot_ref, lse_ref, inner_ref, bias = refs
    dqt, dk, dv = acc
    qs, qe = first[:, at], last[:, at]

    def one_key_tile(j, carry):
        k0 = pl.multiple_of(j * TILE, TILE)
        r = pl.ds(k0, TILE)
        bias[...] = allowed_bias(k0, qs, qe)

        def put(h, gv, gk, gq):
            c, rows = pair_cols(h), pl.ds(h * HEAD, HEAD)
            dv[r, c] += gv
            dk[r, c] += gk
            dqt[rows, at] += gq

        stages = grad_stages(
            lambda h: head_cols(q_ref, h, at), lambda h: head_rows(qt_ref, h, at),
            lambda h: k_ref[r, pair_cols(h)], lambda h: v_ref[r, pair_cols(h)],
            lambda h: kt_ref[pl.ds(h * HEAD, HEAD), r], lambda h: head_cols(do_ref, h, at),
            lambda h: head_rows(dot_ref, h, at), lambda h: lse_ref[pl.ds(h, 1), at],
            lambda h: inner_ref[pl.ds(h, 1), at], bias, put,
        )
        staged(heads, stages, GRAD_LAGS)
        return carry

    for lo, hi in ranges:
        lax.fori_loop(lo, hi, one_key_tile, 0)


def remote_grads_kernel(
    info, first, last, q_ref, qt_ref, k_ref, kt_ref, v_ref, pk_ref, pkt_ref, pv_ref, keep_in, recv_in,
    ot_ref, lse_ref, w_in, give_ref, keep_lo, keep_hi, pre_ref, dqt, do_s, dot_s, inner_s, dk, dv, bias,
    wsc, wsem, *, heads,
):
    copies = start_all([(w_in.at[1], wsc.at[0]), (w_in.at[2], wsc.at[1])], wsem)
    core = info[0]
    tokens = keep_in.shape[0]
    n_q, pre = q_ref.shape[0], pk_ref.shape[0]
    do_s[row_at(core * tokens, tokens), :] = keep_in[...]
    do_s[row_at((1 - core) * tokens, tokens), :] = recv_in[...]
    dk[...] = jnp.zeros_like(dk)
    dv[...] = jnp.zeros_like(dv)
    pre_ref[...] = jnp.zeros_like(pre_ref)

    def one_query_tile(t, carry):
        at = pl.ds(pl.multiple_of(t * TILE, TILE), TILE)
        dot_s[:, at] = do_s[at, :].astype(f32).T.astype(bf16)
        for h in range(heads):
            rows = pl.ds(h * HEAD, HEAD)
            inner_s[pl.ds(h, 1), at] = jnp.sum(
                dot_s[rows, at].astype(f32) * ot_ref[rows, at], axis=0, keepdims=True
            )

        def put(h, gv, gk, gq):
            c = pair_cols(h)
            pre_ref[pl.ds(0, pre), c] += gk
            pre_ref[pl.ds(pre, pre), c] += gv
            dqt[pl.ds(h * HEAD, HEAD), at] = gq

        stages = grad_stages(
            lambda h: head_cols(q_ref, h, at), lambda h: head_rows(qt_ref, h, at),
            lambda h: pk_ref[:, pair_cols(h)], lambda h: pv_ref[:, pair_cols(h)],
            lambda h: pkt_ref[pl.ds(h * HEAD, HEAD), :], lambda h: head_cols(do_s, h, at),
            lambda h: head_rows(dot_s, h, at), lambda h: lse_ref[pl.ds(h, 1), at],
            lambda h: inner_s[pl.ds(h, 1), at], None, put,
        )
        staged(heads, stages, GRAD_LAGS)
        lo, hi = info[1 + 2 * t], info[2 + 2 * t]
        side = 2 * tokens // TILE
        refs = (q_ref, qt_ref, k_ref, kt_ref, v_ref, do_s, dot_s, lse_ref, inner_s, bias)
        ranges = ((lo, jnp.minimum(hi, side)), (jnp.maximum(lo, 2 * side), hi))
        sweep(ranges, at, first, last, refs, (dqt, dk, dv), heads)
        return carry

    lax.fori_loop(0, n_q // TILE, one_query_tile, 0)
    wait_all(copies)
    for i, keep in ((0, keep_lo), (1, keep_hi)):
        for mine in (True, False):
            block = core if mine else 1 - core
            r = row_at(i * 4 * tokens + block * tokens, tokens)
            out = dot(dk[r, :].astype(bf16), wsc[0], 1, 1) + dot(dv[r, :].astype(bf16), wsc[1], 1, 1)
            if mine:
                keep[...] = out
            else:
                give_ref[pl.ds(i * tokens, tokens), :] = out.astype(bf16)


def remote_grads(info, first, last, q, qt, k, kt, v, pk, pkt, pv, keep, recv, ot, lse, w):
    n_q, half = q.shape
    heads, tokens, width = half // HEAD, n_q // 2, w.shape[1]
    n_k, pre = k.shape[0], pk.shape[0]
    return pl.pallas_call(
        functools.partial(remote_grads_kernel, heads=heads),
        out_shape=(
            shape_of((2 * tokens, width), bf16),
            shape_of((tokens, width), f32),
            shape_of((tokens, width), f32),
            shape_of((2 * pre, half), f32),
            shape_of((half, n_q), f32),
            shape_of((n_q, half), bf16),
            shape_of((half, n_q), bf16),
            shape_of((heads, n_q), f32),
        ),
        in_specs=[SM] + [VM] * 14 + [HB],
        out_specs=(VM,) * 8,
        scratch_shapes=[
            pltpu.VMEM((n_k, half), f32),
            pltpu.VMEM((n_k, half), f32),
            pltpu.VMEM((TILE, TILE), f32),
            pltpu.VMEM((2, width, half), bf16),
            pltpu.SemaphoreType.DMA((2,)),
        ],
        compiler_params=pltpu.CompilerParams(vmem_limit_bytes=52 << 20),
        name="remote_grads",
        cost_estimate=cost(14),
    )(info, first, last, q, qt, k, kt, v, pk, pkt, pv, keep, recv, ot, lse, w)


def local_grads_kernel(
    info, first, last, q_ref, qt_ref, k_ref, kt_ref, v_ref, do_ref, dot_ref, lse_ref, inner_ref, dqt_in,
    gh_ref, w_in, keep_ref, give_ref, dqt, dk, dv, bias, wsc, wsem, *, heads,
):
    copies = start_all([(w_in, wsc)], wsem)
    core = info[0]
    n_q = q_ref.shape[0]
    tokens = n_q // 2
    dqt[...] = dqt_in[...]
    dk[...] = jnp.zeros_like(dk)
    dv[...] = jnp.zeros_like(dv)
    side = 2 * tokens // TILE

    def one_query_tile(t, carry):
        at = pl.ds(pl.multiple_of(t * TILE, TILE), TILE)
        lo, hi = info[1 + 2 * t], info[2 + 2 * t]
        refs = (q_ref, qt_ref, k_ref, kt_ref, v_ref, do_ref, dot_ref, lse_ref, inner_ref, bias)
        ranges = ((jnp.maximum(lo, side), jnp.minimum(hi, 2 * side)),)
        sweep(ranges, at, first, last, refs, (dqt, dk, dv), heads)
        return carry

    lax.fori_loop(0, n_q // TILE, one_query_tile, 0)
    wait_all(copies)
    for mine in (False, True):
        block = core if mine else 1 - core
        r = row_at(block * tokens, tokens)
        rk = row_at(block * tokens + n_q, tokens)
        dq = (dqt[:, r] * SCALE).T.astype(bf16)
        out = (
            dot(dq, wsc[0], 1, 1)
            + dot(dk[rk, :].astype(bf16), wsc[1], 1, 1)
            + dot(dv[rk, :].astype(bf16), wsc[2], 1, 1)
        )
        if mine:
            keep_ref[...] = out + gh_ref[...]
        else:
            give_ref[...] = out.astype(bf16)


def local_grads(info, first, last, q, qt, k, kt, v, do, dot_, lse, inner, dqt, gh, w):
    n_q, half = q.shape
    heads, tokens, width = half // HEAD, n_q // 2, w.shape[1]
    n_k = k.shape[0]
    return pl.pallas_call(
        functools.partial(local_grads_kernel, heads=heads),
        out_shape=(shape_of((tokens, width), f32), shape_of((tokens, width), bf16)),
        in_specs=[SM] + [VM] * 13 + [HB],
        out_specs=(VM,) * 2,
        scratch_shapes=[
            pltpu.VMEM((half, n_q), f32),
            pltpu.VMEM((n_k, half), f32),
            pltpu.VMEM((n_k, half), f32),
            pltpu.VMEM((TILE, TILE), f32),
            pltpu.VMEM((3, width, half), bf16),
            pltpu.SemaphoreType.DMA((1,)),
        ],
        compiler_params=pltpu.CompilerParams(vmem_limit_bytes=52 << 20),
        name="local_grads",
        cost_estimate=cost(14),
    )(info, first, last, q, qt, k, kt, v, do, dot_, lse, inner, dqt, gh, w)


def placed(refs, info, at, scale, dst, src_cols=None, dst_cols=None):
    pairs = []
    for i, ref in enumerate(refs):
        src = ref if src_cols is None else ref.at[:, src_cols]
        rows = row_at(info[at + i] * scale, ref.shape[0])
        pairs.append((src, dst.at[rows, :] if dst_cols is None else dst.at[rows, dst_cols]))
    return pairs


def out_pairs(parts, info, width, dst):
    return placed(parts[:2], info, 1, 1, dst) + placed(
        parts[2:], info, 11, 1, dst, pl.ds(3 * width, width)
    )


def up_kernel(info, own_att, got_att, tok, bo, ga, sa, bu, *rest, n_o, count):
    wo, wu = rest[:n_o], rest[n_o : n_o + count]
    nrm_ref, hat_ref, inv_ref, act_ref, slope_ref, wo_s, wu_s, sem_o, sem_u = rest[n_o + count :]
    width, ff = wu_s.shape
    half = own_att.shape[1]
    got_o = start_all(out_pairs(wo, info, width, wo_s), sem_o)
    got_u = []
    for j in range(ff // width):
        cs = pl.ds(j * width, width)
        got_u.append(start_all(placed(wu, info, 1, 1, wu_s, cs, cs), sem_u.at[j]))
    core = info[0]
    wait_all(got_o)
    hidden = (
        tok[...].astype(f32)
        + dot(own_att[...], wo_s[row_at(core * half, half), :])
        + dot(got_att[...], wo_s[row_at((1 - core) * half, half), :])
        + bo[...].astype(f32)
    )
    hat, inv = normalised(hidden)
    hat_ref[...] = hat
    inv_ref[...] = jnp.broadcast_to(inv, inv_ref.shape)
    nrm = hat * ga[...].astype(f32) + sa[...].astype(f32)
    nrm_ref[...] = nrm
    low = nrm.astype(bf16)
    for j in range(ff // CHUNK):
        if (j * CHUNK) % width == 0:
            wait_all(got_u[j * CHUNK // width])
        cs = pl.ds(j * CHUNK, CHUNK)
        v = dot(low, wu_s[:, cs]) + bu[:, cs].astype(f32)
        phi = 0.5 + 0.5 * lax.erf(v * (0.5**0.5))
        act_ref[:, cs] = (v * phi).astype(bf16)
        slope_ref[:, cs] = (phi + v * (jnp.exp(v * v * -0.5) * 0.3989422804014327)).astype(bf16)


def up(info, own_att, got_att, tok, bo, ga, sa, bu, wo, wu):
    tokens, width = tok.shape
    ff, count = bu.shape[1], len(wu)
    return pl.pallas_call(
        functools.partial(up_kernel, n_o=len(wo), count=count),
        out_shape=(
            shape_of((tokens, width), f32),
            shape_of((tokens, width), f32),
            shape_of((tokens, 128), f32),
            shape_of((tokens, ff), bf16),
            shape_of((tokens, ff), bf16),
        ),
        in_specs=[SM] + [VM] * 7 + [HB] * (len(wo) + count),
        out_specs=(VM,) * 5,
        scratch_shapes=[
            pltpu.VMEM((width, width), bf16),
            pltpu.VMEM((width, ff), bf16),
            pltpu.SemaphoreType.DMA((count,)),
            pltpu.SemaphoreType.DMA((ff // width, count)),
        ],
        compiler_params=pltpu.CompilerParams(vmem_limit_bytes=50 << 20),
        name="up",
        cost_estimate=cost(10),
    )(info, own_att, got_att, tok, bo, ga, sa, bu, *wo, *wu)


def down_kernel(info, nrm_ref, hat_ref, inv_ref, act_ref, slope_ref, cot, bd, gf, sf, ga, *rest, n_o, count):
    wo, wu, wd = rest[:n_o], rest[n_o : n_o + count], rest[n_o + count : n_o + 2 * count]
    out_ref, gh_ref, keep_ref, send_ref, wo_s, wu_s, wd_s, sem_o, sem_u, sem_d = rest[n_o + 2 * count :]
    width, ff = wu_s.shape
    half = keep_ref.shape[1]
    got_d = start_all(placed(wd, info, 1, ff // width, wd_s), sem_d)
    got_u = start_all(placed(wu, info, 1, 1, wu_s), sem_u)
    got_o = start_all(out_pairs(wo, info, width, wo_s), sem_o)
    core = info[0]
    summed = nrm_ref[...] + bd[...].astype(f32)
    for i, one in enumerate(got_d):
        one.wait()
        size = wd[i].shape[0]
        at = row_at(info[1 + i] * (ff // width), size)
        cols = pl.ds(pl.multiple_of(info[1 + i] * (ff // width), 128), size)
        summed = summed + dot(act_ref[:, cols], wd_s[at, :])
    n, inv = normalised(summed)
    gain = gf[...].astype(f32)
    out_ref[...] = (n * gain + sf[...].astype(f32)).astype(bf16)
    gs = norm_back(cot[...].astype(f32) * gain, n, inv)
    low = gs.astype(bf16)
    wait_all(got_u)
    total = gs
    for j in range(ff // CHUNK):
        cs = pl.ds(j * CHUNK, CHUNK)
        gp = (dot(low, wd_s[cs, :], 1, 1) * slope_ref[:, cs].astype(f32)).astype(bf16)
        total = total + dot(gp, wu_s[:, cs], 1, 1)
    gh = norm_back(total * ga[...].astype(f32), hat_ref[...], inv_ref[:, :1])
    gh_ref[...] = gh
    gh_low = gh.astype(bf16)
    wait_all(got_o)
    send_ref[...] = dot(gh_low, wo_s[row_at((1 - core) * half, half), :], 1, 1).astype(bf16)
    keep_ref[...] = dot(gh_low, wo_s[row_at(core * half, half), :], 1, 1).astype(bf16)


def down(info, nrm, hat, inv, act, slope, cot, bd, gf, sf, ga, wo, wu, wd):
    tokens, width = nrm.shape
    ff, count = act.shape[1], len(wu)
    return pl.pallas_call(
        functools.partial(down_kernel, n_o=len(wo), count=count),
        out_shape=(
            shape_of((tokens, width), bf16),
            shape_of((tokens, width), f32),
            shape_of((tokens, width // 2), bf16),
            shape_of((tokens, width // 2), bf16),
        ),
        in_specs=[SM] + [VM] * 10 + [HB] * (len(wo) + 2 * count),
        out_specs=(VM,) * 4,
        scratch_shapes=[
            pltpu.VMEM((width, width), bf16),
            pltpu.VMEM((width, ff), bf16),
            pltpu.VMEM((ff, width), bf16),
            pltpu.SemaphoreType.DMA((count,)),
            pltpu.SemaphoreType.DMA((count,)),
            pltpu.SemaphoreType.DMA((count,)),
        ],
        compiler_params=pltpu.CompilerParams(vmem_limit_bytes=58 << 20),
        name="down",
        cost_estimate=cost(16),
    )(info, nrm, hat, inv, act, slope, cot, bd, gf, sf, ga, *wo, *wu, *wd)


def per_device(
    tokens, cotangent, pair_lengths, prefix_key, prefix_value, w_query, b_query, w_key, w_value, b_value,
    w_out, b_out, gain_attn, shift_attn, w_up, b_up, w_down, b_down, gain_ffn, shift_ffn,
):
    n_row, n_seq = lax.axis_size("row"), lax.axis_size("seq")
    r, s = lax.axis_index("row"), lax.axis_index("seq")
    core, x, zbit = r & 1, s & 1, (s >> 1) & 1
    tok_count, width = tokens.shape[1], tokens.shape[2]

    def by_core(a):
        return lax.ppermute(a, "row", [(i, i ^ 1) for i in range(n_row)])

    def by_y(a):
        return lax.ppermute(a, "row", [(i, i ^ 2) for i in range(n_row)])

    def by_seq(a, bit):
        return lax.ppermute(a, "seq", [(i, i ^ bit) for i in range(n_seq)])

    def by_both(a, row_bit, bit):
        route = [(i * n_seq + j, (i ^ row_bit) * n_seq + (j ^ bit)) for i in range(n_row) for j in range(n_seq)]
        return lax.ppermute(a, ("row", "seq"), route)

    def swapped(a, shift):
        route = []
        for i in range(n_row):
            for j in range(n_seq):
                to = (j | 1) + 2 * shift - 1
                if 0 <= to < n_seq:
                    route.append((i * n_seq + j, ((i & ~1) | (j & 1)) * n_seq + to + (i & 1)))
        return lax.ppermute(a, ("row", "seq"), route)

    def after(a, *others):
        return lax.optimization_barrier((a,) + others)[0]

    h = x ^ zbit
    first_q, second_q = 2 * h + x, 2 * h + 1 - x
    which = jnp.stack([first_q, second_q]).astype(jnp.int32)
    attn = (w_query, w_key, w_value, w_out)
    short, ff = w_query.shape[0] // 4, w_up.shape[1]
    (a_half,) = pack(h[None].astype(jnp.int32), attn, [(2 * short, 4 * width)], [(i, 0, 0, i * width) for i in range(4)])
    plan = [(0, 0, 0, 0), (1, 0, 1, 0), (0, 1, 2, 0), (1, 1, 3, 0)]
    shapes = [(short, ff), (w_down.shape[0] // 4, width)] * 2
    a_half = by_y(a_half)
    own, below, above = (swapped(tokens[0], k) for k in (0, 1, -1))
    a_own = [by_core(a) for a in attn]
    mates = a_own
    u_one, d_one, u_two, d_two = pack(after(which, below), (w_up, w_down), shapes, plan)
    a_part = lax.dynamic_slice_in_dim(a_half, x * short, short, 0)
    a_x, a_z = by_seq(a_part, 1), by_seq(a_part, 2)
    u_one = by_y(after(u_one, a_half))
    d_one = by_y(after(d_one, a_x))
    u_two = by_y(after(u_two, a_z))
    toks = [below, own, above]
    toks = toks + [by_core(a) for a in toks]
    a_got = [a_half, a_x, a_z]
    a_got = a_got + [by_core(a_half), by_core(a_x), by_core(a_z)]
    u_own = by_core(after(w_up, a_z))
    m = w_query.shape[0]
    far = [2 * (1 - h) + 1 - x, 2 * (1 - h) + x]
    places = [r * m, (r ^ 1) * m]
    halves = [(r ^ k) * m + j * (m // 4) for k in (2, 3) for j in [2 * h] + far]
    quarters = [(r ^ k) * m + j * (m // 4) for k in (2, 3) for j in [first_q, second_q] + far]

    theirs = by_core(after(pair_lengths, a_half))
    lengths = jnp.where(x == core, pair_lengths, theirs)[0]
    pairs = lengths.shape[0]
    later = jnp.arange(pairs)[:, None] >= jnp.arange(pairs)[None, :]
    ends = jnp.sum(jnp.where(later, lengths[None, :], 0), axis=1)
    base = (s // 2) * 2 * tok_count
    place = base + jnp.arange(2 * tok_count, dtype=jnp.int32)
    passed = ends[:, None] <= place[None, :]
    origin = base - 2 * tok_count
    first = jnp.max(jnp.where(passed, ends[:, None], 0), axis=0) - origin
    last = jnp.min(jnp.where(passed, n_seq * tok_count, ends[:, None]), axis=0) - origin
    bounds = jnp.stack([first[::TILE] // TILE, (last[TILE - 1 :: TILE] + TILE - 1) // TILE], 1)
    tile_info = jnp.concatenate([core[None], bounds.reshape(-1)]).astype(jnp.int32)
    info_a = jnp.stack([core] + places + halves).astype(jnp.int32)
    info = jnp.stack([core] + places + quarters + halves).astype(jnp.int32)
    first, last = first[None], last[None]

    def row(a):
        return a.reshape(1, -1)

    (att_keep, att_send, ot, lse, pk, pkt, pv, q, qt, k, kt, v, w_half, _) = front(
        info_a, tile_info, first, last, row(b_query), row(b_value), prefix_key, prefix_value, toks,
        (w_query, w_key, w_value), mates[:3], a_got,
    )
    u_x, u_z = by_seq(u_one, 1), by_seq(u_one, 2)
    d_own = by_core(after(w_down, lse))
    cot = swapped(after(cotangent[0], lse), 0)
    d_two = by_y(after(d_two, lse))
    d_one, lse = lax.optimization_barrier((d_one, lse))
    d_x, d_z = by_seq(d_one, 1), by_seq(d_one, 2)
    u_got = [u_one, u_two, u_x, u_z]
    u_got = u_got + [by_core(after(a, lse)) for a in u_got]
    parts_o = [w_out, mates[3]] + a_got
    parts_u = [w_up, u_own] + u_got
    nrm, hat, inv, act, slope = up(
        info, att_keep, by_core(att_send), own, row(b_out), row(gain_attn), row(shift_attn), row(b_up),
        parts_o, parts_u,
    )
    d_got = [d_one, d_two, d_x, d_z]
    d_got = d_got + [by_core(a if a is d_one else after(a, inv, cot)) for a in d_got]
    parts_d = [w_down, d_own] + d_got
    result, gh, ga_keep, ga_send = down(
        info, nrm, hat, inv, act, slope, cot, row(b_down), row(gain_ffn), row(shift_ffn), row(gain_attn),
        parts_o, parts_u, parts_d,
    )
    out_tokens = swapped(result, 0)
    give, keep_lo, keep_hi, pre, dqt, do, dot_, inner = remote_grads(
        tile_info, first, last, q, qt, k, kt, v, pk, pkt, pv, ga_keep, by_core(ga_send), ot, lse, w_half
    )
    got = by_core(after(give, out_tokens))
    low_part = (keep_lo + got[:tok_count].astype(f32)).astype(bf16)
    high_part = (keep_hi + got[tok_count:].astype(f32)).astype(bf16)
    tile_info = after(tile_info, low_part, high_part)
    pre = after(pre, low_part)
    low_part = lax.ppermute(low_part, "seq", [(j + 2, j) for j in range(n_seq - 2)])
    high_part = lax.ppermute(high_part, "seq", [(j, j + 2) for j in range(n_seq - 2)])

    def summed(a, one, two):
        low = a.astype(bf16)
        sides = [by_both(low, *one), by_both(low, *two), by_both(low, one[0] | two[0], one[1] | two[1])]
        low, p, q, r = (v.astype(f32) for v in [low] + sides)
        return (low + p) + (q + r)

    bits = [(2, 0)] + [(0, 1 << i) for i in range(n_seq.bit_length() - 1)]
    if len(bits) % 2:
        low = pre.astype(bf16)
        pre = low.astype(f32) + by_both(low, *bits[0]).astype(f32)
        bits = bits[1:]
    pre = summed(pre, bits[0], bits[1])
    keep, give = local_grads(
        tile_info, first, last, q, qt, k, kt, v, do, dot_, lse, inner, dqt, gh, w_half
    )
    pre, give, low_part, high_part = lax.optimization_barrier((pre, give, low_part, high_part))
    mine = (keep + low_part.astype(f32)) + (by_core(give).astype(f32) + high_part.astype(f32))
    grad_tokens = swapped(mine.astype(bf16), 0)
    for i in range(2, len(bits), 2):
        pre = summed(pre, bits[i], bits[i + 1])
    other = by_core(pre)
    pre = jnp.concatenate(
        [jnp.where(core == 0, pre, other), jnp.where(core == 0, other, pre)], axis=1
    )
    n_pre = prefix_key.shape[0]
    return out_tokens[None], grad_tokens[None], pre[:n_pre], pre[n_pre:]


def solution(mesh):
    both, split, whole = P("row", "seq", None), P("row", None), P()
    return jax.shard_map(
        per_device,
        mesh=mesh,
        in_specs=(
            both, both, split, whole, whole, split, whole, split, split, whole, split, whole, whole, whole,
            split, whole, split, whole, whole, whole,
        ),
        out_specs=(both, both, whole, whole),
        check_vma=False,
    )
```

```python
import functools

import jax
import jax.numpy as jnp
from jax import lax
from jax.experimental import pallas as pl
from jax.experimental.pallas import tpu as pltpu
from jax.sharding import PartitionSpec as P

HEAD = 64
SCALE = HEAD**-0.5
LN_EPS = 1e-05
MASKED = -1e30
TILE = 256
CHUNK = 512
UP_PARTS = 4
HALF_AT, Q_AT, H_AT = 11, 17, 19
GRAD_LAGS = (0, 1, 2)

f32 = jnp.float32
bf16 = jnp.bfloat16
VM = pl.BlockSpec(memory_space=pltpu.VMEM)
SM = pl.BlockSpec(memory_space=pltpu.SMEM)
HB = pl.BlockSpec(memory_space=pltpu.HBM)


def cost(us):
    return pl.CostEstimate(flops=int(us * 1e9), bytes_accessed=0, transcendentals=0)


def shape_of(shape, kind):
    return jax.ShapeDtypeStruct(shape, kind)


def dot(a, b, ca=1, cb=0):
    return lax.dot_general(a, b, (((ca,), (cb,)), ((), ())), preferred_element_type=f32)


def row_at(offset, rows):
    return pl.ds(pl.multiple_of(offset, 64), rows)


def start_all(pairs, sems):
    made = [pltpu.make_async_copy(s, d, sems.at[i]) for i, (s, d) in enumerate(pairs)]
    for one in made:
        one.start()
    return made


def wait_all(made):
    for one in made:
        one.wait()


def normalised(v):
    centred = v - jnp.mean(v, axis=-1, keepdims=True)
    inv = lax.rsqrt(jnp.mean(centred * centred, axis=-1, keepdims=True) + LN_EPS)
    return centred * inv, inv


def norm_back(g, n, inv):
    return (g - jnp.mean(g, -1, keepdims=True) - n * jnp.mean(g * n, -1, keepdims=True)) * inv


def pack_kernel(info, *rest, plan, n_in, n_out):
    srcs, outs, bufs = rest[:n_in], rest[n_in : n_in + n_out], rest[n_in + n_out : n_in + 2 * n_out]
    sem_in, sem_out = rest[n_in + 2 * n_out :]
    pairs = []
    for i, which, o, col in plan:
        rows, cols = outs[o].shape[0], srcs[i].shape[1]
        pairs.append((srcs[i].at[row_at(info[which] * rows, rows), :], bufs[o].at[:, pl.ds(col, cols)]))
    wait_all(start_all(pairs, sem_in))
    wait_all(start_all(list(zip(bufs, outs)), sem_out))


def pack(info, srcs, shapes, plan):
    return pl.pallas_call(
        functools.partial(pack_kernel, plan=plan, n_in=len(srcs), n_out=len(shapes)),
        out_shape=tuple(shape_of(a, bf16) for a in shapes),
        in_specs=[SM] + [HB] * len(srcs),
        out_specs=(HB,) * len(shapes),
        scratch_shapes=[pltpu.VMEM(a, bf16) for a in shapes]
        + [pltpu.SemaphoreType.DMA((len(plan),)), pltpu.SemaphoreType.DMA((len(shapes),))],
        compiler_params=pltpu.CompilerParams(vmem_limit_bytes=58 << 20),
        name="pack",
        cost_estimate=cost(2),
    )(info, *srcs)


def head_rows(ref, h, at):
    own = ref[pl.ds(h * HEAD, HEAD), at]
    zero = jnp.zeros_like(own)
    return jnp.concatenate([own, zero] if h % 2 == 0 else [zero, own], 0)


def head_cols(ref, h, at):
    block = ref[at, pl.ds((h // 2) * 2 * HEAD, 2 * HEAD)]
    lane = lax.broadcasted_iota(jnp.int32, block.shape, 1)
    return jnp.where((lane < HEAD) == (h % 2 == 0), block, jnp.zeros_like(block))


def pair_cols(h):
    return pl.ds((h // 2) * 2 * HEAD, 2 * HEAD)


def allowed_bias(k0, first, last):
    place = k0 + lax.broadcasted_iota(jnp.int32, (TILE, TILE), 0)
    return jnp.where((place >= first) & (place < last), 0.0, MASKED).astype(f32)


def staged(heads, stages, lags):
    held = [{} for _ in stages]
    for step in range(heads + sum(lags)):
        behind = 0
        for i, stage in enumerate(stages):
            behind += lags[i]
            h = step - behind
            if 0 <= h < heads:
                held[i][h] = stage(h, held[i - 1].pop(h) if i else None)


def front_kernel(info, tiles, first, last, bq, bv, pk, pv, *rest, count, half):
    tok_in = rest[:6]
    own, mate = rest[6:9], rest[9:12]
    pieces = rest[12 : 12 + count]
    outs = rest[12 + count : 25 + count]
    keep_ref, send_ref, ot_out, lse_out, pk_out, pkt_out, pv_out = outs[:7]
    q_out, qt_out, k_out, kt_out, v_out, w_out = outs[7:]
    (tok, w_ref, q_ref, qt_ref, k_ref, kt_ref, v_ref, vt_ref, pk_ref, pkt_ref, pv_ref, pvt_ref, ot_ref, lse_ref,
     att, stat, acc, bias, sem_x, sem_w, sem_o, sem_a) = rest[25 + count :]
    core = info[0]
    tokens = tok_in[0].shape[0]
    width = tok.shape[1]
    pairs = []
    for i in range(6):
        place = (1, 2 - 2 * tiles[0], 2 * tiles[0])[i % 3]
        slot = 2 * place + (core if i < 3 else 1 - core)
        pairs.append((tok_in[i], tok.at[row_at(slot * tokens, tokens), :]))
    got_tok = start_all(pairs, sem_x)
    cols = pl.multiple_of(core * half, 128)
    got_w = []
    for i in (1, 2, 0):
        pairs = []
        for j, ref in enumerate((own[i], mate[i])):
            pairs.append((ref.at[:, pl.ds(cols, half)], w_ref.at[i, row_at(info[1 + j], ref.shape[0]), :]))
        for j, ref in enumerate(pieces):
            pairs.append(
                (
                    ref.at[:, pl.ds(i * width + cols, half)],
                    w_ref.at[i, row_at(info[HALF_AT + j], ref.shape[0]), :],
                )
            )
        got_w.append(start_all(pairs, sem_w.at[i]))
    pk_half, pv_half = pk[:, pl.ds(cols, half)], pv[:, pl.ds(cols, half)]
    pk_ref[...], pkt_ref[...] = pk_half, pk_half.astype(f32).T.astype(bf16)
    pv_ref[...], pvt_ref[...] = pv_half, pv_half.astype(f32).T.astype(bf16)
    bias_v = bv[pl.ds(cols, half)].astype(f32)[None, :]
    bias_q = bq[pl.ds(cols, half)].astype(f32)[None, :]
    blocks = k_ref.shape[0] // TILE
    wait_all(got_tok)
    wait_all(got_w[0])

    def key_block(b, carry):
        at = pl.ds(pl.multiple_of(b * TILE, TILE), TILE)
        full = dot(tok[at, :], w_ref[1])
        k_ref[at, :] = full.astype(bf16)
        kt_ref[:, at] = full.T.astype(bf16)
        return carry

    lax.fori_loop(0, blocks, key_block, 0, unroll=2)
    wait_all(got_w[1])

    def value_block(b, carry):
        at = pl.ds(pl.multiple_of(b * TILE, TILE), TILE)
        full = dot(tok[at, :], w_ref[2]) + bias_v
        v_ref[at, :] = full.astype(bf16)
        vt_ref[:, at] = full.T.astype(bf16)
        return carry

    lax.fori_loop(0, blocks, value_block, 0, unroll=2)
    wait_all(got_w[2])

    def query_block(b, carry):
        at = pl.ds(pl.multiple_of(b * TILE, TILE), TILE)
        src = pl.ds(pl.multiple_of(b * TILE + 2 * tokens, TILE), TILE)
        full = (dot(tok[src, :], w_ref[0]) + bias_q).astype(bf16).astype(f32) * SCALE
        q_ref[at, :] = full.astype(bf16)
        qt_ref[:, at] = full.T.astype(bf16)
        return carry

    lax.fori_loop(0, 2 * tokens // TILE, query_block, 0, unroll=2)
    pairs = [(w_ref, w_out), (k_ref, k_out), (kt_ref, kt_out), (v_ref, v_out), (q_ref, q_out), (qt_ref, qt_out)]
    pairs += [(pk_ref, pk_out), (pkt_ref, pkt_out), (pv_ref, pv_out)]
    saved = start_all(pairs, sem_o)
    heads = half // HEAD

    def one_query_tile(t, carry):
        at = pl.ds(pl.multiple_of(t * TILE, TILE), TILE)
        qs, qe = first[:, at], last[:, at]

        def prefix_score(h, _):
            return dot(pk_ref[:, pair_cols(h)], head_rows(qt_ref, h, at))

        def prefix_soft(h, s):
            top = jnp.max(s, axis=0, keepdims=True)
            p = jnp.exp(s - top)
            stat[pl.ds(h, 1), :] = top
            stat[pl.ds(heads + h, 1), :] = jnp.sum(p, axis=0, keepdims=True)
            return p.astype(bf16)

        def prefix_mix(h, p):
            acc[pl.ds(h * HEAD, HEAD), :] = dot(pvt_ref[pl.ds(h * HEAD, HEAD), :], p)

        staged(heads, (prefix_score, prefix_soft, prefix_mix), (0, 1, 3))

        def one_key_tile(j, inner):
            k0 = pl.multiple_of(j * TILE, TILE)
            bias[...] = allowed_bias(k0, qs, qe)

            def score(h, _):
                return dot(k_ref[pl.ds(k0, TILE), pair_cols(h)], head_rows(qt_ref, h, at))

            def soft(h, s):
                s = s + bias[...]
                old = stat[pl.ds(h, 1), :]
                top = jnp.maximum(old, jnp.max(s, axis=0, keepdims=True))
                factor = jnp.exp(old - top)
                p = jnp.exp(s - top)
                stat[pl.ds(h, 1), :] = top
                total = jnp.sum(p, axis=0, keepdims=True)
                stat[pl.ds(heads + h, 1), :] = stat[pl.ds(heads + h, 1), :] * factor + total
                return p.astype(bf16), factor

            def mix(h, held):
                p, factor = held
                rows = pl.ds(h * HEAD, HEAD)
                acc[rows, :] = acc[rows, :] * factor + dot(vt_ref[rows, pl.ds(k0, TILE)], p)

            staged(heads, (score, soft, mix), (0, 1, 3))
            return inner

        lax.fori_loop(tiles[1 + 2 * t], tiles[2 + 2 * t], one_key_tile, 0)
        for h in range(heads):
            rows = pl.ds(h * HEAD, HEAD)
            acc[rows, :] = acc[rows, :] / stat[pl.ds(heads + h, 1), :]
        ot_ref[:, at] = acc[...]
        lse_ref[:, at] = stat[pl.ds(0, heads), :] + jnp.log(stat[pl.ds(heads, heads), :])
        att[at, :] = acc[...].T.astype(bf16)
        return carry

    lax.fori_loop(0, 2 * tokens // TILE, one_query_tile, 0)
    mine, theirs = row_at(core * tokens, tokens), row_at((1 - core) * tokens, tokens)
    pairs = [(att.at[theirs, :], send_ref), (att.at[mine, :], keep_ref), (ot_ref, ot_out), (lse_ref, lse_out)]
    wait_all(start_all(pairs, sem_a))
    wait_all(saved)


def front(info, tiles, first, last, bq, bv, pk, pv, toks, own, mate, pieces):
    tokens, width = toks[0].shape
    half = width // 2
    heads, pre = half // HEAD, pk.shape[0]
    n_q, n_k = 2 * tokens, 6 * tokens
    count = len(pieces)
    kept = [(n_q, half), (half, n_q), (n_k, half), (half, n_k), (n_k, half)]
    pres = [(pre, half), (half, pre), (pre, half)]
    stats = [(half, n_q), (heads, n_q)]
    outs = [shape_of((tokens, half), bf16)] * 2 + [shape_of(a, f32) for a in stats]
    outs += [shape_of(a, bf16) for a in pres + kept + [(3, width, half)]]
    vmem = [(n_k, width), (3, width, half)] + kept + [(half, n_k)] + pres + [(half, pre)]
    return pl.pallas_call(
        functools.partial(front_kernel, count=count, half=half),
        out_shape=tuple(outs),
        in_specs=[SM, SM] + [VM] * 6 + [HB] * (12 + count),
        out_specs=(HB,) * len(outs),
        scratch_shapes=[pltpu.VMEM(a, bf16) for a in vmem]
        + [pltpu.VMEM(a, f32) for a in stats]
        + [
            pltpu.VMEM((n_q, half), bf16),
            pltpu.VMEM((2 * heads, TILE), f32),
            pltpu.VMEM((half, TILE), f32),
            pltpu.VMEM((TILE, TILE), f32),
            pltpu.SemaphoreType.DMA((6,)),
            pltpu.SemaphoreType.DMA((3, 2 + count)),
            pltpu.SemaphoreType.DMA((9,)),
            pltpu.SemaphoreType.DMA((4,)),
        ],
        compiler_params=pltpu.CompilerParams(vmem_limit_bytes=60 << 20),
        name="front",
        cost_estimate=cost(20),
    )(info, tiles, first, last, bq, bv, pk, pv, *toks, *own, *mate, *pieces)


def grad_stages(q, qt, kb, vb, ktb, do, do_t, lse, inner, bias, put):
    def products(h, _):
        return dot(kb(h), qt(h)), dot(vb(h), do_t(h))

    def scores(h, held):
        s, dp = held
        if bias is not None:
            s = s + bias[...]
        p = jnp.exp(s - lse(h))
        return p.astype(bf16), (p * (dp - inner(h))).astype(bf16)

    def sums(h, held):
        p, ds = held
        put(h, dot(p, do(h)), dot(ds, q(h)), dot(ktb(h), ds))

    return products, scores, sums


def sweep(ranges, at, first, last, refs, acc, heads):
    q_ref, qt_ref, k_ref, kt_ref, v_ref, do_ref, dot_ref, lse_ref, inner_ref, bias = refs
    dqt, dk, dv = acc
    qs, qe = first[:, at], last[:, at]

    def one_key_tile(j, carry):
        k0 = pl.multiple_of(j * TILE, TILE)
        r = pl.ds(k0, TILE)
        bias[...] = allowed_bias(k0, qs, qe)

        def put(h, gv, gk, gq):
            c, rows = pair_cols(h), pl.ds(h * HEAD, HEAD)
            dv[r, c] += gv
            dk[r, c] += gk
            dqt[rows, at] += gq

        stages = grad_stages(
            lambda h: head_cols(q_ref, h, at), lambda h: head_rows(qt_ref, h, at),
            lambda h: k_ref[r, pair_cols(h)], lambda h: v_ref[r, pair_cols(h)],
            lambda h: kt_ref[pl.ds(h * HEAD, HEAD), r], lambda h: head_cols(do_ref, h, at),
            lambda h: head_rows(dot_ref, h, at), lambda h: lse_ref[pl.ds(h, 1), at],
            lambda h: inner_ref[pl.ds(h, 1), at], bias, put,
        )
        staged(heads, stages, GRAD_LAGS)
        return carry

    for lo, hi in ranges:
        lax.fori_loop(lo, hi, one_key_tile, 0)


def prefix_grads_kernel(
    info, q_ref, qt_ref, pk_ref, pkt_ref, pv_ref, keep_in, recv_in, ot_ref, lse_ref,
    pre_ref, dqt, do_s, dot_s, inner_s, *, heads,
):
    core = info[0]
    tokens = keep_in.shape[0]
    n_q, pre = q_ref.shape[0], pk_ref.shape[0]
    do_s[row_at(core * tokens, tokens), :] = keep_in[...]
    do_s[row_at((1 - core) * tokens, tokens), :] = recv_in[...]
    pre_ref[...] = jnp.zeros_like(pre_ref)

    def one_query_tile(t, carry):
        at = pl.ds(pl.multiple_of(t * TILE, TILE), TILE)
        dot_s[:, at] = do_s[at, :].astype(f32).T.astype(bf16)
        for h in range(heads):
            rows = pl.ds(h * HEAD, HEAD)
            inner_s[pl.ds(h, 1), at] = jnp.sum(
                dot_s[rows, at].astype(f32) * ot_ref[rows, at], axis=0, keepdims=True
            )

        def put(h, gv, gk, gq):
            c = pair_cols(h)
            pre_ref[pl.ds(0, pre), c] += gk
            pre_ref[pl.ds(pre, pre), c] += gv
            dqt[pl.ds(h * HEAD, HEAD), at] = gq

        stages = grad_stages(
            lambda h: head_cols(q_ref, h, at), lambda h: head_rows(qt_ref, h, at),
            lambda h: pk_ref[:, pair_cols(h)], lambda h: pv_ref[:, pair_cols(h)],
            lambda h: pkt_ref[pl.ds(h * HEAD, HEAD), :], lambda h: head_cols(do_s, h, at),
            lambda h: head_rows(dot_s, h, at), lambda h: lse_ref[pl.ds(h, 1), at],
            lambda h: inner_s[pl.ds(h, 1), at], None, put,
        )
        staged(heads, stages, GRAD_LAGS)
        return carry

    lax.fori_loop(0, n_q // TILE, one_query_tile, 0)


def prefix_grads(info, q, qt, pk, pkt, pv, keep, recv, ot, lse):
    n_q, half = q.shape
    heads, pre = half // HEAD, pk.shape[0]
    return pl.pallas_call(
        functools.partial(prefix_grads_kernel, heads=heads),
        out_shape=(
            shape_of((2 * pre, half), f32),
            shape_of((half, n_q), f32),
            shape_of((n_q, half), bf16),
            shape_of((half, n_q), bf16),
            shape_of((heads, n_q), f32),
        ),
        in_specs=[SM] + [VM] * 9,
        out_specs=(VM,) * 5,
        compiler_params=pltpu.CompilerParams(vmem_limit_bytes=10 << 20),
        name="prefix_grads",
        cost_estimate=cost(5),
    )(info, q, qt, pk, pkt, pv, keep, recv, ot, lse)


def remote_grads_kernel(
    info, first, last, q_ref, qt_ref, k_ref, kt_ref, v_ref, do_ref, dot_ref, lse_ref, inner_ref, dqt_in,
    w_in, give_ref, keep_near, keep_far, dqt, dk, dv, bias, wsc, wsem, *, heads,
):
    copies = start_all([(w_in.at[1], wsc.at[0]), (w_in.at[2], wsc.at[1])], wsem)
    n_q = q_ref.shape[0]
    tokens = n_q // 2
    core = info[1 + 2 * (n_q // TILE)]
    dk[...] = jnp.zeros_like(dk)
    dv[...] = jnp.zeros_like(dv)
    dqt[...] = dqt_in[...]

    def one_query_tile(t, carry):
        at = pl.ds(pl.multiple_of(t * TILE, TILE), TILE)
        lo, hi = info[1 + 2 * t], info[2 + 2 * t]
        side = 2 * tokens // TILE
        refs = (q_ref, qt_ref, k_ref, kt_ref, v_ref, do_ref, dot_ref, lse_ref, inner_ref, bias)
        ranges = ((lo, jnp.minimum(hi, side)), (jnp.maximum(lo, 2 * side), hi))
        sweep(ranges, at, first, last, refs, (dqt, dk, dv), heads)
        return carry

    lax.fori_loop(0, n_q // TILE, one_query_tile, 0)
    wait_all(copies)
    for i, keep in ((0, keep_near), (1, keep_far)):
        for mine in (True, False):
            block = core if mine else 1 - core
            side = info[0] if i else 1 - info[0]
            r = row_at(side * 4 * tokens + block * tokens, tokens)
            out = dot(dk[r, :].astype(bf16), wsc[0], 1, 1) + dot(dv[r, :].astype(bf16), wsc[1], 1, 1)
            if mine:
                keep[...] = out.astype(bf16)
            else:
                give_ref[pl.ds(i * tokens, tokens), :] = out.astype(bf16)


def remote_grads(info, first, last, q, qt, k, kt, v, do, dot_, lse, inner, dqt, w):
    n_q, half = q.shape
    heads, tokens, width = half // HEAD, n_q // 2, w.shape[1]
    n_k = k.shape[0]
    return pl.pallas_call(
        functools.partial(remote_grads_kernel, heads=heads),
        out_shape=(
            shape_of((2 * tokens, width), bf16),
            shape_of((tokens, width), bf16),
            shape_of((tokens, width), bf16),
            shape_of((half, n_q), f32),
        ),
        in_specs=[SM] + [VM] * 12 + [HB],
        out_specs=(VM,) * 4,
        scratch_shapes=[
            pltpu.VMEM((n_k, half), f32),
            pltpu.VMEM((n_k, half), f32),
            pltpu.VMEM((TILE, TILE), f32),
            pltpu.VMEM((2, width, half), bf16),
            pltpu.SemaphoreType.DMA((2,)),
        ],
        compiler_params=pltpu.CompilerParams(vmem_limit_bytes=24 << 20),
        name="remote_grads",
        cost_estimate=cost(14),
    )(info, first, last, q, qt, k, kt, v, do, dot_, lse, inner, dqt, w)


def local_grads_kernel(
    info, first, last, q_ref, qt_ref, k_ref, kt_ref, v_ref, do_ref, dot_ref, lse_ref, inner_ref, dqt_in,
    gh_ref, w_in, keep_ref, give_ref, dqt, dk, dv, bias, wsc, wsem, *, heads,
):
    copies = start_all([(w_in, wsc)], wsem)
    core = info[1 + 2 * (q_ref.shape[0] // TILE)]
    n_q = q_ref.shape[0]
    tokens = n_q // 2
    dqt[...] = dqt_in[...]
    dk[...] = jnp.zeros_like(dk)
    dv[...] = jnp.zeros_like(dv)
    side = 2 * tokens // TILE

    def one_query_tile(t, carry):
        at = pl.ds(pl.multiple_of(t * TILE, TILE), TILE)
        lo, hi = info[1 + 2 * t], info[2 + 2 * t]
        refs = (q_ref, qt_ref, k_ref, kt_ref, v_ref, do_ref, dot_ref, lse_ref, inner_ref, bias)
        ranges = ((jnp.maximum(lo, side), jnp.minimum(hi, 2 * side)),)
        sweep(ranges, at, first, last, refs, (dqt, dk, dv), heads)
        return carry

    lax.fori_loop(0, n_q // TILE, one_query_tile, 0)
    wait_all(copies)
    for mine in (False, True):
        block = core if mine else 1 - core
        r = row_at(block * tokens, tokens)
        rk = row_at(block * tokens + n_q, tokens)
        dq = (dqt[:, r] * SCALE).T.astype(bf16)
        out = (
            dot(dq, wsc[0], 1, 1)
            + dot(dk[rk, :].astype(bf16), wsc[1], 1, 1)
            + dot(dv[rk, :].astype(bf16), wsc[2], 1, 1)
        )
        if mine:
            keep_ref[...] = out + gh_ref[...]
        else:
            give_ref[...] = out.astype(bf16)


def local_grads(info, first, last, q, qt, k, kt, v, do, dot_, lse, inner, dqt, gh, w):
    n_q, half = q.shape
    heads, tokens, width = half // HEAD, n_q // 2, w.shape[1]
    n_k = k.shape[0]
    return pl.pallas_call(
        functools.partial(local_grads_kernel, heads=heads),
        out_shape=(shape_of((tokens, width), f32), shape_of((tokens, width), bf16)),
        in_specs=[SM] + [VM] * 13 + [HB],
        out_specs=(VM,) * 2,
        scratch_shapes=[
            pltpu.VMEM((half, n_q), f32),
            pltpu.VMEM((n_k, half), f32),
            pltpu.VMEM((n_k, half), f32),
            pltpu.VMEM((TILE, TILE), f32),
            pltpu.VMEM((3, width, half), bf16),
            pltpu.SemaphoreType.DMA((1,)),
        ],
        compiler_params=pltpu.CompilerParams(vmem_limit_bytes=23 << 20),
        name="local_grads",
        cost_estimate=cost(14),
    )(info, first, last, q, qt, k, kt, v, do, dot_, lse, inner, dqt, gh, w)


def placed(refs, info, at, scale, dst, cols=None):
    pairs = []
    for i, ref in enumerate(refs):
        src = ref if cols is None else ref.at[:, cols[0]]
        rows = row_at(info[at + i] * scale, ref.shape[0])
        pairs.append((src, dst.at[rows, :] if cols is None else dst.at[rows, cols[1]]))
    return pairs


def up_pairs(parts, info, dst, cols):
    return placed((parts[0], parts[2]) + tuple(parts[4:]), info, 1, 1, dst, (cols, cols))


def out_pairs(parts, info, ff, dst):
    whole = pl.ds(0, dst.shape[1])
    return placed((parts[1], parts[3]), info, 1, 1, dst) + placed(
        parts[4:], info, 3, 1, dst, (pl.ds(ff, dst.shape[1]), whole)
    )


def up_kernel(info, own_att, got_att, tok, bo, ga, sa, bu, *rest, count):
    wu = rest[:count]
    nrm_ref, hat_ref, inv_ref, act_ref, slope_ref, wo_s, wu_s, own_s, got_s, tok_s, sem_a, sem_o, sem_u = rest[count:]
    acts = start_all([(own_att, own_s), (got_att, got_s), (tok, tok_s)], sem_a)
    width, ff = wu_s.shape
    half = own_att.shape[1]
    got_o = start_all(out_pairs(wu, info, ff, wo_s), sem_o)
    part = ff // UP_PARTS
    got_u = []
    for j in range(UP_PARTS):
        got_u.append(start_all(up_pairs(wu, info, wu_s, pl.ds(j * part, part)), sem_u.at[j]))
    core = info[0]
    wait_all(acts)
    wait_all(got_o)
    hidden = (
        tok_s[...].astype(f32)
        + dot(own_s[...], wo_s[row_at(core * half, half), :])
        + dot(got_s[...], wo_s[row_at((1 - core) * half, half), :])
        + bo[...].astype(f32)[None, :]
    )
    hat, inv = normalised(hidden)
    hat_ref[...] = hat
    inv_ref[...] = jnp.broadcast_to(inv, inv_ref.shape)
    nrm = hat * ga[...].astype(f32)[None, :] + sa[...].astype(f32)[None, :]
    nrm_ref[...] = nrm
    low = nrm.astype(bf16)
    for j in range(ff // CHUNK):
        if (j * CHUNK) % part == 0:
            wait_all(got_u[j * CHUNK // part])
        cs = pl.ds(j * CHUNK, CHUNK)
        v = dot(low, wu_s[:, cs]) + bu[cs].astype(f32)[None, :]
        phi = 0.5 + 0.5 * lax.erf(v * (0.5**0.5))
        act_ref[:, cs] = (v * phi).astype(bf16)
        slope_ref[:, cs] = (phi + v * (jnp.exp(v * v * -0.5) * 0.3989422804014327)).astype(bf16)


def up(info, own_att, got_att, tok, bo, ga, sa, bu, wu):
    tokens, width = tok.shape
    ff, count = bu.shape[0], len(wu)
    return pl.pallas_call(
        functools.partial(up_kernel, count=count),
        out_shape=(
            shape_of((tokens, width), f32),
            shape_of((tokens, width), f32),
            shape_of((tokens, 128), f32),
            shape_of((tokens, ff), bf16),
            shape_of((tokens, ff), bf16),
        ),
        in_specs=[SM] + [HB] * 3 + [VM] * 4 + [HB] * count,
        out_specs=(VM,) * 5,
        scratch_shapes=[
            pltpu.VMEM((width, width), bf16),
            pltpu.VMEM((width, ff), bf16),
            pltpu.VMEM((tokens, width // 2), bf16),
            pltpu.VMEM((tokens, width // 2), bf16),
            pltpu.VMEM((tokens, width), bf16),
            pltpu.SemaphoreType.DMA((3,)),
            pltpu.SemaphoreType.DMA((count - 2,)),
            pltpu.SemaphoreType.DMA((UP_PARTS, count - 2)),
        ],
        compiler_params=pltpu.CompilerParams(vmem_limit_bytes=55 << 20),
        name="up",
        cost_estimate=cost(10),
    )(info, own_att, got_att, tok, bo, ga, sa, bu, *wu)


def down_kernel(info, nrm_ref, hat_ref, inv_ref, act_ref, slope_ref, cot, bd, gf, sf, ga, *rest, count):
    wu, wd = rest[:count], rest[count : 2 * count - 2]
    out_ref, gh_ref, keep_ref, send_ref, wo_s, wu_s, wd_s, sem_o, sem_u, sem_d = rest[2 * count - 2 :]
    width, ff = wu_s.shape
    half = keep_ref.shape[1]
    got_d = start_all(placed(wd, info, 1, ff // width, wd_s), sem_d)
    got_u = start_all(up_pairs(wu, info, wu_s, pl.ds(0, ff)), sem_u)
    got_o = start_all(out_pairs(wu, info, ff, wo_s), sem_o)
    core = info[0]
    summed = nrm_ref[...] + bd[...].astype(f32)[None, :]
    for i, one in enumerate(got_d):
        one.wait()
        size = wd[i].shape[0]
        at = row_at(info[1 + i] * (ff // width), size)
        cols = pl.ds(pl.multiple_of(info[1 + i] * (ff // width), 128), size)
        summed = summed + dot(act_ref[:, cols], wd_s[at, :])
    n, inv = normalised(summed)
    gain = gf[...].astype(f32)[None, :]
    out_ref[...] = (n * gain + sf[...].astype(f32)[None, :]).astype(bf16)
    gs = norm_back(cot[...].astype(f32) * gain, n, inv)
    low = gs.astype(bf16)
    wait_all(got_u)
    total = gs
    for j in range(ff // CHUNK):
        cs = pl.ds(j * CHUNK, CHUNK)
        gp = (dot(low, wd_s[cs, :], 1, 1) * slope_ref[:, cs].astype(f32)).astype(bf16)
        total = total + dot(gp, wu_s[:, cs], 1, 1)
    gh = norm_back(total * ga[...].astype(f32)[None, :], hat_ref[...], inv_ref[:, :1])
    gh_ref[...] = gh
    gh_low = gh.astype(bf16)
    wait_all(got_o)
    send_ref[...] = dot(gh_low, wo_s[row_at((1 - core) * half, half), :], 1, 1).astype(bf16)
    keep_ref[...] = dot(gh_low, wo_s[row_at(core * half, half), :], 1, 1).astype(bf16)


def down(info, nrm, hat, inv, act, slope, cot, bd, gf, sf, ga, wu, wd):
    tokens, width = nrm.shape
    ff, count = act.shape[1], len(wu)
    return pl.pallas_call(
        functools.partial(down_kernel, count=count),
        out_shape=(
            shape_of((tokens, width), bf16),
            shape_of((tokens, width), f32),
            shape_of((tokens, width // 2), bf16),
            shape_of((tokens, width // 2), bf16),
        ),
        in_specs=[SM] + [VM] * 10 + [HB] * (2 * count - 2),
        out_specs=(VM,) * 4,
        scratch_shapes=[
            pltpu.VMEM((width, width), bf16),
            pltpu.VMEM((width, ff), bf16),
            pltpu.VMEM((ff, width), bf16),
            pltpu.SemaphoreType.DMA((count - 2,)),
            pltpu.SemaphoreType.DMA((count - 2,)),
            pltpu.SemaphoreType.DMA((count - 2,)),
        ],
        compiler_params=pltpu.CompilerParams(vmem_limit_bytes=47 << 20),
        name="down",
        cost_estimate=cost(16),
    )(info, nrm, hat, inv, act, slope, cot, bd, gf, sf, ga, *wu, *wd)


def per_device(
    tokens, cotangent, pair_lengths, prefix_key, prefix_value, w_query, b_query, w_key, w_value, b_value,
    w_out, b_out, gain_attn, shift_attn, w_up, b_up, w_down, b_down, gain_ffn, shift_ffn,
):
    n_row, n_seq = lax.axis_size("row"), lax.axis_size("seq")
    r, s = lax.axis_index("row"), lax.axis_index("seq")
    core, x, zbit = r & 1, s & 1, (s >> 1) & 1
    tok_count, width = tokens.shape[1], tokens.shape[2]

    def by_core(a):
        return lax.ppermute(a, "row", [(i, i ^ 1) for i in range(n_row)])

    def by_y(a):
        return lax.ppermute(a, "row", [(i, i ^ 2) for i in range(n_row)])

    def by_seq(a, bit):
        return lax.ppermute(a, "seq", [(i, i ^ bit) for i in range(n_seq)])

    def by_both(a, row_bit, bit):
        route = [(i * n_seq + j, (i ^ row_bit) * n_seq + (j ^ bit)) for i in range(n_row) for j in range(n_seq)]
        return lax.ppermute(a, ("row", "seq"), route)

    def here(z):
        return z

    def near(z):
        return z ^ 1

    def far(z):
        to = z + 1 if z & 1 else z - 1
        return to if 0 <= to < n_seq // 2 else z

    def along(a, partner):
        return lax.ppermute(a, "seq", [(j, 2 * partner(j // 2) + (j & 1)) for j in range(n_seq)])

    def swapped(a, partner=here):
        route = []
        for i in range(n_row):
            for j in range(n_seq):
                to = ((i & ~1) | (j & 1)) * n_seq + 2 * partner(j // 2) + (i & 1)
                route.append((i * n_seq + j, to))
        return lax.ppermute(a, ("row", "seq"), route)

    def after(a, *others):
        return lax.optimization_barrier((a,) + others)[0]

    h = x ^ zbit
    first_q, second_q = 2 * h + x, 2 * h + 1 - x
    m = w_query.shape[0]
    others = [2 * (1 - h) + 1 - x, 2 * (1 - h) + x]
    places = [r * m, (r ^ 1) * m]
    halves = [(r ^ k) * m + j * (m // 4) for k in (2, 3) for j in [2 * h] + others]
    quarters = [(r ^ k) * m + j * (m // 4) for k in (2, 3) for j in [first_q, second_q] + others]
    odd = (s >> 1) & 1
    info = jnp.stack([core] + places + quarters + halves + [first_q, second_q, h]).astype(jnp.int32)
    attn = (w_query, w_key, w_value)
    short, ff = w_query.shape[0] // 4, w_up.shape[1]
    plan = [(i, H_AT, 0, i * width) for i in range(3)] + [(3, Q_AT, 1, 0), (4, Q_AT, 1, ff)]
    early, late = (w_query, w_key, w_value, w_up, w_out), (w_down, w_up, w_out)
    a_half, u_one = pack(info, early, [(2 * short, 3 * width), (short, ff + width)], plan)
    plan = [(0, Q_AT, 0, 0), (1, Q_AT + 1, 1, 0), (2, Q_AT + 1, 1, ff), (0, Q_AT + 1, 2, 0)]
    low = (w_down.shape[0] // 4, width)
    d_one, u_two, d_two = pack(after(info, u_one), late, [low, (short, ff + width), low], plan)
    a_half = by_y(a_half)
    own, close, distant = (swapped(tokens[0], k) for k in (here, near, far))
    a_own = [by_core(after(a, a_half)) for a in attn]
    mates = a_own
    a_part = lax.dynamic_slice_in_dim(a_half, x * short, short, 0)
    a_x, a_z = by_seq(a_part, 1), by_seq(a_part, 2)
    u_one = by_y(u_one)
    d_one = by_y(after(d_one, a_x))
    u_two = by_y(after(u_two, a_z))
    toks = [own, close, distant]
    toks = toks + [by_core(a) for a in toks]
    a_got = [a_half, a_x, a_z]
    a_got = a_got + [by_core(a_half), by_core(a_x), by_core(a_z)]
    u_own, o_own = by_core(after(w_up, a_z)), by_core(after(w_out, a_z))
    theirs = by_core(after(pair_lengths, a_x))
    lengths = jnp.where(x == core, pair_lengths, theirs)[0]
    pairs = lengths.shape[0]
    later = jnp.arange(pairs)[:, None] >= jnp.arange(pairs)[None, :]
    ends = jnp.sum(jnp.where(later, lengths[None, :], 0), axis=1)
    base = (s // 2) * 2 * tok_count
    place = base + jnp.arange(2 * tok_count, dtype=jnp.int32)
    passed = ends[:, None] <= place[None, :]
    origin = base - 2 * tok_count
    first = jnp.max(jnp.where(passed, ends[:, None], 0), axis=0) - origin
    last = jnp.min(jnp.where(passed, n_seq * tok_count, ends[:, None]), axis=0) - origin
    bounds = jnp.stack([first[::TILE] // TILE, (last[TILE - 1 :: TILE] + TILE - 1) // TILE], 1)
    tile_info = jnp.concatenate([odd[None], bounds.reshape(-1), core[None]]).astype(jnp.int32)
    first, last = first[None], last[None]

    (att_keep, att_send, ot, lse, pk, pkt, pv, q, qt, k, kt, v, w_half) = front(
        info, tile_info, first, last, b_query, b_value, prefix_key, prefix_value, toks,
        (w_query, w_key, w_value), mates[:3], a_got,
    )
    u_x, u_z = by_seq(u_one, 1), by_seq(u_one, 2)
    d_own = by_core(after(w_down, lse))
    cot = swapped(after(cotangent[0], lse))
    d_two = by_y(after(d_two, lse))
    d_one, lse = lax.optimization_barrier((d_one, lse))
    d_x, d_z = by_seq(d_one, 1), by_seq(d_one, 2)
    u_got = [u_one, u_two, u_x, u_z]
    u_got = u_got + [by_core(after(a, lse)) for a in u_got]
    parts_u = [w_up, w_out, u_own, o_own] + u_got
    nrm, hat, inv, act, slope = up(
        info, att_keep, by_core(att_send), own, b_out, gain_attn, shift_attn, b_up,
        parts_u,
    )
    d_got = [d_one, d_two, d_x, d_z]
    d_got = d_got + [by_core(a if a is d_one else after(a, inv, cot)) for a in d_got]
    parts_d = [w_down, d_own] + d_got
    result, gh, ga_keep, ga_send = down(
        info, nrm, hat, inv, act, slope, cot, b_down, gain_ffn, shift_ffn, gain_attn,
        parts_u, parts_d,
    )
    out_tokens = swapped(result)
    pre, dqt, do, dot_, inner = prefix_grads(info, q, qt, pk, pkt, pv, ga_keep, by_core(ga_send), ot, lse)

    def summed(a, one, two):
        low = a.astype(bf16)
        sides = [by_both(low, *one), by_both(low, *two), by_both(low, one[0] | two[0], one[1] | two[1])]
        low, p, q, r = (v.astype(f32) for v in [low] + sides)
        return (low + p) + (q + r)

    bits = [(2, 0)] + [(0, 1 << i) for i in range(n_seq.bit_length() - 1)]
    if len(bits) % 2:
        low = pre.astype(bf16)
        pre = low.astype(f32) + by_both(low, *bits[0]).astype(f32)
        bits = bits[1:]
    pre = summed(pre, bits[0], bits[1])
    give, keep_near, keep_far, dqt = remote_grads(
        tile_info, first, last, q, qt, k, kt, v, do, dot_, lse, inner, dqt, w_half
    )
    give, out_tokens, pre = lax.optimization_barrier((give, out_tokens, pre))
    got = by_core(give)
    near_part = (keep_near.astype(f32) + got[:tok_count].astype(f32)).astype(bf16)
    far_part = (keep_far.astype(f32) + got[tok_count:].astype(f32)).astype(bf16)
    tile_info, near_part, far_part = lax.optimization_barrier((tile_info, near_part, far_part))
    pre = after(pre, near_part)
    near_part, far_part = along(near_part, near), along(far_part, far)
    for i in range(2, len(bits), 2):
        pre = summed(pre, bits[i], bits[i + 1])
    keep, give = local_grads(
        tile_info, first, last, q, qt, k, kt, v, do, dot_, lse, inner, dqt, gh, w_half
    )
    pre, give, near_part, far_part = lax.optimization_barrier((pre, give, near_part, far_part))
    mine = (keep + near_part.astype(f32)) + (by_core(give).astype(f32) + far_part.astype(f32))
    grad_tokens = swapped(mine.astype(bf16))
    other = by_core(pre)
    pre = jnp.concatenate(
        [jnp.where(core == 0, pre, other), jnp.where(core == 0, other, pre)], axis=1
    )
    n_pre = prefix_key.shape[0]
    return out_tokens[None], grad_tokens[None], pre[:n_pre], pre[n_pre:]


def solution(mesh):
    both, split, whole = P("row", "seq", None), P("row", None), P()
    return jax.shard_map(
        per_device,
        mesh=mesh,
        in_specs=(
            both, both, split, whole, whole, split, whole, split, split, whole, split, whole, whole, whole,
            split, whole, split, whole, whole, whole,
        ),
        out_specs=(both, both, whole, whole),
        check_vma=False,
    )
```

```python
import functools

import jax
import jax.numpy as jnp
from jax import lax
from jax.experimental import pallas as pl
from jax.experimental.pallas import tpu as pltpu
from jax.sharding import PartitionSpec as P

HEAD = 64
SCALE = HEAD**-0.5
LN_EPS = 1e-05
MASKED = -1e30
TILE = 256
CHUNK = 512
UP_PARTS = 1
HALF_AT, Q_AT, H_AT = 11, 17, 19
GRAD_LAGS = (0, 2, 2)

f32 = jnp.float32
bf16 = jnp.bfloat16
VM = pl.BlockSpec(memory_space=pltpu.VMEM)
SM = pl.BlockSpec(memory_space=pltpu.SMEM)
HB = pl.BlockSpec(memory_space=pltpu.HBM)


def cost(us):
    return pl.CostEstimate(flops=int(us * 1e9), bytes_accessed=0, transcendentals=0)


def shape_of(shape, kind):
    return jax.ShapeDtypeStruct(shape, kind)


def dot(a, b, ca=1, cb=0):
    return lax.dot_general(a, b, (((ca,), (cb,)), ((), ())), preferred_element_type=f32)


def row_at(offset, rows):
    return pl.ds(pl.multiple_of(offset, 64), rows)


def start_all(pairs, sems):
    made = [pltpu.make_async_copy(s, d, sems.at[i]) for i, (s, d) in enumerate(pairs)]
    for one in made:
        one.start()
    return made


def wait_all(made):
    for one in made:
        one.wait()


def normalised(v):
    centred = v - jnp.mean(v, axis=-1, keepdims=True)
    inv = lax.rsqrt(jnp.mean(centred * centred, axis=-1, keepdims=True) + LN_EPS)
    return centred * inv, inv


def norm_back(g, n, inv):
    return (g - jnp.mean(g, -1, keepdims=True) - n * jnp.mean(g * n, -1, keepdims=True)) * inv


def pack_kernel(info, *rest, plan, n_in, n_out):
    srcs, outs, bufs = rest[:n_in], rest[n_in : n_in + n_out], rest[n_in + n_out : n_in + 2 * n_out]
    sem_in, sem_out = rest[n_in + 2 * n_out :]
    pairs = []
    for i, which, o, col in plan:
        rows, cols = outs[o].shape[0], srcs[i].shape[1]
        pairs.append((srcs[i].at[row_at(info[which] * rows, rows), :], bufs[o].at[:, pl.ds(col, cols)]))
    wait_all(start_all(pairs, sem_in))
    wait_all(start_all(list(zip(bufs, outs)), sem_out))


def pack(info, srcs, shapes, plan):
    return pl.pallas_call(
        functools.partial(pack_kernel, plan=plan, n_in=len(srcs), n_out=len(shapes)),
        out_shape=tuple(shape_of(a, bf16) for a in shapes),
        in_specs=[SM] + [HB] * len(srcs),
        out_specs=(HB,) * len(shapes),
        scratch_shapes=[pltpu.VMEM(a, bf16) for a in shapes]
        + [pltpu.SemaphoreType.DMA((len(plan),)), pltpu.SemaphoreType.DMA((len(shapes),))],
        compiler_params=pltpu.CompilerParams(vmem_limit_bytes=58 << 20),
        name="pack",
        cost_estimate=cost(2),
    )(info, *srcs)


def head_rows(ref, h, at):
    own = ref[pl.ds(h * HEAD, HEAD), at]
    zero = jnp.zeros_like(own)
    return jnp.concatenate([own, zero] if h % 2 == 0 else [zero, own], 0)


def head_cols(ref, h, at):
    block = ref[at, pl.ds((h // 2) * 2 * HEAD, 2 * HEAD)]
    lane = lax.broadcasted_iota(jnp.int32, block.shape, 1)
    return jnp.where((lane < HEAD) == (h % 2 == 0), block, jnp.zeros_like(block))


def pair_cols(h):
    return pl.ds((h // 2) * 2 * HEAD, 2 * HEAD)


def allowed_bias(k0, first, last):
    place = k0 + lax.broadcasted_iota(jnp.int32, (TILE, TILE), 0)
    return jnp.where((place >= first) & (place < last), 0.0, MASKED).astype(f32)


def staged(heads, stages, lags):
    held = [{} for _ in stages]
    for step in range(heads + sum(lags)):
        behind = 0
        for i, stage in enumerate(stages):
            behind += lags[i]
            h = step - behind
            if 0 <= h < heads:
                held[i][h] = stage(h, held[i - 1].pop(h) if i else None)


def front_kernel(info, tiles, first, last, bq, bv, pk, pv, *rest, count, half):
    tok_in = rest[:6]
    own, mate = rest[6:9], rest[9:12]
    pieces = rest[12 : 12 + count]
    outs = rest[12 + count : 25 + count]
    keep_ref, send_ref, ot_out, lse_out, pk_out, pkt_out, pv_out = outs[:7]
    q_out, qt_out, k_out, kt_out, v_out, w_out = outs[7:]
    (tok, w_ref, q_ref, qt_ref, k_ref, kt_ref, v_ref, vt_ref, pk_ref, pkt_ref, pv_ref, pvt_ref, ot_ref, lse_ref,
     att, stat, acc, bias, sem_x, sem_w, sem_o, sem_a) = rest[25 + count :]
    core = info[0]
    tokens = tok_in[0].shape[0]
    width = tok.shape[1]
    pairs = []
    for i in range(6):
        place = (1, 2 - 2 * tiles[0], 2 * tiles[0])[i % 3]
        slot = 2 * place + (core if i < 3 else 1 - core)
        pairs.append((tok_in[i], tok.at[row_at(slot * tokens, tokens), :]))
    got_tok = start_all(pairs, sem_x)
    cols = pl.multiple_of(core * half, 128)
    got_w = []
    for i in (1, 2, 0):
        pairs = []
        for j, ref in enumerate((own[i], mate[i])):
            pairs.append((ref.at[:, pl.ds(cols, half)], w_ref.at[i, row_at(info[1 + j], ref.shape[0]), :]))
        for j, ref in enumerate(pieces):
            pairs.append(
                (
                    ref.at[:, pl.ds(i * width + cols, half)],
                    w_ref.at[i, row_at(info[HALF_AT + j], ref.shape[0]), :],
                )
            )
        got_w.append(start_all(pairs, sem_w.at[i]))
    pk_half, pv_half = pk[:, pl.ds(cols, half)], pv[:, pl.ds(cols, half)]
    pk_ref[...], pkt_ref[...] = pk_half, pk_half.astype(f32).T.astype(bf16)
    pv_ref[...], pvt_ref[...] = pv_half, pv_half.astype(f32).T.astype(bf16)
    bias_v = bv[pl.ds(cols, half)].astype(f32)[None, :]
    bias_q = bq[pl.ds(cols, half)].astype(f32)[None, :]
    blocks = k_ref.shape[0] // TILE
    wait_all(got_tok)
    wait_all(got_w[0])

    def key_block(b, carry):
        at = pl.ds(pl.multiple_of(b * TILE, TILE), TILE)
        full = dot(tok[at, :], w_ref[1])
        k_ref[at, :] = full.astype(bf16)
        kt_ref[:, at] = full.T.astype(bf16)
        return carry

    lax.fori_loop(0, blocks, key_block, 0, unroll=2)
    wait_all(got_w[1])

    def value_block(b, carry):
        at = pl.ds(pl.multiple_of(b * TILE, TILE), TILE)
        full = dot(tok[at, :], w_ref[2]) + bias_v
        v_ref[at, :] = full.astype(bf16)
        vt_ref[:, at] = full.T.astype(bf16)
        return carry

    lax.fori_loop(0, blocks, value_block, 0, unroll=2)
    wait_all(got_w[2])

    def query_block(b, carry):
        at = pl.ds(pl.multiple_of(b * TILE, TILE), TILE)
        src = pl.ds(pl.multiple_of(b * TILE + 2 * tokens, TILE), TILE)
        full = (dot(tok[src, :], w_ref[0]) + bias_q).astype(bf16).astype(f32) * SCALE
        q_ref[at, :] = full.astype(bf16)
        qt_ref[:, at] = full.T.astype(bf16)
        return carry

    lax.fori_loop(0, 2 * tokens // TILE, query_block, 0, unroll=2)
    pairs = [(w_ref, w_out), (k_ref, k_out), (kt_ref, kt_out), (v_ref, v_out), (q_ref, q_out), (qt_ref, qt_out)]
    pairs += [(pk_ref, pk_out), (pkt_ref, pkt_out), (pv_ref, pv_out)]
    saved = start_all(pairs, sem_o)
    heads = half // HEAD

    def one_query_tile(t, carry):
        at = pl.ds(pl.multiple_of(t * TILE, TILE), TILE)
        qs, qe = first[:, at], last[:, at]

        def prefix_score(h, _):
            return dot(pk_ref[:, pair_cols(h)], head_rows(qt_ref, h, at))

        def prefix_soft(h, s):
            top = jnp.max(s, axis=0, keepdims=True)
            p = jnp.exp(s - top)
            stat[pl.ds(h, 1), :] = top
            stat[pl.ds(heads + h, 1), :] = jnp.sum(p, axis=0, keepdims=True)
            return p.astype(bf16)

        def prefix_mix(h, p):
            acc[pl.ds(h * HEAD, HEAD), :] = dot(pvt_ref[pl.ds(h * HEAD, HEAD), :], p)

        staged(heads, (prefix_score, prefix_soft, prefix_mix), (0, 1, 3))

        def one_key_tile(j, inner):
            k0 = pl.multiple_of(j * TILE, TILE)
            bias[...] = allowed_bias(k0, qs, qe)

            def score(h, _):
                return dot(k_ref[pl.ds(k0, TILE), pair_cols(h)], head_rows(qt_ref, h, at))

            def soft(h, s):
                s = s + bias[...]
                old = stat[pl.ds(h, 1), :]
                top = jnp.maximum(old, jnp.max(s, axis=0, keepdims=True))
                factor = jnp.exp(old - top)
                p = jnp.exp(s - top)
                stat[pl.ds(h, 1), :] = top
                total = jnp.sum(p, axis=0, keepdims=True)
                stat[pl.ds(heads + h, 1), :] = stat[pl.ds(heads + h, 1), :] * factor + total
                return p.astype(bf16), factor

            def mix(h, held):
                p, factor = held
                rows = pl.ds(h * HEAD, HEAD)
                acc[rows, :] = acc[rows, :] * factor + dot(vt_ref[rows, pl.ds(k0, TILE)], p)

            staged(heads, (score, soft, mix), (0, 1, 3))
            return inner

        lax.fori_loop(tiles[1 + 2 * t], tiles[2 + 2 * t], one_key_tile, 0)
        for h in range(heads):
            rows = pl.ds(h * HEAD, HEAD)
            acc[rows, :] = acc[rows, :] / stat[pl.ds(heads + h, 1), :]
        ot_ref[:, at] = acc[...]
        lse_ref[:, at] = stat[pl.ds(0, heads), :] + jnp.log(stat[pl.ds(heads, heads), :])
        att[at, :] = acc[...].T.astype(bf16)
        return carry

    lax.fori_loop(0, 2 * tokens // TILE, one_query_tile, 0)
    mine, theirs = row_at(core * tokens, tokens), row_at((1 - core) * tokens, tokens)
    pairs = [(att.at[theirs, :], send_ref), (att.at[mine, :], keep_ref), (ot_ref, ot_out), (lse_ref, lse_out)]
    wait_all(start_all(pairs, sem_a))
    wait_all(saved)


def front(info, tiles, first, last, bq, bv, pk, pv, toks, own, mate, pieces):
    tokens, width = toks[0].shape
    half = width // 2
    heads, pre = half // HEAD, pk.shape[0]
    n_q, n_k = 2 * tokens, 6 * tokens
    count = len(pieces)
    kept = [(n_q, half), (half, n_q), (n_k, half), (half, n_k), (n_k, half)]
    pres = [(pre, half), (half, pre), (pre, half)]
    stats = [(half, n_q), (heads, n_q)]
    outs = [shape_of((tokens, half), bf16)] * 2 + [shape_of(a, f32) for a in stats]
    outs += [shape_of(a, bf16) for a in pres + kept + [(3, width, half)]]
    vmem = [(n_k, width), (3, width, half)] + kept + [(half, n_k)] + pres + [(half, pre)]
    return pl.pallas_call(
        functools.partial(front_kernel, count=count, half=half),
        out_shape=tuple(outs),
        in_specs=[SM, SM] + [VM] * 6 + [HB] * (12 + count),
        out_specs=(HB,) * len(outs),
        scratch_shapes=[pltpu.VMEM(a, bf16) for a in vmem]
        + [pltpu.VMEM(a, f32) for a in stats]
        + [
            pltpu.VMEM((n_q, half), bf16),
            pltpu.VMEM((2 * heads, TILE), f32),
            pltpu.VMEM((half, TILE), f32),
            pltpu.VMEM((TILE, TILE), f32),
            pltpu.SemaphoreType.DMA((6,)),
            pltpu.SemaphoreType.DMA((3, 2 + count)),
            pltpu.SemaphoreType.DMA((9,)),
            pltpu.SemaphoreType.DMA((4,)),
        ],
        compiler_params=pltpu.CompilerParams(vmem_limit_bytes=60 << 20),
        name="front",
        cost_estimate=cost(20),
    )(info, tiles, first, last, bq, bv, pk, pv, *toks, *own, *mate, *pieces)


def grad_stages(q, qt, kb, vb, ktb, do, do_t, lse, inner, bias, put):
    def products(h, _):
        return dot(kb(h), qt(h)), dot(vb(h), do_t(h))

    def scores(h, held):
        s, dp = held
        if bias is not None:
            s = s + bias[...]
        p = jnp.exp(s - lse(h))
        return p.astype(bf16), (p * (dp - inner(h))).astype(bf16)

    def sums(h, held):
        p, ds = held
        put(h, dot(p, do(h)), dot(ds, q(h)), dot(ktb(h), ds))

    return products, scores, sums


def sweep(ranges, at, first, last, refs, acc, heads):
    q_ref, qt_ref, k_ref, kt_ref, v_ref, do_ref, dot_ref, lse_ref, inner_ref, bias = refs
    dqt, dk, dv = acc
    qs, qe = first[:, at], last[:, at]

    def one_key_tile(j, carry):
        k0 = pl.multiple_of(j * TILE, TILE)
        r = pl.ds(k0, TILE)
        bias[...] = allowed_bias(k0, qs, qe)

        def put(h, gv, gk, gq):
            c, rows = pair_cols(h), pl.ds(h * HEAD, HEAD)
            dv[r, c] += gv
            dk[r, c] += gk
            dqt[rows, at] += gq

        stages = grad_stages(
            lambda h: head_cols(q_ref, h, at), lambda h: head_rows(qt_ref, h, at),
            lambda h: k_ref[r, pair_cols(h)], lambda h: v_ref[r, pair_cols(h)],
            lambda h: kt_ref[pl.ds(h * HEAD, HEAD), r], lambda h: head_cols(do_ref, h, at),
            lambda h: head_rows(dot_ref, h, at), lambda h: lse_ref[pl.ds(h, 1), at],
            lambda h: inner_ref[pl.ds(h, 1), at], bias, put,
        )
        staged(heads, stages, GRAD_LAGS)
        return carry

    for lo, hi in ranges:
        lax.fori_loop(lo, hi, one_key_tile, 0)


def prefix_grads_kernel(
    info, q_ref, qt_ref, pk_ref, pkt_ref, pv_ref, keep_in, recv_in, ot_ref, lse_ref,
    pre_ref, dqt, do_s, dot_s, inner_s, *, heads,
):
    core = info[0]
    tokens = keep_in.shape[0]
    n_q, pre = q_ref.shape[0], pk_ref.shape[0]
    do_s[row_at(core * tokens, tokens), :] = keep_in[...]
    do_s[row_at((1 - core) * tokens, tokens), :] = recv_in[...]
    pre_ref[...] = jnp.zeros_like(pre_ref)

    def one_query_tile(t, carry):
        at = pl.ds(pl.multiple_of(t * TILE, TILE), TILE)
        dot_s[:, at] = do_s[at, :].astype(f32).T.astype(bf16)
        for h in range(heads):
            rows = pl.ds(h * HEAD, HEAD)
            inner_s[pl.ds(h, 1), at] = jnp.sum(
                dot_s[rows, at].astype(f32) * ot_ref[rows, at], axis=0, keepdims=True
            )

        def put(h, gv, gk, gq):
            c = pair_cols(h)
            pre_ref[pl.ds(0, pre), c] += gk
            pre_ref[pl.ds(pre, pre), c] += gv
            dqt[pl.ds(h * HEAD, HEAD), at] = gq

        stages = grad_stages(
            lambda h: head_cols(q_ref, h, at), lambda h: head_rows(qt_ref, h, at),
            lambda h: pk_ref[:, pair_cols(h)], lambda h: pv_ref[:, pair_cols(h)],
            lambda h: pkt_ref[pl.ds(h * HEAD, HEAD), :], lambda h: head_cols(do_s, h, at),
            lambda h: head_rows(dot_s, h, at), lambda h: lse_ref[pl.ds(h, 1), at],
            lambda h: inner_s[pl.ds(h, 1), at], None, put,
        )
        staged(heads, stages, GRAD_LAGS)
        return carry

    lax.fori_loop(0, n_q // TILE, one_query_tile, 0)


def prefix_grads(info, q, qt, pk, pkt, pv, keep, recv, ot, lse):
    n_q, half = q.shape
    heads, pre = half // HEAD, pk.shape[0]
    return pl.pallas_call(
        functools.partial(prefix_grads_kernel, heads=heads),
        out_shape=(
            shape_of((2 * pre, half), f32),
            shape_of((half, n_q), f32),
            shape_of((n_q, half), bf16),
            shape_of((half, n_q), bf16),
            shape_of((heads, n_q), f32),
        ),
        in_specs=[SM] + [VM] * 9,
        out_specs=(VM,) * 5,
        compiler_params=pltpu.CompilerParams(vmem_limit_bytes=10 << 20),
        name="prefix_grads",
        cost_estimate=cost(5),
    )(info, q, qt, pk, pkt, pv, keep, recv, ot, lse)


def remote_grads_kernel(
    info, first, last, q_ref, qt_ref, k_ref, kt_ref, v_ref, do_ref, dot_ref, lse_ref, inner_ref, dqt_in,
    w_in, give_ref, keep_near, keep_far, dqt, dk, dv, bias, wsc, wsem, *, heads,
):
    copies = start_all([(w_in.at[1], wsc.at[0]), (w_in.at[2], wsc.at[1])], wsem)
    n_q = q_ref.shape[0]
    tokens = n_q // 2
    core = info[1 + 2 * (n_q // TILE)]
    dk[...] = jnp.zeros_like(dk)
    dv[...] = jnp.zeros_like(dv)
    dqt[...] = dqt_in[...]

    def one_query_tile(t, carry):
        at = pl.ds(pl.multiple_of(t * TILE, TILE), TILE)
        lo, hi = info[1 + 2 * t], info[2 + 2 * t]
        side = 2 * tokens // TILE
        refs = (q_ref, qt_ref, k_ref, kt_ref, v_ref, do_ref, dot_ref, lse_ref, inner_ref, bias)
        ranges = ((lo, jnp.minimum(hi, side)), (jnp.maximum(lo, 2 * side), hi))
        sweep(ranges, at, first, last, refs, (dqt, dk, dv), heads)
        return carry

    lax.fori_loop(0, n_q // TILE, one_query_tile, 0)
    wait_all(copies)
    for i, keep in ((0, keep_near), (1, keep_far)):
        for mine in (True, False):
            block = core if mine else 1 - core
            side = info[0] if i else 1 - info[0]
            r = row_at(side * 4 * tokens + block * tokens, tokens)
            out = dot(dk[r, :].astype(bf16), wsc[0], 1, 1) + dot(dv[r, :].astype(bf16), wsc[1], 1, 1)
            if mine:
                keep[...] = out.astype(bf16)
            else:
                give_ref[pl.ds(i * tokens, tokens), :] = out.astype(bf16)


def remote_grads(info, first, last, q, qt, k, kt, v, do, dot_, lse, inner, dqt, w):
    n_q, half = q.shape
    heads, tokens, width = half // HEAD, n_q // 2, w.shape[1]
    n_k = k.shape[0]
    return pl.pallas_call(
        functools.partial(remote_grads_kernel, heads=heads),
        out_shape=(
            shape_of((2 * tokens, width), bf16),
            shape_of((tokens, width), bf16),
            shape_of((tokens, width), bf16),
            shape_of((half, n_q), f32),
        ),
        in_specs=[SM] + [VM] * 12 + [HB],
        out_specs=(VM,) * 4,
        scratch_shapes=[
            pltpu.VMEM((n_k, half), f32),
            pltpu.VMEM((n_k, half), f32),
            pltpu.VMEM((TILE, TILE), f32),
            pltpu.VMEM((2, width, half), bf16),
            pltpu.SemaphoreType.DMA((2,)),
        ],
        compiler_params=pltpu.CompilerParams(vmem_limit_bytes=24 << 20),
        name="remote_grads",
        cost_estimate=cost(14),
    )(info, first, last, q, qt, k, kt, v, do, dot_, lse, inner, dqt, w)


def local_grads_kernel(
    info, first, last, q_ref, qt_ref, k_ref, kt_ref, v_ref, do_ref, dot_ref, lse_ref, inner_ref, dqt_in,
    gh_ref, w_in, keep_ref, give_ref, dqt, dk, dv, bias, wsc, wsem, *, heads,
):
    copies = start_all([(w_in, wsc)], wsem)
    core = info[1 + 2 * (q_ref.shape[0] // TILE)]
    n_q = q_ref.shape[0]
    tokens = n_q // 2
    dqt[...] = dqt_in[...]
    dk[...] = jnp.zeros_like(dk)
    dv[...] = jnp.zeros_like(dv)
    side = 2 * tokens // TILE

    def one_query_tile(t, carry):
        at = pl.ds(pl.multiple_of(t * TILE, TILE), TILE)
        lo, hi = info[1 + 2 * t], info[2 + 2 * t]
        refs = (q_ref, qt_ref, k_ref, kt_ref, v_ref, do_ref, dot_ref, lse_ref, inner_ref, bias)
        ranges = ((jnp.maximum(lo, side), jnp.minimum(hi, 2 * side)),)
        sweep(ranges, at, first, last, refs, (dqt, dk, dv), heads)
        return carry

    lax.fori_loop(0, n_q // TILE, one_query_tile, 0)
    wait_all(copies)
    for mine in (False, True):
        block = core if mine else 1 - core
        r = row_at(block * tokens, tokens)
        rk = row_at(block * tokens + n_q, tokens)
        dq = (dqt[:, r] * SCALE).T.astype(bf16)
        out = (
            dot(dq, wsc[0], 1, 1)
            + dot(dk[rk, :].astype(bf16), wsc[1], 1, 1)
            + dot(dv[rk, :].astype(bf16), wsc[2], 1, 1)
        )
        if mine:
            keep_ref[...] = out + gh_ref[...]
        else:
            give_ref[...] = out.astype(bf16)


def local_grads(info, first, last, q, qt, k, kt, v, do, dot_, lse, inner, dqt, gh, w):
    n_q, half = q.shape
    heads, tokens, width = half // HEAD, n_q // 2, w.shape[1]
    n_k = k.shape[0]
    return pl.pallas_call(
        functools.partial(local_grads_kernel, heads=heads),
        out_shape=(shape_of((tokens, width), f32), shape_of((tokens, width), bf16)),
        in_specs=[SM] + [VM] * 13 + [HB],
        out_specs=(VM,) * 2,
        scratch_shapes=[
            pltpu.VMEM((half, n_q), f32),
            pltpu.VMEM((n_k, half), f32),
            pltpu.VMEM((n_k, half), f32),
            pltpu.VMEM((TILE, TILE), f32),
            pltpu.VMEM((3, width, half), bf16),
            pltpu.SemaphoreType.DMA((1,)),
        ],
        compiler_params=pltpu.CompilerParams(vmem_limit_bytes=23 << 20),
        name="local_grads",
        cost_estimate=cost(14),
    )(info, first, last, q, qt, k, kt, v, do, dot_, lse, inner, dqt, gh, w)


def placed(refs, info, at, scale, dst, cols=None):
    pairs = []
    for i, ref in enumerate(refs):
        src = ref if cols is None else ref.at[:, cols[0]]
        rows = row_at(info[at + i] * scale, ref.shape[0])
        pairs.append((src, dst.at[rows, :] if cols is None else dst.at[rows, cols[1]]))
    return pairs


def up_pairs(parts, info, dst, cols):
    return placed((parts[0], parts[2]) + tuple(parts[4:]), info, 1, 1, dst, (cols, cols))


def out_pairs(parts, info, ff, dst):
    whole = pl.ds(0, dst.shape[1])
    return placed((parts[1], parts[3]), info, 1, 1, dst) + placed(
        parts[4:], info, 3, 1, dst, (pl.ds(ff, dst.shape[1]), whole)
    )


def up_kernel(info, own_att, got_att, tok, bo, ga, sa, bu, *rest, count):
    wu = rest[:count]
    hat_ref, inv_ref, act_ref, slope_ref, wo_s, wu_s, own_s, got_s, tok_s, sem_a, sem_o, sem_u = rest[count:]
    acts = start_all([(own_att, own_s), (got_att, got_s), (tok, tok_s)], sem_a)
    width, ff = wu_s.shape
    half = own_att.shape[1]
    got_o = start_all(out_pairs(wu, info, ff, wo_s), sem_o)
    part = ff // UP_PARTS
    got_u = []
    for j in range(UP_PARTS):
        got_u.append(start_all(up_pairs(wu, info, wu_s, pl.ds(j * part, part)), sem_u.at[j]))
    core = info[0]
    wait_all(acts)
    wait_all(got_o)
    hidden = (
        tok_s[...].astype(f32)
        + dot(own_s[...], wo_s[row_at(core * half, half), :])
        + dot(got_s[...], wo_s[row_at((1 - core) * half, half), :])
        + bo[...].astype(f32)[None, :]
    )
    hat, inv = normalised(hidden)
    hat_ref[...] = hat
    inv_ref[...] = jnp.broadcast_to(inv, inv_ref.shape)
    nrm = hat * ga[...].astype(f32)[None, :] + sa[...].astype(f32)[None, :]
    low = nrm.astype(bf16)
    for j in range(ff // CHUNK):
        if (j * CHUNK) % part == 0:
            wait_all(got_u[j * CHUNK // part])
        cs = pl.ds(j * CHUNK, CHUNK)
        v = dot(low, wu_s[:, cs]) + bu[cs].astype(f32)[None, :]
        phi = 0.5 + 0.5 * lax.erf(v * (0.5**0.5))
        act_ref[:, cs] = (v * phi).astype(bf16)
        slope_ref[:, cs] = (phi + v * (jnp.exp(v * v * -0.5) * 0.3989422804014327)).astype(bf16)


def up(info, own_att, got_att, tok, bo, ga, sa, bu, wu):
    tokens, width = tok.shape
    ff, count = bu.shape[0], len(wu)
    return pl.pallas_call(
        functools.partial(up_kernel, count=count),
        out_shape=(
            shape_of((tokens, width), f32),
            shape_of((tokens, 128), f32),
            shape_of((tokens, ff), bf16),
            shape_of((tokens, ff), bf16),
        ),
        in_specs=[SM] + [HB] * 3 + [VM] * 4 + [HB] * count,
        out_specs=(VM,) * 4,
        scratch_shapes=[
            pltpu.VMEM((width, width), bf16),
            pltpu.VMEM((width, ff), bf16),
            pltpu.VMEM((tokens, width // 2), bf16),
            pltpu.VMEM((tokens, width // 2), bf16),
            pltpu.VMEM((tokens, width), bf16),
            pltpu.SemaphoreType.DMA((3,)),
            pltpu.SemaphoreType.DMA((count - 2,)),
            pltpu.SemaphoreType.DMA((UP_PARTS, count - 2)),
        ],
        compiler_params=pltpu.CompilerParams(vmem_limit_bytes=55 << 20),
        name="up",
        cost_estimate=cost(10),
    )(info, own_att, got_att, tok, bo, ga, sa, bu, *wu)


def down_kernel(info, hat_ref, inv_ref, act_ref, slope_ref, cot, bd, gf, sf, ga, sa, *rest, count):
    wu, wd = rest[:count], rest[count : 2 * count - 2]
    out_ref, gh_ref, keep_ref, send_ref, wo_s, wu_s, wd_s, sem_o, sem_u, sem_d = rest[2 * count - 2 :]
    width, ff = wu_s.shape
    half = keep_ref.shape[1]
    got_d = start_all(placed(wd, info, 1, ff // width, wd_s), sem_d)
    got_u = start_all(up_pairs(wu, info, wu_s, pl.ds(0, ff)), sem_u)
    got_o = start_all(out_pairs(wu, info, ff, wo_s), sem_o)
    core = info[0]
    nrm = hat_ref[...] * ga[...].astype(f32)[None, :] + sa[...].astype(f32)[None, :]
    summed = nrm + bd[...].astype(f32)[None, :]
    for i, one in enumerate(got_d):
        one.wait()
        size = wd[i].shape[0]
        at = row_at(info[1 + i] * (ff // width), size)
        cols = pl.ds(pl.multiple_of(info[1 + i] * (ff // width), 128), size)
        summed = summed + dot(act_ref[:, cols], wd_s[at, :])
    n, inv = normalised(summed)
    gain = gf[...].astype(f32)[None, :]
    out_ref[...] = (n * gain + sf[...].astype(f32)[None, :]).astype(bf16)
    gs = norm_back(cot[...].astype(f32) * gain, n, inv)
    low = gs.astype(bf16)
    wait_all(got_u)
    total = gs
    for j in range(ff // CHUNK):
        cs = pl.ds(j * CHUNK, CHUNK)
        gp = (dot(low, wd_s[cs, :], 1, 1) * slope_ref[:, cs].astype(f32)).astype(bf16)
        total = total + dot(gp, wu_s[:, cs], 1, 1)
    gh = norm_back(total * ga[...].astype(f32)[None, :], hat_ref[...], inv_ref[:, :1])
    gh_ref[...] = gh
    gh_low = gh.astype(bf16)
    wait_all(got_o)
    send_ref[...] = dot(gh_low, wo_s[row_at((1 - core) * half, half), :], 1, 1).astype(bf16)
    keep_ref[...] = dot(gh_low, wo_s[row_at(core * half, half), :], 1, 1).astype(bf16)


def down(info, hat, inv, act, slope, cot, bd, gf, sf, ga, sa, wu, wd):
    tokens, width = hat.shape
    ff, count = act.shape[1], len(wu)
    return pl.pallas_call(
        functools.partial(down_kernel, count=count),
        out_shape=(
            shape_of((tokens, width), bf16),
            shape_of((tokens, width), f32),
            shape_of((tokens, width // 2), bf16),
            shape_of((tokens, width // 2), bf16),
        ),
        in_specs=[SM] + [VM] * 10 + [HB] * (2 * count - 2),
        out_specs=(VM,) * 4,
        scratch_shapes=[
            pltpu.VMEM((width, width), bf16),
            pltpu.VMEM((width, ff), bf16),
            pltpu.VMEM((ff, width), bf16),
            pltpu.SemaphoreType.DMA((count - 2,)),
            pltpu.SemaphoreType.DMA((count - 2,)),
            pltpu.SemaphoreType.DMA((count - 2,)),
        ],
        compiler_params=pltpu.CompilerParams(vmem_limit_bytes=47 << 20),
        name="down",
        cost_estimate=cost(16),
    )(info, hat, inv, act, slope, cot, bd, gf, sf, ga, sa, *wu, *wd)


def per_device(
    tokens, cotangent, pair_lengths, prefix_key, prefix_value, w_query, b_query, w_key, w_value, b_value,
    w_out, b_out, gain_attn, shift_attn, w_up, b_up, w_down, b_down, gain_ffn, shift_ffn,
):
    n_row, n_seq = lax.axis_size("row"), lax.axis_size("seq")
    r, s = lax.axis_index("row"), lax.axis_index("seq")
    core, x, zbit = r & 1, s & 1, (s >> 1) & 1
    tok_count, width = tokens.shape[1], tokens.shape[2]

    def by_core(a):
        return lax.ppermute(a, "row", [(i, i ^ 1) for i in range(n_row)])

    def by_y(a):
        return lax.ppermute(a, "row", [(i, i ^ 2) for i in range(n_row)])

    def by_seq(a, bit):
        return lax.ppermute(a, "seq", [(i, i ^ bit) for i in range(n_seq)])

    def by_both(a, row_bit, bit):
        route = [(i * n_seq + j, (i ^ row_bit) * n_seq + (j ^ bit)) for i in range(n_row) for j in range(n_seq)]
        return lax.ppermute(a, ("row", "seq"), route)

    def here(z):
        return z

    def near(z):
        return z ^ 1

    def far(z):
        to = z + 1 if z & 1 else z - 1
        return to if 0 <= to < n_seq // 2 else z

    def along(a, partner):
        return lax.ppermute(a, "seq", [(j, 2 * partner(j // 2) + (j & 1)) for j in range(n_seq)])

    def swapped(a, partner=here):
        route = []
        for i in range(n_row):
            for j in range(n_seq):
                to = ((i & ~1) | (j & 1)) * n_seq + 2 * partner(j // 2) + (i & 1)
                route.append((i * n_seq + j, to))
        return lax.ppermute(a, ("row", "seq"), route)

    def after(a, *others):
        return lax.optimization_barrier((a,) + others)[0]

    h = x ^ zbit
    first_q, second_q = 2 * h + x, 2 * h + 1 - x
    m = w_query.shape[0]
    others = [2 * (1 - h) + 1 - x, 2 * (1 - h) + x]
    places = [r * m, (r ^ 1) * m]
    halves = [(r ^ k) * m + j * (m // 4) for k in (2, 3) for j in [2 * h] + others]
    quarters = [(r ^ k) * m + j * (m // 4) for k in (2, 3) for j in [first_q, second_q] + others]
    odd = (s >> 1) & 1
    info = jnp.stack([core] + places + quarters + halves + [first_q, second_q, h]).astype(jnp.int32)
    attn = (w_query, w_key, w_value)
    short, ff = w_query.shape[0] // 4, w_up.shape[1]
    plan = [(i, H_AT, 0, i * width) for i in range(3)] + [(3, Q_AT, 1, 0), (4, Q_AT, 1, ff)]
    early, late = (w_query, w_key, w_value, w_up, w_out), (w_down, w_up, w_out)
    a_half, u_one = pack(info, early, [(2 * short, 3 * width), (short, ff + width)], plan)
    plan = [(0, Q_AT, 0, 0), (1, Q_AT + 1, 1, 0), (2, Q_AT + 1, 1, ff), (0, Q_AT + 1, 2, 0)]
    low = (w_down.shape[0] // 4, width)
    d_one, u_two, d_two = pack(after(info, u_one), late, [low, (short, ff + width), low], plan)
    a_half = by_y(a_half)
    own, close, distant = (swapped(tokens[0], k) for k in (here, near, far))
    a_own = [by_core(after(a, a_half)) for a in attn]
    mates = a_own
    a_part = lax.dynamic_slice_in_dim(a_half, x * short, short, 0)
    a_x, a_z = by_seq(a_part, 1), by_seq(a_part, 2)
    u_one = by_y(u_one)
    u_two = by_y(u_two)
    d_one = by_y(after(d_one, a_x))
    toks = [own, close, distant]
    toks = toks + [by_core(a) for a in toks]
    a_got = [a_half, a_x, a_z]
    a_got = a_got + [by_core(a_half), by_core(a_x), by_core(a_z)]
    u_own, o_own = by_core(after(w_up, a_z)), by_core(after(w_out, a_z))
    theirs = by_core(after(pair_lengths, a_x))
    lengths = jnp.where(x == core, pair_lengths, theirs)[0]
    pairs = lengths.shape[0]
    later = jnp.arange(pairs)[:, None] >= jnp.arange(pairs)[None, :]
    ends = jnp.sum(jnp.where(later, lengths[None, :], 0), axis=1)
    base = (s // 2) * 2 * tok_count
    place = base + jnp.arange(2 * tok_count, dtype=jnp.int32)
    passed = ends[:, None] <= place[None, :]
    origin = base - 2 * tok_count
    first = jnp.max(jnp.where(passed, ends[:, None], 0), axis=0) - origin
    last = jnp.min(jnp.where(passed, n_seq * tok_count, ends[:, None]), axis=0) - origin
    bounds = jnp.stack([first[::TILE] // TILE, (last[TILE - 1 :: TILE] + TILE - 1) // TILE], 1)
    tile_info = jnp.concatenate([odd[None], bounds.reshape(-1), core[None]]).astype(jnp.int32)
    first, last = first[None], last[None]

    (att_keep, att_send, ot, lse, pk, pkt, pv, q, qt, k, kt, v, w_half) = front(
        info, tile_info, first, last, b_query, b_value, prefix_key, prefix_value, toks,
        (w_query, w_key, w_value), mates[:3], a_got,
    )
    u_x, u_z = by_seq(u_one, 1), by_seq(u_one, 2)
    d_own = by_core(after(w_down, lse))
    cot = swapped(after(cotangent[0], lse))
    d_two = by_y(after(d_two, lse))
    d_one, lse = lax.optimization_barrier((d_one, lse))
    d_x, d_z = by_seq(d_one, 1), by_seq(d_one, 2)
    u_got = [u_one, u_two, u_x, u_z]
    u_got = u_got + [by_core(after(a, lse)) for a in u_got]
    parts_u = [w_up, w_out, u_own, o_own] + u_got
    hat, inv, act, slope = up(
        info, att_keep, by_core(att_send), own, b_out, gain_attn, shift_attn, b_up,
        parts_u,
    )
    d_got = [d_one, d_two, d_x, d_z]
    d_got = d_got + [by_core(a if a is d_one else after(a, inv, cot)) for a in d_got]
    parts_d = [w_down, d_own] + d_got
    result, gh, ga_keep, ga_send = down(
        info, hat, inv, act, slope, cot, b_down, gain_ffn, shift_ffn, gain_attn, shift_attn,
        parts_u, parts_d,
    )
    out_tokens = swapped(result)
    pre, dqt, do, dot_, inner = prefix_grads(info, q, qt, pk, pkt, pv, ga_keep, by_core(ga_send), ot, lse)

    def summed(a, row_bit, bit):
        low = a.astype(bf16)
        return low.astype(f32) + by_both(low, row_bit, bit).astype(f32)

    pre = summed(pre, 2, 0)
    give, keep_near, keep_far, dqt = remote_grads(
        tile_info, first, last, q, qt, k, kt, v, do, dot_, lse, inner, dqt, w_half
    )
    give, out_tokens, pre = lax.optimization_barrier((give, out_tokens, pre))
    got = by_core(give)
    near_part = (keep_near.astype(f32) + got[:tok_count].astype(f32)).astype(bf16)
    far_part = (keep_far.astype(f32) + got[tok_count:].astype(f32)).astype(bf16)
    tile_info, near_part, far_part = lax.optimization_barrier((tile_info, near_part, far_part))
    pre = summed(pre, 0, 1)
    near_part, far_part = along(near_part, near), along(far_part, far)
    keep, give = local_grads(
        tile_info, first, last, q, qt, k, kt, v, do, dot_, lse, inner, dqt, gh, w_half
    )
    pre, give, near_part, far_part = lax.optimization_barrier((pre, give, near_part, far_part))
    for i in range(1, n_seq.bit_length() - 1):
        pre = summed(pre, 0, 1 << i)
    mine = (keep + near_part.astype(f32)) + (by_core(give).astype(f32) + far_part.astype(f32))
    grad_tokens = swapped(mine.astype(bf16))
    other = by_core(after(pre, grad_tokens))
    pre = jnp.concatenate(
        [jnp.where(core == 0, pre, other), jnp.where(core == 0, other, pre)], axis=1
    )
    n_pre = prefix_key.shape[0]
    return out_tokens[None], grad_tokens[None], pre[:n_pre], pre[n_pre:]


def solution(mesh):
    both, split, whole = P("row", "seq", None), P("row", None), P()
    return jax.shard_map(
        per_device,
        mesh=mesh,
        in_specs=(
            both, both, split, whole, whole, split, whole, split, split, whole, split, whole, whole, whole,
            split, whole, split, whole, whole, whole,
        ),
        out_specs=(both, both, whole, whole),
        check_vma=False,
    )
```

```python
import functools

import jax
import jax.numpy as jnp
from jax import lax
from jax.experimental import pallas as pl
from jax.experimental.pallas import tpu as pltpu
from jax.sharding import PartitionSpec as P

HEAD = 64
SCALE = HEAD**-0.5
LN_EPS = 1e-05
MASKED = -1e30
TILE = 256
CHUNK = 512
UP_PARTS = 1
HALF_AT, Q_AT, H_AT = 11, 17, 19
GRAD_LAGS = (0, 2, 2)

f32 = jnp.float32
bf16 = jnp.bfloat16
VM = pl.BlockSpec(memory_space=pltpu.VMEM)
SM = pl.BlockSpec(memory_space=pltpu.SMEM)
HB = pl.BlockSpec(memory_space=pltpu.HBM)


def cost(us):
    return pl.CostEstimate(flops=int(us * 1e9), bytes_accessed=0, transcendentals=0)


def shape_of(shape, kind):
    return jax.ShapeDtypeStruct(shape, kind)


def dot(a, b, ca=1, cb=0):
    return lax.dot_general(a, b, (((ca,), (cb,)), ((), ())), preferred_element_type=f32)


def row_at(offset, rows):
    return pl.ds(pl.multiple_of(offset, 64), rows)


def start_all(pairs, sems):
    made = [pltpu.make_async_copy(s, d, sems.at[i]) for i, (s, d) in enumerate(pairs)]
    for one in made:
        one.start()
    return made


def wait_all(made):
    for one in made:
        one.wait()


def normalised(v):
    centred = v - jnp.mean(v, axis=-1, keepdims=True)
    inv = lax.rsqrt(jnp.mean(centred * centred, axis=-1, keepdims=True) + LN_EPS)
    return centred * inv, inv


def norm_back(g, n, inv):
    return (g - jnp.mean(g, -1, keepdims=True) - n * jnp.mean(g * n, -1, keepdims=True)) * inv


def pack_kernel(info, *rest, plan, n_in, n_out):
    srcs, outs, bufs = rest[:n_in], rest[n_in : n_in + n_out], rest[n_in + n_out : n_in + 2 * n_out]
    sem_in, sem_out = rest[n_in + 2 * n_out :]
    pairs = []
    for i, which, o, col in plan:
        rows, cols = outs[o].shape[0], srcs[i].shape[1]
        pairs.append((srcs[i].at[row_at(info[which] * rows, rows), :], bufs[o].at[:, pl.ds(col, cols)]))
    wait_all(start_all(pairs, sem_in))
    wait_all(start_all(list(zip(bufs, outs)), sem_out))


def pack(info, srcs, shapes, plan):
    return pl.pallas_call(
        functools.partial(pack_kernel, plan=plan, n_in=len(srcs), n_out=len(shapes)),
        out_shape=tuple(shape_of(a, bf16) for a in shapes),
        in_specs=[SM] + [HB] * len(srcs),
        out_specs=(HB,) * len(shapes),
        scratch_shapes=[pltpu.VMEM(a, bf16) for a in shapes]
        + [pltpu.SemaphoreType.DMA((len(plan),)), pltpu.SemaphoreType.DMA((len(shapes),))],
        compiler_params=pltpu.CompilerParams(vmem_limit_bytes=58 << 20),
        name="pack",
        cost_estimate=cost(2),
    )(info, *srcs)


def head_rows(ref, h, at):
    own = ref[pl.ds(h * HEAD, HEAD), at]
    zero = jnp.zeros_like(own)
    return jnp.concatenate([own, zero] if h % 2 == 0 else [zero, own], 0)


def head_cols(ref, h, at):
    block = ref[at, pl.ds((h // 2) * 2 * HEAD, 2 * HEAD)]
    lane = lax.broadcasted_iota(jnp.int32, block.shape, 1)
    return jnp.where((lane < HEAD) == (h % 2 == 0), block, jnp.zeros_like(block))


def pair_cols(h):
    return pl.ds((h // 2) * 2 * HEAD, 2 * HEAD)


def allowed_bias(k0, first, last):
    place = k0 + lax.broadcasted_iota(jnp.int32, (TILE, TILE), 0)
    return jnp.where((place >= first) & (place < last), 0.0, MASKED).astype(f32)


def staged(heads, stages, lags):
    held = [{} for _ in stages]
    for step in range(heads + sum(lags)):
        behind = 0
        for i, stage in enumerate(stages):
            behind += lags[i]
            h = step - behind
            if 0 <= h < heads:
                held[i][h] = stage(h, held[i - 1].pop(h) if i else None)


def front_kernel(info, tiles, first, last, bq, bv, pk, pv, *rest, count, half):
    tok_in = rest[:6]
    own, mate = rest[6:9], rest[9:12]
    pieces = rest[12 : 12 + count]
    outs = rest[12 + count : 25 + count]
    keep_ref, send_ref, ot_out, lse_out, pk_out, pkt_out, pv_out = outs[:7]
    q_out, qt_out, k_out, kt_out, v_out, w_out = outs[7:]
    (tok, w_ref, q_ref, qt_ref, k_ref, kt_ref, v_ref, vt_ref, pk_ref, pkt_ref, pv_ref, pvt_ref, ot_ref, lse_ref,
     att, stat, acc, bias, sem_x, sem_w, sem_o, sem_a) = rest[25 + count :]
    core = info[0]
    tokens = tok_in[0].shape[0]
    width = tok.shape[1]
    pairs = []
    for i in range(6):
        place = (1, 2 - 2 * tiles[0], 2 * tiles[0])[i % 3]
        slot = 2 * place + (core if i < 3 else 1 - core)
        pairs.append((tok_in[i], tok.at[row_at(slot * tokens, tokens), :]))
    got_tok = start_all(pairs, sem_x)
    cols = pl.multiple_of(core * half, 128)
    got_w = []
    for i in (1, 2, 0):
        pairs = []
        for j, ref in enumerate((own[i], mate[i])):
            pairs.append((ref.at[:, pl.ds(cols, half)], w_ref.at[i, row_at(info[1 + j], ref.shape[0]), :]))
        for j, ref in enumerate(pieces):
            pairs.append(
                (
                    ref.at[:, pl.ds(i * width + cols, half)],
                    w_ref.at[i, row_at(info[HALF_AT + j], ref.shape[0]), :],
                )
            )
        got_w.append(start_all(pairs, sem_w.at[i]))
    pk_half, pv_half = pk[:, pl.ds(cols, half)], pv[:, pl.ds(cols, half)]
    pk_ref[...], pkt_ref[...] = pk_half, pk_half.astype(f32).T.astype(bf16)
    pv_ref[...], pvt_ref[...] = pv_half, pv_half.astype(f32).T.astype(bf16)
    bias_v = bv[pl.ds(cols, half)].astype(f32)[None, :]
    bias_q = bq[pl.ds(cols, half)].astype(f32)[None, :]
    blocks = k_ref.shape[0] // TILE
    wait_all(got_tok)
    wait_all(got_w[0])

    def key_block(b, carry):
        at = pl.ds(pl.multiple_of(b * TILE, TILE), TILE)
        full = dot(tok[at, :], w_ref[1])
        k_ref[at, :] = full.astype(bf16)
        kt_ref[:, at] = full.T.astype(bf16)
        return carry

    lax.fori_loop(0, blocks, key_block, 0, unroll=2)
    wait_all(got_w[1])

    def value_block(b, carry):
        at = pl.ds(pl.multiple_of(b * TILE, TILE), TILE)
        full = dot(tok[at, :], w_ref[2]) + bias_v
        v_ref[at, :] = full.astype(bf16)
        vt_ref[:, at] = full.T.astype(bf16)
        return carry

    lax.fori_loop(0, blocks, value_block, 0, unroll=2)
    wait_all(got_w[2])

    def query_block(b, carry):
        at = pl.ds(pl.multiple_of(b * TILE, TILE), TILE)
        src = pl.ds(pl.multiple_of(b * TILE + 2 * tokens, TILE), TILE)
        full = (dot(tok[src, :], w_ref[0]) + bias_q).astype(bf16).astype(f32) * SCALE
        q_ref[at, :] = full.astype(bf16)
        qt_ref[:, at] = full.T.astype(bf16)
        return carry

    lax.fori_loop(0, 2 * tokens // TILE, query_block, 0, unroll=2)
    pairs = [(w_ref, w_out), (k_ref, k_out), (kt_ref, kt_out), (v_ref, v_out), (q_ref, q_out), (qt_ref, qt_out)]
    pairs += [(pk_ref, pk_out), (pkt_ref, pkt_out), (pv_ref, pv_out)]
    saved = start_all(pairs, sem_o)
    heads = half // HEAD

    def one_query_tile(t, carry):
        at = pl.ds(pl.multiple_of(t * TILE, TILE), TILE)
        qs, qe = first[:, at], last[:, at]

        def prefix_score(h, _):
            return dot(pk_ref[:, pair_cols(h)], head_rows(qt_ref, h, at))

        def prefix_soft(h, s):
            top = jnp.max(s, axis=0, keepdims=True)
            p = jnp.exp(s - top)
            stat[pl.ds(h, 1), :] = top
            stat[pl.ds(heads + h, 1), :] = jnp.sum(p, axis=0, keepdims=True)
            return p.astype(bf16)

        def prefix_mix(h, p):
            acc[pl.ds(h * HEAD, HEAD), :] = dot(pvt_ref[pl.ds(h * HEAD, HEAD), :], p)

        staged(heads, (prefix_score, prefix_soft, prefix_mix), (0, 1, 3))

        def one_key_tile(j, inner):
            k0 = pl.multiple_of(j * TILE, TILE)
            bias[...] = allowed_bias(k0, qs, qe)

            def score(h, _):
                return dot(k_ref[pl.ds(k0, TILE), pair_cols(h)], head_rows(qt_ref, h, at))

            def soft(h, s):
                s = s + bias[...]
                old = stat[pl.ds(h, 1), :]
                top = jnp.maximum(old, jnp.max(s, axis=0, keepdims=True))
                factor = jnp.exp(old - top)
                p = jnp.exp(s - top)
                stat[pl.ds(h, 1), :] = top
                total = jnp.sum(p, axis=0, keepdims=True)
                stat[pl.ds(heads + h, 1), :] = stat[pl.ds(heads + h, 1), :] * factor + total
                return p.astype(bf16), factor

            def mix(h, held):
                p, factor = held
                rows = pl.ds(h * HEAD, HEAD)
                acc[rows, :] = acc[rows, :] * factor + dot(vt_ref[rows, pl.ds(k0, TILE)], p)

            staged(heads, (score, soft, mix), (0, 1, 3))
            return inner

        lax.fori_loop(tiles[1 + 2 * t], tiles[2 + 2 * t], one_key_tile, 0)
        for h in range(heads):
            rows = pl.ds(h * HEAD, HEAD)
            acc[rows, :] = acc[rows, :] / stat[pl.ds(heads + h, 1), :]
        ot_ref[:, at] = acc[...]
        lse_ref[:, at] = stat[pl.ds(0, heads), :] + jnp.log(stat[pl.ds(heads, heads), :])
        att[at, :] = acc[...].T.astype(bf16)
        return carry

    lax.fori_loop(0, 2 * tokens // TILE, one_query_tile, 0)
    mine, theirs = row_at(core * tokens, tokens), row_at((1 - core) * tokens, tokens)
    pairs = [(att.at[theirs, :], send_ref), (att.at[mine, :], keep_ref), (ot_ref, ot_out), (lse_ref, lse_out)]
    wait_all(start_all(pairs, sem_a))
    wait_all(saved)


def front(info, tiles, first, last, bq, bv, pk, pv, toks, own, mate, pieces):
    tokens, width = toks[0].shape
    half = width // 2
    heads, pre = half // HEAD, pk.shape[0]
    n_q, n_k = 2 * tokens, 6 * tokens
    count = len(pieces)
    kept = [(n_q, half), (half, n_q), (n_k, half), (half, n_k), (n_k, half)]
    pres = [(pre, half), (half, pre), (pre, half)]
    stats = [(half, n_q), (heads, n_q)]
    outs = [shape_of((tokens, half), bf16)] * 2 + [shape_of(a, f32) for a in stats]
    outs += [shape_of(a, bf16) for a in pres + kept + [(3, width, half)]]
    vmem = [(n_k, width), (3, width, half)] + kept + [(half, n_k)] + pres + [(half, pre)]
    return pl.pallas_call(
        functools.partial(front_kernel, count=count, half=half),
        out_shape=tuple(outs),
        in_specs=[SM, SM] + [VM] * 6 + [HB] * (12 + count),
        out_specs=(HB,) * len(outs),
        scratch_shapes=[pltpu.VMEM(a, bf16) for a in vmem]
        + [pltpu.VMEM(a, f32) for a in stats]
        + [
            pltpu.VMEM((n_q, half), bf16),
            pltpu.VMEM((2 * heads, TILE), f32),
            pltpu.VMEM((half, TILE), f32),
            pltpu.VMEM((TILE, TILE), f32),
            pltpu.SemaphoreType.DMA((6,)),
            pltpu.SemaphoreType.DMA((3, 2 + count)),
            pltpu.SemaphoreType.DMA((9,)),
            pltpu.SemaphoreType.DMA((4,)),
        ],
        compiler_params=pltpu.CompilerParams(vmem_limit_bytes=60 << 20),
        name="front",
        cost_estimate=cost(20),
    )(info, tiles, first, last, bq, bv, pk, pv, *toks, *own, *mate, *pieces)


def grad_stages(q, qt, kb, vb, ktb, do, do_t, lse, inner, bias, put):
    def products(h, _):
        return dot(kb(h), qt(h)), dot(vb(h), do_t(h))

    def scores(h, held):
        s, dp = held
        if bias is not None:
            s = s + bias[...]
        p = jnp.exp(s - lse(h))
        return p.astype(bf16), (p * (dp - inner(h))).astype(bf16)

    def sums(h, held):
        p, ds = held
        put(h, dot(p, do(h)), dot(ds, q(h)), dot(ktb(h), ds))

    return products, scores, sums


def sweep(ranges, at, first, last, refs, acc, heads):
    q_ref, qt_ref, k_ref, kt_ref, v_ref, do_ref, dot_ref, lse_ref, inner_ref, bias = refs
    dqt, dk, dv = acc
    qs, qe = first[:, at], last[:, at]

    def one_key_tile(j, carry):
        k0 = pl.multiple_of(j * TILE, TILE)
        r = pl.ds(k0, TILE)
        bias[...] = allowed_bias(k0, qs, qe)

        def put(h, gv, gk, gq):
            c, rows = pair_cols(h), pl.ds(h * HEAD, HEAD)
            dv[r, c] += gv
            dk[r, c] += gk
            dqt[rows, at] += gq

        stages = grad_stages(
            lambda h: head_cols(q_ref, h, at), lambda h: head_rows(qt_ref, h, at),
            lambda h: k_ref[r, pair_cols(h)], lambda h: v_ref[r, pair_cols(h)],
            lambda h: kt_ref[pl.ds(h * HEAD, HEAD), r], lambda h: head_cols(do_ref, h, at),
            lambda h: head_rows(dot_ref, h, at), lambda h: lse_ref[pl.ds(h, 1), at],
            lambda h: inner_ref[pl.ds(h, 1), at], bias, put,
        )
        staged(heads, stages, GRAD_LAGS)
        return carry

    for lo, hi in ranges:
        lax.fori_loop(lo, hi, one_key_tile, 0)


def prefix_grads_kernel(
    info, q_ref, qt_ref, pk_ref, pkt_ref, pv_ref, keep_in, recv_in, ot_ref, lse_ref,
    pre_ref, dqt, do_s, dot_s, inner_s, *, heads,
):
    core = info[0]
    tokens = keep_in.shape[0]
    n_q, pre = q_ref.shape[0], pk_ref.shape[0]
    do_s[row_at(core * tokens, tokens), :] = keep_in[...]
    do_s[row_at((1 - core) * tokens, tokens), :] = recv_in[...]
    pre_ref[...] = jnp.zeros_like(pre_ref)

    def one_query_tile(t, carry):
        at = pl.ds(pl.multiple_of(t * TILE, TILE), TILE)
        dot_s[:, at] = do_s[at, :].astype(f32).T.astype(bf16)
        for h in range(heads):
            rows = pl.ds(h * HEAD, HEAD)
            inner_s[pl.ds(h, 1), at] = jnp.sum(
                dot_s[rows, at].astype(f32) * ot_ref[rows, at], axis=0, keepdims=True
            )

        def put(h, gv, gk, gq):
            c = pair_cols(h)
            pre_ref[pl.ds(0, pre), c] += gk
            pre_ref[pl.ds(pre, pre), c] += gv
            dqt[pl.ds(h * HEAD, HEAD), at] = gq

        stages = grad_stages(
            lambda h: head_cols(q_ref, h, at), lambda h: head_rows(qt_ref, h, at),
            lambda h: pk_ref[:, pair_cols(h)], lambda h: pv_ref[:, pair_cols(h)],
            lambda h: pkt_ref[pl.ds(h * HEAD, HEAD), :], lambda h: head_cols(do_s, h, at),
            lambda h: head_rows(dot_s, h, at), lambda h: lse_ref[pl.ds(h, 1), at],
            lambda h: inner_s[pl.ds(h, 1), at], None, put,
        )
        staged(heads, stages, GRAD_LAGS)
        return carry

    lax.fori_loop(0, n_q // TILE, one_query_tile, 0)


def prefix_grads(info, q, qt, pk, pkt, pv, keep, recv, ot, lse):
    n_q, half = q.shape
    heads, pre = half // HEAD, pk.shape[0]
    return pl.pallas_call(
        functools.partial(prefix_grads_kernel, heads=heads),
        out_shape=(
            shape_of((2 * pre, half), f32),
            shape_of((half, n_q), f32),
            shape_of((n_q, half), bf16),
            shape_of((half, n_q), bf16),
            shape_of((heads, n_q), f32),
        ),
        in_specs=[SM] + [VM] * 9,
        out_specs=(VM,) * 5,
        compiler_params=pltpu.CompilerParams(vmem_limit_bytes=10 << 20),
        name="prefix_grads",
        cost_estimate=cost(5),
    )(info, q, qt, pk, pkt, pv, keep, recv, ot, lse)


def remote_grads_kernel(
    info, first, last, q_ref, qt_ref, k_ref, kt_ref, v_ref, do_ref, dot_ref, lse_ref, inner_ref, dqt_in,
    w_in, give_ref, keep_near, keep_far, dqt, dk, dv, bias, wsc, wsem, *, heads,
):
    copies = start_all([(w_in.at[1], wsc.at[0]), (w_in.at[2], wsc.at[1])], wsem)
    n_q = q_ref.shape[0]
    tokens = n_q // 2
    core = info[1 + 2 * (n_q // TILE)]
    dk[...] = jnp.zeros_like(dk)
    dv[...] = jnp.zeros_like(dv)
    dqt[...] = dqt_in[...]

    def one_query_tile(t, carry):
        at = pl.ds(pl.multiple_of(t * TILE, TILE), TILE)
        lo, hi = info[1 + 2 * t], info[2 + 2 * t]
        side = 2 * tokens // TILE
        refs = (q_ref, qt_ref, k_ref, kt_ref, v_ref, do_ref, dot_ref, lse_ref, inner_ref, bias)
        ranges = ((lo, jnp.minimum(hi, side)), (jnp.maximum(lo, 2 * side), hi))
        sweep(ranges, at, first, last, refs, (dqt, dk, dv), heads)
        return carry

    lax.fori_loop(0, n_q // TILE, one_query_tile, 0)
    wait_all(copies)
    for i, keep in ((0, keep_near), (1, keep_far)):
        for mine in (True, False):
            block = core if mine else 1 - core
            side = info[0] if i else 1 - info[0]
            r = row_at(side * 4 * tokens + block * tokens, tokens)
            out = dot(dk[r, :].astype(bf16), wsc[0], 1, 1) + dot(dv[r, :].astype(bf16), wsc[1], 1, 1)
            if mine:
                keep[...] = out.astype(bf16)
            else:
                give_ref[pl.ds(i * tokens, tokens), :] = out.astype(bf16)


def remote_grads(info, first, last, q, qt, k, kt, v, do, dot_, lse, inner, dqt, w):
    n_q, half = q.shape
    heads, tokens, width = half // HEAD, n_q // 2, w.shape[1]
    n_k = k.shape[0]
    return pl.pallas_call(
        functools.partial(remote_grads_kernel, heads=heads),
        out_shape=(
            shape_of((2 * tokens, width), bf16),
            shape_of((tokens, width), bf16),
            shape_of((tokens, width), bf16),
            shape_of((half, n_q), f32),
        ),
        in_specs=[SM] + [VM] * 12 + [HB],
        out_specs=(VM,) * 4,
        scratch_shapes=[
            pltpu.VMEM((n_k, half), f32),
            pltpu.VMEM((n_k, half), f32),
            pltpu.VMEM((TILE, TILE), f32),
            pltpu.VMEM((2, width, half), bf16),
            pltpu.SemaphoreType.DMA((2,)),
        ],
        compiler_params=pltpu.CompilerParams(vmem_limit_bytes=24 << 20),
        name="remote_grads",
        cost_estimate=cost(14),
    )(info, first, last, q, qt, k, kt, v, do, dot_, lse, inner, dqt, w)


def local_grads_kernel(
    info, first, last, q_ref, qt_ref, k_ref, kt_ref, v_ref, do_ref, dot_ref, lse_ref, inner_ref, dqt_in,
    gh_ref, w_in, keep_ref, give_ref, dqt, dk, dv, bias, wsc, wsem, *, heads,
):
    copies = start_all([(w_in, wsc)], wsem)
    core = info[1 + 2 * (q_ref.shape[0] // TILE)]
    n_q = q_ref.shape[0]
    tokens = n_q // 2
    dqt[...] = dqt_in[...]
    dk[...] = jnp.zeros_like(dk)
    dv[...] = jnp.zeros_like(dv)
    side = 2 * tokens // TILE

    def one_query_tile(t, carry):
        at = pl.ds(pl.multiple_of(t * TILE, TILE), TILE)
        lo, hi = info[1 + 2 * t], info[2 + 2 * t]
        refs = (q_ref, qt_ref, k_ref, kt_ref, v_ref, do_ref, dot_ref, lse_ref, inner_ref, bias)
        ranges = ((jnp.maximum(lo, side), jnp.minimum(hi, 2 * side)),)
        sweep(ranges, at, first, last, refs, (dqt, dk, dv), heads)
        return carry

    lax.fori_loop(0, n_q // TILE, one_query_tile, 0)
    wait_all(copies)
    for mine in (False, True):
        block = core if mine else 1 - core
        r = row_at(block * tokens, tokens)
        rk = row_at(block * tokens + n_q, tokens)
        dq = (dqt[:, r] * SCALE).T.astype(bf16)
        out = (
            dot(dq, wsc[0], 1, 1)
            + dot(dk[rk, :].astype(bf16), wsc[1], 1, 1)
            + dot(dv[rk, :].astype(bf16), wsc[2], 1, 1)
        )
        if mine:
            keep_ref[...] = out + gh_ref[...]
        else:
            give_ref[...] = out.astype(bf16)


def local_grads(info, first, last, q, qt, k, kt, v, do, dot_, lse, inner, dqt, gh, w):
    n_q, half = q.shape
    heads, tokens, width = half // HEAD, n_q // 2, w.shape[1]
    n_k = k.shape[0]
    return pl.pallas_call(
        functools.partial(local_grads_kernel, heads=heads),
        out_shape=(shape_of((tokens, width), f32), shape_of((tokens, width), bf16)),
        in_specs=[SM] + [VM] * 13 + [HB],
        out_specs=(VM,) * 2,
        scratch_shapes=[
            pltpu.VMEM((half, n_q), f32),
            pltpu.VMEM((n_k, half), f32),
            pltpu.VMEM((n_k, half), f32),
            pltpu.VMEM((TILE, TILE), f32),
            pltpu.VMEM((3, width, half), bf16),
            pltpu.SemaphoreType.DMA((1,)),
        ],
        compiler_params=pltpu.CompilerParams(vmem_limit_bytes=23 << 20),
        name="local_grads",
        cost_estimate=cost(14),
    )(info, first, last, q, qt, k, kt, v, do, dot_, lse, inner, dqt, gh, w)


def placed(refs, info, at, scale, dst, cols=None):
    pairs = []
    for i, ref in enumerate(refs):
        src = ref if cols is None else ref.at[:, cols[0]]
        rows = row_at(info[at + i] * scale, ref.shape[0])
        pairs.append((src, dst.at[rows, :] if cols is None else dst.at[rows, cols[1]]))
    return pairs


def up_pairs(parts, info, dst, cols):
    return placed((parts[0], parts[2]) + tuple(parts[4:]), info, 1, 1, dst, (cols, cols))


def out_pairs(parts, info, ff, dst):
    whole = pl.ds(0, dst.shape[1])
    return placed((parts[1], parts[3]), info, 1, 1, dst) + placed(
        parts[4:], info, 3, 1, dst, (pl.ds(ff, dst.shape[1]), whole)
    )


def up_kernel(info, own_att, got_att, tok, bo, ga, sa, bu, *rest, count):
    wu = rest[:count]
    hat_ref, inv_ref, act_ref, slope_ref, wo_s, wu_s, own_s, got_s, tok_s, sem_a, sem_o, sem_u = rest[count:]
    acts = start_all([(own_att, own_s), (got_att, got_s), (tok, tok_s)], sem_a)
    width, ff = wu_s.shape
    half = own_att.shape[1]
    got_o = start_all(out_pairs(wu, info, ff, wo_s), sem_o)
    part = ff // UP_PARTS
    got_u = []
    for j in range(UP_PARTS):
        got_u.append(start_all(up_pairs(wu, info, wu_s, pl.ds(j * part, part)), sem_u.at[j]))
    core = info[0]
    wait_all(acts)
    wait_all(got_o)
    hidden = (
        tok_s[...].astype(f32)
        + dot(own_s[...], wo_s[row_at(core * half, half), :])
        + dot(got_s[...], wo_s[row_at((1 - core) * half, half), :])
        + bo[...].astype(f32)[None, :]
    )
    hat, inv = normalised(hidden)
    hat_ref[...] = hat
    inv_ref[...] = jnp.broadcast_to(inv, inv_ref.shape)
    nrm = hat * ga[...].astype(f32)[None, :] + sa[...].astype(f32)[None, :]
    low = nrm.astype(bf16)
    for j in range(ff // CHUNK):
        if (j * CHUNK) % part == 0:
            wait_all(got_u[j * CHUNK // part])
        cs = pl.ds(j * CHUNK, CHUNK)
        v = dot(low, wu_s[:, cs]) + bu[cs].astype(f32)[None, :]
        phi = 0.5 + 0.5 * lax.erf(v * (0.5**0.5))
        act_ref[:, cs] = (v * phi).astype(bf16)
        slope_ref[:, cs] = (phi + v * (jnp.exp(v * v * -0.5) * 0.3989422804014327)).astype(bf16)


def up(info, own_att, got_att, tok, bo, ga, sa, bu, wu):
    tokens, width = tok.shape
    ff, count = bu.shape[0], len(wu)
    return pl.pallas_call(
        functools.partial(up_kernel, count=count),
        out_shape=(
            shape_of((tokens, width), f32),
            shape_of((tokens, 128), f32),
            shape_of((tokens, ff), bf16),
            shape_of((tokens, ff), bf16),
        ),
        in_specs=[SM] + [HB] * 3 + [VM] * 4 + [HB] * count,
        out_specs=(VM,) * 4,
        scratch_shapes=[
            pltpu.VMEM((width, width), bf16),
            pltpu.VMEM((width, ff), bf16),
            pltpu.VMEM((tokens, width // 2), bf16),
            pltpu.VMEM((tokens, width // 2), bf16),
            pltpu.VMEM((tokens, width), bf16),
            pltpu.SemaphoreType.DMA((3,)),
            pltpu.SemaphoreType.DMA((count - 2,)),
            pltpu.SemaphoreType.DMA((UP_PARTS, count - 2)),
        ],
        compiler_params=pltpu.CompilerParams(vmem_limit_bytes=50 << 20),
        name="up",
        cost_estimate=cost(10),
    )(info, own_att, got_att, tok, bo, ga, sa, bu, *wu)


def down_kernel(info, hat_ref, inv_ref, act_ref, slope_ref, cot, bd, gf, sf, ga, sa, *rest, count):
    wu, wd = rest[:count], rest[count : 2 * count - 2]
    out_ref, gh_ref, keep_ref, send_ref, wo_s, wu_s, wd_s, sem_o, sem_u, sem_d = rest[2 * count - 2 :]
    width, ff = wu_s.shape
    half = keep_ref.shape[1]
    got_d = start_all(placed(wd, info, 1, ff // width, wd_s), sem_d)
    got_u = start_all(up_pairs(wu, info, wu_s, pl.ds(0, ff)), sem_u)
    got_o = start_all(out_pairs(wu, info, ff, wo_s), sem_o)
    core = info[0]
    nrm = hat_ref[...] * ga[...].astype(f32)[None, :] + sa[...].astype(f32)[None, :]
    summed = nrm + bd[...].astype(f32)[None, :]
    for i, one in enumerate(got_d):
        one.wait()
        size = wd[i].shape[0]
        at = row_at(info[1 + i] * (ff // width), size)
        cols = pl.ds(pl.multiple_of(info[1 + i] * (ff // width), 128), size)
        summed = summed + dot(act_ref[:, cols], wd_s[at, :])
    n, inv = normalised(summed)
    gain = gf[...].astype(f32)[None, :]
    out_ref[...] = (n * gain + sf[...].astype(f32)[None, :]).astype(bf16)
    gs = norm_back(cot[...].astype(f32) * gain, n, inv)
    low = gs.astype(bf16)
    wait_all(got_u)
    total = gs
    for j in range(ff // CHUNK):
        cs = pl.ds(j * CHUNK, CHUNK)
        gp = (dot(low, wd_s[cs, :], 1, 1) * slope_ref[:, cs].astype(f32)).astype(bf16)
        total = total + dot(gp, wu_s[:, cs], 1, 1)
    gh = norm_back(total * ga[...].astype(f32)[None, :], hat_ref[...], inv_ref[:, :1])
    gh_ref[...] = gh
    gh_low = gh.astype(bf16)
    wait_all(got_o)
    send_ref[...] = dot(gh_low, wo_s[row_at((1 - core) * half, half), :], 1, 1).astype(bf16)
    keep_ref[...] = dot(gh_low, wo_s[row_at(core * half, half), :], 1, 1).astype(bf16)


def down(info, hat, inv, act, slope, cot, bd, gf, sf, ga, sa, wu, wd):
    tokens, width = hat.shape
    ff, count = act.shape[1], len(wu)
    return pl.pallas_call(
        functools.partial(down_kernel, count=count),
        out_shape=(
            shape_of((tokens, width), bf16),
            shape_of((tokens, width), f32),
            shape_of((tokens, width // 2), bf16),
            shape_of((tokens, width // 2), bf16),
        ),
        in_specs=[SM] + [VM] * 10 + [HB] * (2 * count - 2),
        out_specs=(VM,) * 4,
        scratch_shapes=[
            pltpu.VMEM((width, width), bf16),
            pltpu.VMEM((width, ff), bf16),
            pltpu.VMEM((ff, width), bf16),
            pltpu.SemaphoreType.DMA((count - 2,)),
            pltpu.SemaphoreType.DMA((count - 2,)),
            pltpu.SemaphoreType.DMA((count - 2,)),
        ],
        compiler_params=pltpu.CompilerParams(vmem_limit_bytes=46 << 20),
        name="down",
        cost_estimate=cost(16),
    )(info, hat, inv, act, slope, cot, bd, gf, sf, ga, sa, *wu, *wd)


def per_device(
    tokens, cotangent, pair_lengths, prefix_key, prefix_value, w_query, b_query, w_key, w_value, b_value,
    w_out, b_out, gain_attn, shift_attn, w_up, b_up, w_down, b_down, gain_ffn, shift_ffn,
):
    n_row, n_seq = lax.axis_size("row"), lax.axis_size("seq")
    r, s = lax.axis_index("row"), lax.axis_index("seq")
    core, x, zbit = r & 1, s & 1, (s >> 1) & 1
    tok_count, width = tokens.shape[1], tokens.shape[2]

    def by_core(a):
        return lax.ppermute(a, "row", [(i, i ^ 1) for i in range(n_row)])

    def by_y(a):
        return lax.ppermute(a, "row", [(i, i ^ 2) for i in range(n_row)])

    def by_seq(a, bit):
        return lax.ppermute(a, "seq", [(i, i ^ bit) for i in range(n_seq)])

    def by_both(a, row_bit, bit):
        route = [(i * n_seq + j, (i ^ row_bit) * n_seq + (j ^ bit)) for i in range(n_row) for j in range(n_seq)]
        return lax.ppermute(a, ("row", "seq"), route)

    def here(z):
        return z

    def near(z):
        return z ^ 1

    def far(z):
        to = z + 1 if z & 1 else z - 1
        return to if 0 <= to < n_seq // 2 else z

    def along(a, partner):
        return lax.ppermute(a, "seq", [(j, 2 * partner(j // 2) + (j & 1)) for j in range(n_seq)])

    def swapped(a, partner=here):
        route = []
        for i in range(n_row):
            for j in range(n_seq):
                to = ((i & ~1) | (j & 1)) * n_seq + 2 * partner(j // 2) + (i & 1)
                route.append((i * n_seq + j, to))
        return lax.ppermute(a, ("row", "seq"), route)

    def after(a, *others):
        return lax.optimization_barrier((a,) + others)[0]

    h = x ^ zbit
    first_q, second_q = 2 * h + x, 2 * h + 1 - x
    m = w_query.shape[0]
    others = [2 * (1 - h) + 1 - x, 2 * (1 - h) + x]
    places = [r * m, (r ^ 1) * m]
    halves = [(r ^ k) * m + j * (m // 4) for k in (2, 3) for j in [2 * h] + others]
    quarters = [(r ^ k) * m + j * (m // 4) for k in (2, 3) for j in [first_q, second_q] + others]
    odd = (s >> 1) & 1
    info = jnp.stack([core] + places + quarters + halves + [first_q, second_q, h]).astype(jnp.int32)
    attn = (w_query, w_key, w_value)
    short, ff = w_query.shape[0] // 4, w_up.shape[1]
    plan = [(i, H_AT, 0, i * width) for i in range(3)] + [(3, Q_AT, 1, 0), (4, Q_AT, 1, ff)]
    early, late = (w_query, w_key, w_value, w_up, w_out), (w_down, w_up, w_out)
    a_half, u_one = pack(info, early, [(2 * short, 3 * width), (short, ff + width)], plan)
    plan = [(0, Q_AT, 0, 0), (1, Q_AT + 1, 1, 0), (2, Q_AT + 1, 1, ff), (0, Q_AT + 1, 2, 0)]
    low = (w_down.shape[0] // 4, width)
    d_one, u_two, d_two = pack(after(info, u_one), late, [low, (short, ff + width), low], plan)
    a_half = by_y(a_half)
    own, close, distant = (swapped(tokens[0], k) for k in (here, near, far))
    a_own = [by_core(after(a, a_half)) for a in attn]
    mates = a_own
    a_part = lax.dynamic_slice_in_dim(a_half, x * short, short, 0)
    a_x, a_z = by_seq(a_part, 1), by_seq(a_part, 2)
    u_one = by_y(u_one)
    u_two = by_y(u_two)
    d_one = by_y(after(d_one, a_x))
    toks = [own, close, distant]
    toks = toks + [by_core(a) for a in toks]
    a_got = [a_half, a_x, a_z]
    a_got = a_got + [by_core(a_half), by_core(a_x), by_core(a_z)]
    u_own, o_own = by_core(after(w_up, a_z)), by_core(after(w_out, a_z))
    theirs = by_core(after(pair_lengths, a_x))
    lengths = jnp.where(x == core, pair_lengths, theirs)[0]
    pairs = lengths.shape[0]
    later = jnp.arange(pairs)[:, None] >= jnp.arange(pairs)[None, :]
    ends = jnp.sum(jnp.where(later, lengths[None, :], 0), axis=1)
    base = (s // 2) * 2 * tok_count
    place = base + jnp.arange(2 * tok_count, dtype=jnp.int32)
    passed = ends[:, None] <= place[None, :]
    origin = base - 2 * tok_count
    first = jnp.max(jnp.where(passed, ends[:, None], 0), axis=0) - origin
    last = jnp.min(jnp.where(passed, n_seq * tok_count, ends[:, None]), axis=0) - origin
    bounds = jnp.stack([first[::TILE] // TILE, (last[TILE - 1 :: TILE] + TILE - 1) // TILE], 1)
    tile_info = jnp.concatenate([odd[None], bounds.reshape(-1), core[None]]).astype(jnp.int32)
    first, last = first[None], last[None]

    (att_keep, att_send, ot, lse, pk, pkt, pv, q, qt, k, kt, v, w_half) = front(
        info, tile_info, first, last, b_query, b_value, prefix_key, prefix_value, toks,
        (w_query, w_key, w_value), mates[:3], a_got,
    )
    u_x, u_z = by_seq(u_one, 1), by_seq(u_one, 2)
    d_own = by_core(after(w_down, lse))
    cot = swapped(after(cotangent[0], lse))
    d_two = by_y(after(d_two, lse))
    d_one, lse = lax.optimization_barrier((d_one, lse))
    d_x, d_z = by_seq(d_one, 1), by_seq(d_one, 2)
    u_got = [u_one, u_two, u_x, u_z]
    u_got = u_got + [by_core(after(a, lse)) for a in u_got]
    parts_u = [w_up, w_out, u_own, o_own] + u_got
    hat, inv, act, slope = up(
        info, att_keep, by_core(att_send), own, b_out, gain_attn, shift_attn, b_up,
        parts_u,
    )
    d_got = [d_one, d_two, d_x, d_z]
    d_got = d_got + [by_core(a if a is d_one else after(a, inv, cot)) for a in d_got]
    parts_d = [w_down, d_own] + d_got
    result, gh, ga_keep, ga_send = down(
        info, hat, inv, act, slope, cot, b_down, gain_ffn, shift_ffn, gain_attn, shift_attn,
        parts_u, parts_d,
    )
    out_tokens = swapped(result)
    pre, dqt, do, dot_, inner = prefix_grads(info, q, qt, pk, pkt, pv, ga_keep, by_core(ga_send), ot, lse)

    def summed(a, row_bit, bit):
        low = a.astype(bf16)
        return low.astype(f32) + by_both(low, row_bit, bit).astype(f32)

    pre = summed(pre, 2, 0)
    give, keep_near, keep_far, dqt = remote_grads(
        tile_info, first, last, q, qt, k, kt, v, do, dot_, lse, inner, dqt, w_half
    )
    give, out_tokens, pre = lax.optimization_barrier((give, out_tokens, pre))
    got = by_core(give)
    near_part = (keep_near.astype(f32) + got[:tok_count].astype(f32)).astype(bf16)
    far_part = (keep_far.astype(f32) + got[tok_count:].astype(f32)).astype(bf16)
    tile_info, near_part, far_part = lax.optimization_barrier((tile_info, near_part, far_part))
    pre = summed(after(pre, near_part), 0, 1)
    near_part, far_part = along(near_part, near), along(far_part, far)
    keep, give = local_grads(
        tile_info, first, last, q, qt, k, kt, v, do, dot_, lse, inner, dqt, gh, w_half
    )
    pre, give, near_part, far_part = lax.optimization_barrier((pre, give, near_part, far_part))
    for i in range(1, n_seq.bit_length() - 1):
        pre = summed(pre, 0, 1 << i)
    mine = (keep + near_part.astype(f32)) + (by_core(give).astype(f32) + far_part.astype(f32))
    grad_tokens = swapped(mine.astype(bf16))
    other = by_core(after(pre, grad_tokens))
    pre = jnp.concatenate(
        [jnp.where(core == 0, pre, other), jnp.where(core == 0, other, pre)], axis=1
    )
    n_pre = prefix_key.shape[0]
    return out_tokens[None], grad_tokens[None], pre[:n_pre], pre[n_pre:]


def solution(mesh):
    both, split, whole = P("row", "seq", None), P("row", None), P()
    return jax.shard_map(
        per_device,
        mesh=mesh,
        in_specs=(
            both, both, split, whole, whole, split, whole, split, split, whole, split, whole, whole, whole,
            split, whole, split, whole, whole, whole,
        ),
        out_specs=(both, both, whole, whole),
        check_vma=False,
    )
```

```python
import functools

import jax
import jax.numpy as jnp
from jax import lax
from jax.experimental import pallas as pl
from jax.experimental.pallas import tpu as pltpu
from jax.sharding import PartitionSpec as P

HEAD = 64
SCALE = HEAD**-0.5
LN_EPS = 1e-05
MASKED = -1e30
TILE = 256
CHUNK = 512
UP_PARTS = 1
HALF_AT, Q_AT, H_AT = 11, 17, 19
GRAD_LAGS = (0, 2, 2)

f32 = jnp.float32
bf16 = jnp.bfloat16
VM = pl.BlockSpec(memory_space=pltpu.VMEM)
SM = pl.BlockSpec(memory_space=pltpu.SMEM)
HB = pl.BlockSpec(memory_space=pltpu.HBM)


def cost(us):
    return pl.CostEstimate(flops=int(us * 1e9), bytes_accessed=0, transcendentals=0)


def shape_of(shape, kind):
    return jax.ShapeDtypeStruct(shape, kind)


def dot(a, b, ca=1, cb=0):
    return lax.dot_general(a, b, (((ca,), (cb,)), ((), ())), preferred_element_type=f32)


def row_at(offset, rows):
    return pl.ds(pl.multiple_of(offset, 64), rows)


def start_all(pairs, sems):
    made = [pltpu.make_async_copy(s, d, sems.at[i]) for i, (s, d) in enumerate(pairs)]
    for one in made:
        one.start()
    return made


def wait_all(made):
    for one in made:
        one.wait()


def normalised(v):
    centred = v - jnp.mean(v, axis=-1, keepdims=True)
    inv = lax.rsqrt(jnp.mean(centred * centred, axis=-1, keepdims=True) + LN_EPS)
    return centred * inv, inv


def norm_back(g, n, inv):
    return (g - jnp.mean(g, -1, keepdims=True) - n * jnp.mean(g * n, -1, keepdims=True)) * inv


def pack_kernel(info, *rest, plan, n_in, n_out):
    srcs, outs, bufs = rest[:n_in], rest[n_in : n_in + n_out], rest[n_in + n_out : n_in + 2 * n_out]
    sem_in, sem_out = rest[n_in + 2 * n_out :]
    pairs = []
    for i, which, o, col in plan:
        rows, cols = outs[o].shape[0], srcs[i].shape[1]
        pairs.append((srcs[i].at[row_at(info[which] * rows, rows), :], bufs[o].at[:, pl.ds(col, cols)]))
    wait_all(start_all(pairs, sem_in))
    wait_all(start_all(list(zip(bufs, outs)), sem_out))


def pack(info, srcs, shapes, plan):
    return pl.pallas_call(
        functools.partial(pack_kernel, plan=plan, n_in=len(srcs), n_out=len(shapes)),
        out_shape=tuple(shape_of(a, bf16) for a in shapes),
        in_specs=[SM] + [HB] * len(srcs),
        out_specs=(HB,) * len(shapes),
        scratch_shapes=[pltpu.VMEM(a, bf16) for a in shapes]
        + [pltpu.SemaphoreType.DMA((len(plan),)), pltpu.SemaphoreType.DMA((len(shapes),))],
        compiler_params=pltpu.CompilerParams(vmem_limit_bytes=58 << 20),
        name="pack",
        cost_estimate=cost(2),
    )(info, *srcs)


def head_rows(ref, h, at):
    own = ref[pl.ds(h * HEAD, HEAD), at]
    zero = jnp.zeros_like(own)
    return jnp.concatenate([own, zero] if h % 2 == 0 else [zero, own], 0)


def head_cols(ref, h, at):
    block = ref[at, pl.ds((h // 2) * 2 * HEAD, 2 * HEAD)]
    lane = lax.broadcasted_iota(jnp.int32, block.shape, 1)
    return jnp.where((lane < HEAD) == (h % 2 == 0), block, jnp.zeros_like(block))


def pair_cols(h):
    return pl.ds((h // 2) * 2 * HEAD, 2 * HEAD)


def allowed_bias(k0, first, last):
    place = k0 + lax.broadcasted_iota(jnp.int32, (TILE, TILE), 0)
    return jnp.where((place >= first) & (place < last), 0.0, MASKED).astype(f32)


def staged(heads, stages, lags):
    held = [{} for _ in stages]
    for step in range(heads + sum(lags)):
        behind = 0
        for i, stage in enumerate(stages):
            behind += lags[i]
            h = step - behind
            if 0 <= h < heads:
                held[i][h] = stage(h, held[i - 1].pop(h) if i else None)


def front_kernel(info, tiles, first, last, bq, bv, pk, pv, *rest, count, half):
    tok_in = rest[:6]
    own, mate = rest[6:9], rest[9:12]
    pieces = rest[12 : 12 + count]
    outs = rest[12 + count : 25 + count]
    keep_ref, send_ref, ot_out, lse_out, pk_out, pkt_out, pv_out = outs[:7]
    q_out, qt_out, k_out, kt_out, v_out, w_out = outs[7:]
    (tok, w_ref, q_ref, qt_ref, k_ref, kt_ref, v_ref, vt_ref, pk_ref, pkt_ref, pv_ref, pvt_ref, ot_ref, lse_ref,
     att, stat, acc, bias, sem_x, sem_w, sem_o, sem_a) = rest[25 + count :]
    core = info[0]
    tokens = tok_in[0].shape[0]
    width = tok.shape[1]
    pairs = []
    for i in range(6):
        place = (1, 2 - 2 * tiles[0], 2 * tiles[0])[i % 3]
        slot = 2 * place + (core if i < 3 else 1 - core)
        pairs.append((tok_in[i], tok.at[row_at(slot * tokens, tokens), :]))
    got_tok = start_all(pairs, sem_x)
    cols = pl.multiple_of(core * half, 128)
    got_w = []
    for i in (1, 2, 0):
        pairs = []
        for j, ref in enumerate((own[i], mate[i])):
            pairs.append((ref.at[:, pl.ds(cols, half)], w_ref.at[i, row_at(info[1 + j], ref.shape[0]), :]))
        for j, ref in enumerate(pieces):
            pairs.append(
                (
                    ref.at[:, pl.ds(i * width + cols, half)],
                    w_ref.at[i, row_at(info[HALF_AT + j], ref.shape[0]), :],
                )
            )
        got_w.append(start_all(pairs, sem_w.at[i]))
    pk_half, pv_half = pk[:, pl.ds(cols, half)], pv[:, pl.ds(cols, half)]
    pk_ref[...], pkt_ref[...] = pk_half, pk_half.astype(f32).T.astype(bf16)
    pv_ref[...], pvt_ref[...] = pv_half, pv_half.astype(f32).T.astype(bf16)
    bias_v = bv[pl.ds(cols, half)].astype(f32)[None, :]
    bias_q = bq[pl.ds(cols, half)].astype(f32)[None, :]
    blocks = k_ref.shape[0] // TILE
    wait_all(got_tok)
    wait_all(got_w[0])

    def key_block(b, carry):
        at = pl.ds(pl.multiple_of(b * TILE, TILE), TILE)
        full = dot(tok[at, :], w_ref[1])
        k_ref[at, :] = full.astype(bf16)
        kt_ref[:, at] = full.T.astype(bf16)
        return carry

    lax.fori_loop(0, blocks, key_block, 0, unroll=3)
    wait_all(got_w[1])

    def value_block(b, carry):
        at = pl.ds(pl.multiple_of(b * TILE, TILE), TILE)
        full = dot(tok[at, :], w_ref[2]) + bias_v
        v_ref[at, :] = full.astype(bf16)
        vt_ref[:, at] = full.T.astype(bf16)
        return carry

    lax.fori_loop(0, blocks, value_block, 0, unroll=3)
    wait_all(got_w[2])

    def query_block(b, carry):
        at = pl.ds(pl.multiple_of(b * TILE, TILE), TILE)
        src = pl.ds(pl.multiple_of(b * TILE + 2 * tokens, TILE), TILE)
        full = (dot(tok[src, :], w_ref[0]) + bias_q).astype(bf16).astype(f32) * SCALE
        q_ref[at, :] = full.astype(bf16)
        qt_ref[:, at] = full.T.astype(bf16)
        return carry

    lax.fori_loop(0, 2 * tokens // TILE, query_block, 0, unroll=2)
    pairs = [(w_ref, w_out), (k_ref, k_out), (kt_ref, kt_out), (v_ref, v_out), (q_ref, q_out), (qt_ref, qt_out)]
    pairs += [(pk_ref, pk_out), (pkt_ref, pkt_out), (pv_ref, pv_out)]
    saved = start_all(pairs, sem_o)
    heads = half // HEAD

    def one_query_tile(t, carry):
        at = pl.ds(pl.multiple_of(t * TILE, TILE), TILE)
        qs, qe = first[:, at], last[:, at]

        def prefix_score(h, _):
            return dot(pk_ref[:, pair_cols(h)], head_rows(qt_ref, h, at))

        def prefix_soft(h, s):
            top = jnp.max(s, axis=0, keepdims=True)
            p = jnp.exp(s - top)
            stat[pl.ds(h, 1), :] = top
            stat[pl.ds(heads + h, 1), :] = jnp.sum(p, axis=0, keepdims=True)
            return p.astype(bf16)

        def prefix_mix(h, p):
            acc[pl.ds(h * HEAD, HEAD), :] = dot(pvt_ref[pl.ds(h * HEAD, HEAD), :], p)

        staged(heads, (prefix_score, prefix_soft, prefix_mix), (0, 1, 3))

        def one_key_tile(j, inner):
            k0 = pl.multiple_of(j * TILE, TILE)
            bias[...] = allowed_bias(k0, qs, qe)

            def score(h, _):
                return dot(k_ref[pl.ds(k0, TILE), pair_cols(h)], head_rows(qt_ref, h, at))

            def soft(h, s):
                s = s + bias[...]
                old = stat[pl.ds(h, 1), :]
                top = jnp.maximum(old, jnp.max(s, axis=0, keepdims=True))
                factor = jnp.exp(old - top)
                p = jnp.exp(s - top)
                stat[pl.ds(h, 1), :] = top
                total = jnp.sum(p, axis=0, keepdims=True)
                stat[pl.ds(heads + h, 1), :] = stat[pl.ds(heads + h, 1), :] * factor + total
                return p.astype(bf16), factor

            def mix(h, held):
                p, factor = held
                rows = pl.ds(h * HEAD, HEAD)
                acc[rows, :] = acc[rows, :] * factor + dot(vt_ref[rows, pl.ds(k0, TILE)], p)

            staged(heads, (score, soft, mix), (0, 1, 3))
            return inner

        lax.fori_loop(tiles[1 + 2 * t], tiles[2 + 2 * t], one_key_tile, 0)
        for h in range(heads):
            rows = pl.ds(h * HEAD, HEAD)
            acc[rows, :] = acc[rows, :] / stat[pl.ds(heads + h, 1), :]
        ot_ref[:, at] = acc[...]
        lse_ref[:, at] = stat[pl.ds(0, heads), :] + jnp.log(stat[pl.ds(heads, heads), :])
        att[at, :] = acc[...].T.astype(bf16)
        return carry

    lax.fori_loop(0, 2 * tokens // TILE, one_query_tile, 0)
    mine, theirs = row_at(core * tokens, tokens), row_at((1 - core) * tokens, tokens)
    pairs = [(att.at[theirs, :], send_ref), (att.at[mine, :], keep_ref), (ot_ref, ot_out), (lse_ref, lse_out)]
    wait_all(start_all(pairs, sem_a))
    wait_all(saved)


def front(info, tiles, first, last, bq, bv, pk, pv, toks, own, mate, pieces):
    tokens, width = toks[0].shape
    half = width // 2
    heads, pre = half // HEAD, pk.shape[0]
    n_q, n_k = 2 * tokens, 6 * tokens
    count = len(pieces)
    kept = [(n_q, half), (half, n_q), (n_k, half), (half, n_k), (n_k, half)]
    pres = [(pre, half), (half, pre), (pre, half)]
    stats = [(half, n_q), (heads, n_q)]
    outs = [shape_of((tokens, half), bf16)] * 2 + [shape_of(a, f32) for a in stats]
    outs += [shape_of(a, bf16) for a in pres + kept + [(3, width, half)]]
    vmem = [(n_k, width), (3, width, half)] + kept + [(half, n_k)] + pres + [(half, pre)]
    return pl.pallas_call(
        functools.partial(front_kernel, count=count, half=half),
        out_shape=tuple(outs),
        in_specs=[SM, SM] + [VM] * 6 + [HB] * (12 + count),
        out_specs=(HB,) * len(outs),
        scratch_shapes=[pltpu.VMEM(a, bf16) for a in vmem]
        + [pltpu.VMEM(a, f32) for a in stats]
        + [
            pltpu.VMEM((n_q, half), bf16),
            pltpu.VMEM((2 * heads, TILE), f32),
            pltpu.VMEM((half, TILE), f32),
            pltpu.VMEM((TILE, TILE), f32),
            pltpu.SemaphoreType.DMA((6,)),
            pltpu.SemaphoreType.DMA((3, 2 + count)),
            pltpu.SemaphoreType.DMA((9,)),
            pltpu.SemaphoreType.DMA((4,)),
        ],
        compiler_params=pltpu.CompilerParams(vmem_limit_bytes=60 << 20),
        name="front",
        cost_estimate=cost(20),
    )(info, tiles, first, last, bq, bv, pk, pv, *toks, *own, *mate, *pieces)


def grad_stages(q, qt, kb, vb, ktb, do, do_t, lse, inner, bias, put):
    def products(h, _):
        return dot(kb(h), qt(h)), dot(vb(h), do_t(h))

    def scores(h, held):
        s, dp = held
        if bias is not None:
            s = s + bias[...]
        p = jnp.exp(s - lse(h))
        return p.astype(bf16), (p * (dp - inner(h))).astype(bf16)

    def sums(h, held):
        p, ds = held
        put(h, dot(p, do(h)), dot(ds, q(h)), dot(ktb(h), ds))

    return products, scores, sums


def sweep(ranges, at, first, last, refs, acc, heads):
    q_ref, qt_ref, k_ref, kt_ref, v_ref, do_ref, dot_ref, lse_ref, inner_ref, bias = refs
    dqt, dk, dv = acc
    qs, qe = first[:, at], last[:, at]

    def one_key_tile(j, carry):
        k0 = pl.multiple_of(j * TILE, TILE)
        r = pl.ds(k0, TILE)
        bias[...] = allowed_bias(k0, qs, qe)

        def put(h, gv, gk, gq):
            c, rows = pair_cols(h), pl.ds(h * HEAD, HEAD)
            dv[r, c] += gv
            dk[r, c] += gk
            dqt[rows, at] += gq

        stages = grad_stages(
            lambda h: head_cols(q_ref, h, at), lambda h: head_rows(qt_ref, h, at),
            lambda h: k_ref[r, pair_cols(h)], lambda h: v_ref[r, pair_cols(h)],
            lambda h: kt_ref[pl.ds(h * HEAD, HEAD), r], lambda h: head_cols(do_ref, h, at),
            lambda h: head_rows(dot_ref, h, at), lambda h: lse_ref[pl.ds(h, 1), at],
            lambda h: inner_ref[pl.ds(h, 1), at], bias, put,
        )
        staged(heads, stages, GRAD_LAGS)
        return carry

    for lo, hi in ranges:
        lax.fori_loop(lo, hi, one_key_tile, 0)


def prefix_grads_kernel(
    info, q_ref, qt_ref, pk_ref, pkt_ref, pv_ref, keep_in, recv_in, ot_ref, lse_ref,
    pre_ref, dqt, do_s, dot_s, inner_s, *, heads,
):
    core = info[0]
    tokens = keep_in.shape[0]
    n_q, pre = q_ref.shape[0], pk_ref.shape[0]
    do_s[row_at(core * tokens, tokens), :] = keep_in[...]
    do_s[row_at((1 - core) * tokens, tokens), :] = recv_in[...]
    pre_ref[...] = jnp.zeros_like(pre_ref)

    def one_query_tile(t, carry):
        at = pl.ds(pl.multiple_of(t * TILE, TILE), TILE)
        dot_s[:, at] = do_s[at, :].astype(f32).T.astype(bf16)
        for h in range(heads):
            rows = pl.ds(h * HEAD, HEAD)
            inner_s[pl.ds(h, 1), at] = jnp.sum(
                dot_s[rows, at].astype(f32) * ot_ref[rows, at], axis=0, keepdims=True
            )

        def put(h, gv, gk, gq):
            c = pair_cols(h)
            pre_ref[pl.ds(0, pre), c] += gk
            pre_ref[pl.ds(pre, pre), c] += gv
            dqt[pl.ds(h * HEAD, HEAD), at] = gq

        stages = grad_stages(
            lambda h: head_cols(q_ref, h, at), lambda h: head_rows(qt_ref, h, at),
            lambda h: pk_ref[:, pair_cols(h)], lambda h: pv_ref[:, pair_cols(h)],
            lambda h: pkt_ref[pl.ds(h * HEAD, HEAD), :], lambda h: head_cols(do_s, h, at),
            lambda h: head_rows(dot_s, h, at), lambda h: lse_ref[pl.ds(h, 1), at],
            lambda h: inner_s[pl.ds(h, 1), at], None, put,
        )
        staged(heads, stages, GRAD_LAGS)
        return carry

    lax.fori_loop(0, n_q // TILE, one_query_tile, 0)


def prefix_grads(info, q, qt, pk, pkt, pv, keep, recv, ot, lse):
    n_q, half = q.shape
    heads, pre = half // HEAD, pk.shape[0]
    return pl.pallas_call(
        functools.partial(prefix_grads_kernel, heads=heads),
        out_shape=(
            shape_of((2 * pre, half), f32),
            shape_of((half, n_q), f32),
            shape_of((n_q, half), bf16),
            shape_of((half, n_q), bf16),
            shape_of((heads, n_q), f32),
        ),
        in_specs=[SM] + [VM] * 9,
        out_specs=(VM,) * 5,
        compiler_params=pltpu.CompilerParams(vmem_limit_bytes=10 << 20),
        name="prefix_grads",
        cost_estimate=cost(5),
    )(info, q, qt, pk, pkt, pv, keep, recv, ot, lse)


def remote_grads_kernel(
    info, first, last, q_ref, qt_ref, k_ref, kt_ref, v_ref, do_ref, dot_ref, lse_ref, inner_ref, dqt_in,
    w_in, give_ref, keep_near, keep_far, dqt, dk, dv, bias, wsc, wsem, *, heads,
):
    copies = start_all([(w_in.at[1], wsc.at[0]), (w_in.at[2], wsc.at[1])], wsem)
    n_q = q_ref.shape[0]
    tokens = n_q // 2
    core = info[1 + 2 * (n_q // TILE)]
    for ref in (dk, dv):
        for low in (0, 2 * n_q):
            ref[pl.ds(low, n_q), :] = jnp.zeros((n_q, ref.shape[1]), f32)
    dqt[...] = dqt_in[...]

    def one_query_tile(t, carry):
        at = pl.ds(pl.multiple_of(t * TILE, TILE), TILE)
        lo, hi = info[1 + 2 * t], info[2 + 2 * t]
        side = 2 * tokens // TILE
        refs = (q_ref, qt_ref, k_ref, kt_ref, v_ref, do_ref, dot_ref, lse_ref, inner_ref, bias)
        ranges = ((lo, jnp.minimum(hi, side)), (jnp.maximum(lo, 2 * side), hi))
        sweep(ranges, at, first, last, refs, (dqt, dk, dv), heads)
        return carry

    lax.fori_loop(0, n_q // TILE, one_query_tile, 0)
    wait_all(copies)
    for i, keep in ((0, keep_near), (1, keep_far)):
        for mine in (True, False):
            block = core if mine else 1 - core
            side = info[0] if i else 1 - info[0]
            r = row_at(side * 4 * tokens + block * tokens, tokens)
            out = dot(dk[r, :].astype(bf16), wsc[0], 1, 1) + dot(dv[r, :].astype(bf16), wsc[1], 1, 1)
            if mine:
                keep[...] = out.astype(bf16)
            else:
                give_ref[pl.ds(i * tokens, tokens), :] = out.astype(bf16)


def remote_grads(info, first, last, q, qt, k, kt, v, do, dot_, lse, inner, dqt, w):
    n_q, half = q.shape
    heads, tokens, width = half // HEAD, n_q // 2, w.shape[1]
    n_k = k.shape[0]
    return pl.pallas_call(
        functools.partial(remote_grads_kernel, heads=heads),
        out_shape=(
            shape_of((2 * tokens, width), bf16),
            shape_of((tokens, width), bf16),
            shape_of((tokens, width), bf16),
            shape_of((half, n_q), f32),
        ),
        in_specs=[SM] + [VM] * 12 + [HB],
        out_specs=(VM,) * 4,
        scratch_shapes=[
            pltpu.VMEM((n_k, half), f32),
            pltpu.VMEM((n_k, half), f32),
            pltpu.VMEM((TILE, TILE), f32),
            pltpu.VMEM((2, width, half), bf16),
            pltpu.SemaphoreType.DMA((2,)),
        ],
        compiler_params=pltpu.CompilerParams(vmem_limit_bytes=24 << 20),
        name="remote_grads",
        cost_estimate=cost(14),
    )(info, first, last, q, qt, k, kt, v, do, dot_, lse, inner, dqt, w)


def local_grads_kernel(
    info, first, last, q_ref, qt_ref, k_ref, kt_ref, v_ref, do_ref, dot_ref, lse_ref, inner_ref, dqt_in,
    gh_ref, w_in, keep_ref, give_ref, dqt, dk, dv, bias, wsc, wsem, *, heads,
):
    copies = start_all([(w_in, wsc)], wsem)
    core = info[1 + 2 * (q_ref.shape[0] // TILE)]
    n_q = q_ref.shape[0]
    tokens = n_q // 2
    dqt[...] = dqt_in[...]
    for ref in (dk, dv):
        ref[pl.ds(n_q, n_q), :] = jnp.zeros((n_q, ref.shape[1]), f32)
    side = 2 * tokens // TILE

    def one_query_tile(t, carry):
        at = pl.ds(pl.multiple_of(t * TILE, TILE), TILE)
        lo, hi = info[1 + 2 * t], info[2 + 2 * t]
        refs = (q_ref, qt_ref, k_ref, kt_ref, v_ref, do_ref, dot_ref, lse_ref, inner_ref, bias)
        ranges = ((jnp.maximum(lo, side), jnp.minimum(hi, 2 * side)),)
        sweep(ranges, at, first, last, refs, (dqt, dk, dv), heads)
        return carry

    lax.fori_loop(0, n_q // TILE, one_query_tile, 0)
    wait_all(copies)
    for mine in (False, True):
        block = core if mine else 1 - core
        r = row_at(block * tokens, tokens)
        rk = row_at(block * tokens + n_q, tokens)
        dq = (dqt[:, r] * SCALE).T.astype(bf16)
        out = (
            dot(dq, wsc[0], 1, 1)
            + dot(dk[rk, :].astype(bf16), wsc[1], 1, 1)
            + dot(dv[rk, :].astype(bf16), wsc[2], 1, 1)
        )
        if mine:
            keep_ref[...] = out + gh_ref[...]
        else:
            give_ref[...] = out.astype(bf16)


def local_grads(info, first, last, q, qt, k, kt, v, do, dot_, lse, inner, dqt, gh, w):
    n_q, half = q.shape
    heads, tokens, width = half // HEAD, n_q // 2, w.shape[1]
    n_k = k.shape[0]
    return pl.pallas_call(
        functools.partial(local_grads_kernel, heads=heads),
        out_shape=(shape_of((tokens, width), f32), shape_of((tokens, width), bf16)),
        in_specs=[SM] + [VM] * 13 + [HB],
        out_specs=(VM,) * 2,
        scratch_shapes=[
            pltpu.VMEM((half, n_q), f32),
            pltpu.VMEM((n_k, half), f32),
            pltpu.VMEM((n_k, half), f32),
            pltpu.VMEM((TILE, TILE), f32),
            pltpu.VMEM((3, width, half), bf16),
            pltpu.SemaphoreType.DMA((1,)),
        ],
        compiler_params=pltpu.CompilerParams(vmem_limit_bytes=23 << 20),
        name="local_grads",
        cost_estimate=cost(14),
    )(info, first, last, q, qt, k, kt, v, do, dot_, lse, inner, dqt, gh, w)


def placed(refs, info, at, scale, dst, cols=None):
    pairs = []
    for i, ref in enumerate(refs):
        src = ref if cols is None else ref.at[:, cols[0]]
        rows = row_at(info[at + i] * scale, ref.shape[0])
        pairs.append((src, dst.at[rows, :] if cols is None else dst.at[rows, cols[1]]))
    return pairs


def up_pairs(parts, info, dst, cols):
    return placed((parts[0], parts[2]) + tuple(parts[4:]), info, 1, 1, dst, (cols, cols))


def out_pairs(parts, info, ff, dst):
    whole = pl.ds(0, dst.shape[1])
    return placed((parts[1], parts[3]), info, 1, 1, dst) + placed(
        parts[4:], info, 3, 1, dst, (pl.ds(ff, dst.shape[1]), whole)
    )


def up_kernel(info, own_att, got_att, tok, bo, ga, sa, bu, *rest, count):
    wu = rest[:count]
    hat_ref, inv_ref, act_ref, slope_ref, wo_s, wu_s, own_s, got_s, tok_s, sem_a, sem_o, sem_u = rest[count:]
    acts = start_all([(own_att, own_s), (got_att, got_s), (tok, tok_s)], sem_a)
    width, ff = wu_s.shape
    half = own_att.shape[1]
    got_o = start_all(out_pairs(wu, info, ff, wo_s), sem_o)
    part = ff // UP_PARTS
    got_u = []
    for j in range(UP_PARTS):
        got_u.append(start_all(up_pairs(wu, info, wu_s, pl.ds(j * part, part)), sem_u.at[j]))
    core = info[0]
    wait_all(acts)
    wait_all(got_o)
    hidden = (
        tok_s[...].astype(f32)
        + dot(own_s[...], wo_s[row_at(core * half, half), :])
        + dot(got_s[...], wo_s[row_at((1 - core) * half, half), :])
        + bo[...].astype(f32)[None, :]
    )
    hat, inv = normalised(hidden)
    hat_ref[...] = hat
    inv_ref[...] = jnp.broadcast_to(inv, inv_ref.shape)
    nrm = hat * ga[...].astype(f32)[None, :] + sa[...].astype(f32)[None, :]
    low = nrm.astype(bf16)
    for j in range(ff // CHUNK):
        if (j * CHUNK) % part == 0:
            wait_all(got_u[j * CHUNK // part])
        cs = pl.ds(j * CHUNK, CHUNK)
        v = dot(low, wu_s[:, cs]) + bu[cs].astype(f32)[None, :]
        phi = 0.5 + 0.5 * lax.erf(v * (0.5**0.5))
        act_ref[:, cs] = (v * phi).astype(bf16)
        slope_ref[:, cs] = (phi + v * (jnp.exp(v * v * -0.5) * 0.3989422804014327)).astype(bf16)


def up(info, own_att, got_att, tok, bo, ga, sa, bu, wu):
    tokens, width = tok.shape
    ff, count = bu.shape[0], len(wu)
    return pl.pallas_call(
        functools.partial(up_kernel, count=count),
        out_shape=(
            shape_of((tokens, width), f32),
            shape_of((tokens, 128), f32),
            shape_of((tokens, ff), bf16),
            shape_of((tokens, ff), bf16),
        ),
        in_specs=[SM] + [HB] * 3 + [VM] * 4 + [HB] * count,
        out_specs=(VM,) * 4,
        scratch_shapes=[
            pltpu.VMEM((width, width), bf16),
            pltpu.VMEM((width, ff), bf16),
            pltpu.VMEM((tokens, width // 2), bf16),
            pltpu.VMEM((tokens, width // 2), bf16),
            pltpu.VMEM((tokens, width), bf16),
            pltpu.SemaphoreType.DMA((3,)),
            pltpu.SemaphoreType.DMA((count - 2,)),
            pltpu.SemaphoreType.DMA((UP_PARTS, count - 2)),
        ],
        compiler_params=pltpu.CompilerParams(vmem_limit_bytes=50 << 20),
        name="up",
        cost_estimate=cost(10),
    )(info, own_att, got_att, tok, bo, ga, sa, bu, *wu)


def down_kernel(info, hat_ref, inv_ref, act_ref, slope_ref, cot, bd, gf, sf, ga, sa, *rest, count):
    wu, wd = rest[:count], rest[count : 2 * count - 2]
    out_ref, gh_ref, keep_ref, send_ref, wo_s, wu_s, wd_s, sem_o, sem_u, sem_d = rest[2 * count - 2 :]
    width, ff = wu_s.shape
    half = keep_ref.shape[1]
    got_d = start_all(placed(wd, info, 1, ff // width, wd_s), sem_d)
    got_u = start_all(up_pairs(wu, info, wu_s, pl.ds(0, ff)), sem_u)
    got_o = start_all(out_pairs(wu, info, ff, wo_s), sem_o)
    core = info[0]
    nrm = hat_ref[...] * ga[...].astype(f32)[None, :] + sa[...].astype(f32)[None, :]
    summed = nrm + bd[...].astype(f32)[None, :]
    for i, one in enumerate(got_d):
        one.wait()
        size = wd[i].shape[0]
        at = row_at(info[1 + i] * (ff // width), size)
        cols = pl.ds(pl.multiple_of(info[1 + i] * (ff // width), 128), size)
        summed = summed + dot(act_ref[:, cols], wd_s[at, :])
    n, inv = normalised(summed)
    gain = gf[...].astype(f32)[None, :]
    out_ref[...] = (n * gain + sf[...].astype(f32)[None, :]).astype(bf16)
    gs = norm_back(cot[...].astype(f32) * gain, n, inv)
    low = gs.astype(bf16)
    wait_all(got_u)
    total = gs
    for j in range(ff // CHUNK):
        cs = pl.ds(j * CHUNK, CHUNK)
        gp = (dot(low, wd_s[cs, :], 1, 1) * slope_ref[:, cs].astype(f32)).astype(bf16)
        total = total + dot(gp, wu_s[:, cs], 1, 1)
    gh = norm_back(total * ga[...].astype(f32)[None, :], hat_ref[...], inv_ref[:, :1])
    gh_ref[...] = gh
    gh_low = gh.astype(bf16)
    wait_all(got_o)
    send_ref[...] = dot(gh_low, wo_s[row_at((1 - core) * half, half), :], 1, 1).astype(bf16)
    keep_ref[...] = dot(gh_low, wo_s[row_at(core * half, half), :], 1, 1).astype(bf16)


def down(info, hat, inv, act, slope, cot, bd, gf, sf, ga, sa, wu, wd):
    tokens, width = hat.shape
    ff, count = act.shape[1], len(wu)
    return pl.pallas_call(
        functools.partial(down_kernel, count=count),
        out_shape=(
            shape_of((tokens, width), bf16),
            shape_of((tokens, width), f32),
            shape_of((tokens, width // 2), bf16),
            shape_of((tokens, width // 2), bf16),
        ),
        in_specs=[SM] + [VM] * 10 + [HB] * (2 * count - 2),
        out_specs=(VM,) * 4,
        scratch_shapes=[
            pltpu.VMEM((width, width), bf16),
            pltpu.VMEM((width, ff), bf16),
            pltpu.VMEM((ff, width), bf16),
            pltpu.SemaphoreType.DMA((count - 2,)),
            pltpu.SemaphoreType.DMA((count - 2,)),
            pltpu.SemaphoreType.DMA((count - 2,)),
        ],
        compiler_params=pltpu.CompilerParams(vmem_limit_bytes=46 << 20),
        name="down",
        cost_estimate=cost(16),
    )(info, hat, inv, act, slope, cot, bd, gf, sf, ga, sa, *wu, *wd)


def per_device(
    tokens, cotangent, pair_lengths, prefix_key, prefix_value, w_query, b_query, w_key, w_value, b_value,
    w_out, b_out, gain_attn, shift_attn, w_up, b_up, w_down, b_down, gain_ffn, shift_ffn,
):
    n_row, n_seq = lax.axis_size("row"), lax.axis_size("seq")
    r, s = lax.axis_index("row"), lax.axis_index("seq")
    core, x, zbit = r & 1, s & 1, (s >> 1) & 1
    tok_count, width = tokens.shape[1], tokens.shape[2]

    def by_core(a):
        return lax.ppermute(a, "row", [(i, i ^ 1) for i in range(n_row)])

    def by_y(a):
        return lax.ppermute(a, "row", [(i, i ^ 2) for i in range(n_row)])

    def by_seq(a, bit):
        return lax.ppermute(a, "seq", [(i, i ^ bit) for i in range(n_seq)])

    def by_both(a, row_bit, bit):
        route = [(i * n_seq + j, (i ^ row_bit) * n_seq + (j ^ bit)) for i in range(n_row) for j in range(n_seq)]
        return lax.ppermute(a, ("row", "seq"), route)

    def here(z):
        return z

    def near(z):
        return z ^ 1

    def far(z):
        to = z + 1 if z & 1 else z - 1
        return to if 0 <= to < n_seq // 2 else z

    def along(a, partner):
        return lax.ppermute(a, "seq", [(j, 2 * partner(j // 2) + (j & 1)) for j in range(n_seq)])

    def swapped(a, partner=here):
        route = []
        for i in range(n_row):
            for j in range(n_seq):
                to = ((i & ~1) | (j & 1)) * n_seq + 2 * partner(j // 2) + (i & 1)
                route.append((i * n_seq + j, to))
        return lax.ppermute(a, ("row", "seq"), route)

    def after(a, *others):
        return lax.optimization_barrier((a,) + others)[0]

    h = x ^ zbit
    first_q, second_q = 2 * h + x, 2 * h + 1 - x
    m = w_query.shape[0]
    others = [2 * (1 - h) + 1 - x, 2 * (1 - h) + x]
    places = [r * m, (r ^ 1) * m]
    halves = [(r ^ k) * m + j * (m // 4) for k in (2, 3) for j in [2 * h] + others]
    quarters = [(r ^ k) * m + j * (m // 4) for k in (2, 3) for j in [first_q, second_q] + others]
    odd = (s >> 1) & 1
    info = jnp.stack([core] + places + quarters + halves + [first_q, second_q, h]).astype(jnp.int32)
    attn = (w_query, w_key, w_value)
    short, ff = w_query.shape[0] // 4, w_up.shape[1]
    plan = [(i, H_AT, 0, i * width) for i in range(3)] + [(3, Q_AT, 1, 0), (4, Q_AT, 1, ff)]
    early, late = (w_query, w_key, w_value, w_up, w_out), (w_down, w_up, w_out)
    a_half, u_one = pack(info, early, [(2 * short, 3 * width), (short, ff + width)], plan)
    plan = [(0, Q_AT, 0, 0), (1, Q_AT + 1, 1, 0), (2, Q_AT + 1, 1, ff), (0, Q_AT + 1, 2, 0)]
    low = (w_down.shape[0] // 4, width)
    d_one, u_two, d_two = pack(after(info, u_one), late, [low, (short, ff + width), low], plan)
    a_half = by_y(a_half)
    own, close, distant = (swapped(tokens[0], k) for k in (here, near, far))
    a_own = [by_core(after(a, a_half)) for a in attn]
    mates = a_own
    a_part = lax.dynamic_slice_in_dim(a_half, x * short, short, 0)
    a_x, a_z = by_seq(a_part, 1), by_seq(a_part, 2)
    u_one = by_y(u_one)
    u_two = by_y(u_two)
    d_one = by_y(after(d_one, a_x))
    toks = [own, close, distant]
    toks = toks + [by_core(a) for a in toks]
    a_got = [a_half, a_x, a_z]
    a_got = a_got + [by_core(a_half), by_core(a_x), by_core(a_z)]
    u_own, o_own = by_core(after(w_up, a_z)), by_core(after(w_out, a_z))
    theirs = by_core(after(pair_lengths, a_x))
    lengths = jnp.where(x == core, pair_lengths, theirs)[0]
    pairs = lengths.shape[0]
    later = jnp.arange(pairs)[:, None] >= jnp.arange(pairs)[None, :]
    ends = jnp.sum(jnp.where(later, lengths[None, :], 0), axis=1)
    base = (s // 2) * 2 * tok_count
    place = base + jnp.arange(2 * tok_count, dtype=jnp.int32)
    passed = ends[:, None] <= place[None, :]
    origin = base - 2 * tok_count
    first = jnp.max(jnp.where(passed, ends[:, None], 0), axis=0) - origin
    last = jnp.min(jnp.where(passed, n_seq * tok_count, ends[:, None]), axis=0) - origin
    bounds = jnp.stack([first[::TILE] // TILE, (last[TILE - 1 :: TILE] + TILE - 1) // TILE], 1)
    tile_info = jnp.concatenate([odd[None], bounds.reshape(-1), core[None]]).astype(jnp.int32)
    first, last = first[None], last[None]

    (att_keep, att_send, ot, lse, pk, pkt, pv, q, qt, k, kt, v, w_half) = front(
        info, tile_info, first, last, b_query, b_value, prefix_key, prefix_value, toks,
        (w_query, w_key, w_value), mates[:3], a_got,
    )
    u_x, u_z = by_seq(u_one, 1), by_seq(u_one, 2)
    d_own = by_core(after(w_down, lse))
    cot = swapped(after(cotangent[0], lse))
    d_two = by_y(after(d_two, lse))
    d_one, lse = lax.optimization_barrier((d_one, lse))
    d_x, d_z = by_seq(d_one, 1), by_seq(d_one, 2)
    u_got = [u_one, u_two, u_x, u_z]
    u_got = u_got + [by_core(after(a, lse)) for a in u_got]
    parts_u = [w_up, w_out, u_own, o_own] + u_got
    hat, inv, act, slope = up(
        info, att_keep, by_core(att_send), own, b_out, gain_attn, shift_attn, b_up,
        parts_u,
    )
    d_got = [d_one, d_two, d_x, d_z]
    d_got = d_got + [by_core(a if a is d_one else after(a, inv, cot)) for a in d_got]
    parts_d = [w_down, d_own] + d_got
    result, gh, ga_keep, ga_send = down(
        info, hat, inv, act, slope, cot, b_down, gain_ffn, shift_ffn, gain_attn, shift_attn,
        parts_u, parts_d,
    )
    out_tokens = swapped(result)
    pre, dqt, do, dot_, inner = prefix_grads(info, q, qt, pk, pkt, pv, ga_keep, by_core(ga_send), ot, lse)

    def summed(a, row_bit, bit):
        low = a.astype(bf16)
        return low.astype(f32) + by_both(low, row_bit, bit).astype(f32)

    pre = summed(pre, 2, 0)
    give, keep_near, keep_far, dqt = remote_grads(
        tile_info, first, last, q, qt, k, kt, v, do, dot_, lse, inner, dqt, w_half
    )
    give, out_tokens, pre = lax.optimization_barrier((give, out_tokens, pre))
    got = by_core(give)
    near_part = (keep_near.astype(f32) + got[:tok_count].astype(f32)).astype(bf16)
    far_part = (keep_far.astype(f32) + got[tok_count:].astype(f32)).astype(bf16)
    tile_info, near_part, far_part = lax.optimization_barrier((tile_info, near_part, far_part))
    pre = summed(after(pre, near_part), 0, 1)
    near_part, far_part = along(near_part, near), along(far_part, far)
    keep, give = local_grads(
        tile_info, first, last, q, qt, k, kt, v, do, dot_, lse, inner, dqt, gh, w_half
    )
    pre, give, near_part, far_part = lax.optimization_barrier((pre, give, near_part, far_part))
    for i in range(1, n_seq.bit_length() - 1):
        pre = summed(pre, 0, 1 << i)
    mine = (keep + near_part.astype(f32)) + (by_core(give).astype(f32) + far_part.astype(f32))
    grad_tokens = swapped(mine.astype(bf16))
    other = by_core(after(pre, grad_tokens))
    pre = jnp.concatenate(
        [jnp.where(core == 0, pre, other), jnp.where(core == 0, other, pre)], axis=1
    )
    n_pre = prefix_key.shape[0]
    return out_tokens[None], grad_tokens[None], pre[:n_pre], pre[n_pre:]


def solution(mesh):
    both, split, whole = P("row", "seq", None), P("row", None), P()
    return jax.shard_map(
        per_device,
        mesh=mesh,
        in_specs=(
            both, both, split, whole, whole, split, whole, split, split, whole, split, whole, whole, whole,
            split, whole, split, whole, whole, whole,
        ),
        out_specs=(both, both, whole, whole),
        check_vma=False,
    )
```
